32 devices in a mesh: img: 8 (over z, y), rep: 4 (over x, core).
Axes of the slice: x: 2, y: 2, z: 4, core: 2. Of those that a mesh axis runs over, the one named last changes fastest.
Arguments:
- descriptors: bfloat16 [16, 256, 1024], P('img', 'rep'), may hold values from -0.5 to 0.5
- cell_counts: int32 [16, 256], P('img', 'rep'), may hold values from 1 to 8
- pair_images: int32 [64, 2], P('img'), may hold values from 0 to 15, as said below
- query_cells: int32 [64, 16], P('img'), may hold values from 0 to 255
- cand_cells: int32 [64, 4, 16], P('img', 'rep'), may hold values from 0 to 255, as said below
- cand_counts: int32 [64, 4], P('img', 'rep'), may hold values from 8 to 16, as said below
Outputs:
- matches: float32 [64, 2, 128], P('img')
- image_score: float32 [16], P('img')
The draws below stay inside these ranges and needn't reach their ends.
Inputs may be any that keep to these rules, and one draw needn't show every extreme that they name: `pair_images`: the pairs are numbered by blocks of 8: pair k * 8 + j has its first image among images k * 2 to k * 2 + 1 and its second among images j * 2 to j * 2 + 1; the two images of a pair differ. cand_cells[p, r, s] lies in quarter r, between r * 64 and r * 64 + 63; cells may repeat. `cand_counts`: every count is 8 or 16, and every draw holds at least one count of 16.
All inputs are finite; a program needn't handle non-finite values.
Results may differ from the reference program's by a relative error of at most 0.0003.
Values may be sent and summed in bfloat16 or wider, within the bound.
A program may use at most 64 MiB of HBM per device.

```python
import jax
import jax.numpy as jnp
from jax import lax

DESC = 128
KP = 8
CELLS = 256
IMG_DEV = 2
QCELL = 16
SLOT = 16
QDESC = 128
IMAGES = 16
PAIRS = 64
N_IMG = 8
N_REP = 4


def draw_pair_images(key, part):
    index = jnp.arange(N_IMG * N_IMG, dtype=jnp.int32)
    owner = index // N_IMG
    partner = index % N_IMG
    key_first = jax.random.fold_in(key, 11)
    key_second = jax.random.fold_in(key, 12)
    key_same = jax.random.fold_in(key, 13)
    local_first = jax.random.randint(key_first, (N_IMG * N_IMG,), 0, IMG_DEV, dtype=jnp.int32)
    local_any = jax.random.randint(key_second, (N_IMG * N_IMG,), 0, IMG_DEV, dtype=jnp.int32)
    local_other = jax.random.randint(key_same, (N_IMG * N_IMG,), 0, IMG_DEV - 1, dtype=jnp.int32)
    local_other = jnp.where(local_other >= local_first, local_other + 1, local_other)
    local_second = jnp.where(owner == partner, local_other, local_any)
    first = owner * IMG_DEV + local_first
    second = partner * IMG_DEV + local_second
    return jnp.stack([first, second], axis=1).astype(jnp.int32)


def draw_cand_cells(key, part):
    share = CELLS // N_REP
    offsets = jax.random.randint(jax.random.fold_in(key, 21), (N_IMG * N_IMG, N_REP, SLOT), 0, share, dtype=jnp.int32)
    quarter = jnp.arange(N_REP, dtype=jnp.int32)[None, :, None] * share
    return (offsets + quarter).astype(jnp.int32)


def draw_cand_counts(key, part):
    divisor = jax.random.randint(jax.random.fold_in(key, 31), (N_IMG * N_IMG * N_REP,), 1, 3, dtype=jnp.int32)
    counts = SLOT // divisor
    spot = jax.random.randint(jax.random.fold_in(key, 32), (), 0, N_IMG * N_IMG * N_REP, dtype=jnp.int32)
    counts = jnp.where(jnp.arange(N_IMG * N_IMG * N_REP, dtype=jnp.int32) == spot, SLOT, counts)
    return counts.reshape(N_IMG * N_IMG, N_REP).astype(jnp.int32)


def touch_ends(array, own_key, smallest, largest):
    spot = [jax.random.randint(jax.random.fold_in(own_key, axis), (), 0, length) for axis, length in enumerate(array.shape)]
    longest = array.shape.index(max(array.shape))
    next_to = spot[:longest] + [(spot[longest] + 1) % array.shape[longest]] + spot[longest + 1:]
    return array.at[tuple(spot)].set(smallest).at[tuple(next_to)].set(largest)


def levels(own_key, dims, shards, low, largest):
    gain, own = 1.0, jax.random.fold_in(own_key, 6)
    for position, blocks in shards:
        heights = jnp.exp(jax.random.uniform(jax.random.fold_in(own, position), (blocks,), jnp.float32, low / len(shards), largest / len(shards)))
        gain = gain * jnp.repeat(heights, dims[position] // blocks).reshape([-1 if axis == position else 1 for axis in range(len(dims))])
    return gain


def gaussian(rng, shape, width, limit, split=(), kind=jnp.bfloat16):
    entries = width * jax.random.normal(rng, shape, jnp.float32)
    if split:
        entries = entries * levels(rng, shape, split, -0.22, 0.18)
    return jnp.clip(entries, -limit, limit).astype(kind)


def setup_inputs(seed: int = 0) -> dict:
    keys = jax.random.split(jax.random.key(seed), 7)
    descriptors = gaussian(keys[0], (IMAGES, CELLS, KP * DESC), 0.0884, 0.5, ((0, 8), (1, 4)))
    cell_counts = touch_ends(jax.random.randint(keys[1], (IMAGES, CELLS), 1, KP + 1), jax.random.fold_in(keys[1], 1), 1, KP).astype(jnp.int32)
    pair_images = draw_pair_images(jax.random.fold_in(keys[6], 71), 0)
    query_cells = touch_ends(jax.random.randint(keys[3], (PAIRS, QCELL), 0, CELLS), jax.random.fold_in(keys[3], 1), 0, CELLS - 1).astype(jnp.int32)
    cand_cells = draw_cand_cells(jax.random.fold_in(keys[6], 71), 0)
    cand_counts = draw_cand_counts(jax.random.fold_in(keys[6], 71), 0)
    return {"descriptors": descriptors, "cell_counts": cell_counts, "pair_images": pair_images, "query_cells": query_cells, "cand_cells": cand_cells, "cand_counts": cand_counts}


distant = 1.0e9


def reference(descriptors, cell_counts, pair_images, query_cells, cand_cells, cand_counts):
    flat = descriptors.reshape(IMAGES * CELLS, KP * DESC)
    flat_counts = cell_counts.reshape(IMAGES * CELLS)
    first = pair_images[:, 0].astype(jnp.int32)
    second = pair_images[:, 1].astype(jnp.int32)
    query_rows = (first[:, None] * CELLS + query_cells).astype(jnp.int32)
    cand_rows = (second[:, None, None] * CELLS + cand_cells).astype(jnp.int32)
    slot_ids = jnp.arange(KP, dtype=jnp.int32)
    cand_ids = jnp.arange(SLOT, dtype=jnp.int32)

    def one_pair(index):
        qrow = query_rows[index]
        crow = cand_rows[index].reshape(N_REP * SLOT)
        queries = flat[qrow].reshape(QDESC, DESC).astype(jnp.float32)
        qlive = (slot_ids[None, :] < flat_counts[qrow][:, None]).reshape(QDESC)
        cands = flat[crow].reshape(N_REP * SLOT * KP, DESC).astype(jnp.float32)
        cell_live = cand_ids[None, :] < cand_counts[index][:, None]
        slot_live = slot_ids[None, None, :] < flat_counts[crow].reshape(N_REP, SLOT)[:, :, None]
        clive = (cell_live[:, :, None] & slot_live).reshape(N_REP * SLOT * KP)
        qnorm = jnp.sum(queries * queries, axis=1)
        cnorm = jnp.sum(cands * cands, axis=1)
        inner = jnp.dot(queries, cands.T, precision=lax.Precision.HIGHEST, preferred_element_type=jnp.float32)
        dist = qnorm[:, None] + cnorm[None, :] - 2.0 * inner
        dist = jnp.where(clive[None, :], dist, jnp.float32(distant))
        lowest = -lax.top_k(-dist, 2)[0]
        best = jnp.where(qlive, lowest[:, 0], jnp.float32(0.0))
        runner = jnp.where(qlive, lowest[:, 1], jnp.float32(0.0))
        margin = jnp.where(qlive, (runner - best) / (runner + 1.0), jnp.float32(0.0))
        score = jnp.sum(margin) / jnp.sum(qlive.astype(jnp.float32))
        return jnp.stack([best, runner]), score

    matches, scores = lax.map(one_pair, jnp.arange(PAIRS, dtype=jnp.int32))
    image_score = jnp.zeros((IMAGES,), jnp.float32).at[first].add(scores).at[second].add(scores)
    return matches, image_score
```

```python
import functools

import jax
import jax.numpy as jnp
from jax import lax
from jax.experimental import pallas as pl
from jax.experimental.pallas import tpu as pltpu
from jax.sharding import PartitionSpec as P

DESC = 128
MESH = pl.DeviceIdType.MESH
distant = 1.0e9
far_entry = 32768.0
f32, bf16, i32 = jnp.float32, jnp.bfloat16, jnp.int32


def partner(me, step, size):
    other, bit = 0, 1
    while bit < size:
        other = other + ((me // bit + step // bit) % 2) * bit
        bit *= 2
    return other


def repeat(first, last, body):
    if last - first <= 8:
        for t in range(first, last):
            body(t)
    else:
        lax.fori_loop(first, last, lambda t, c: (body(t), c)[1], 0)


def dot(a, b):
    return jnp.dot(a, b, preferred_element_type=f32)


def dot_t(a, b):
    return lax.dot_general(a, b, (((1,), (1,)), ((), ())), preferred_element_type=f32)


def split(square):
    high = square.astype(bf16)
    return high, (square - high.astype(f32)).astype(bf16)


def column(row, length):
    rows = lax.broadcasted_iota(i32, (length, length), 0)
    cols = lax.broadcasted_iota(i32, (length, length), 1)
    return jnp.sum(jnp.where(rows == cols, row, 0.0), axis=1, keepdims=True)


def merge(a, b):
    low = jnp.minimum(a[0], b[0])
    high = jnp.minimum(jnp.maximum(a[0], b[0]), jnp.minimum(a[1], b[1]))
    return low, high


def lowest_two(d):
    half = d.shape[0] // 2
    a, b = d[:half], d[half:]
    two = (jnp.minimum(a, b), jnp.maximum(a, b))
    while half > 1:
        half //= 2
        two = merge((two[0][:half], two[1][:half]), (two[0][half:], two[1][half:]))
    return two


def stacked(cells):
    kp = cells.shape[1] // DESC
    return jnp.concatenate([cells[:, s * DESC : (s + 1) * DESC] for s in range(kp)], axis=0)


def kernel(
    n, sides,
    desc_hbm, counts_hbm, pairs_hbm, qcells_hbm, ccells_hbm, ccounts_hbm,
    own, arr,
    both, counts, pairs, qcells, ccells, ccounts, in_sem,
    info, lists_out, lists_in, q_out, q_in, lhs, part_out,
    info_send, info_recv, both_send, both_recv, list_send, list_recv,
    q_send, q_recv, own_send, own_recv, arr_send, arr_recv,
):
    me, r = lax.axis_index("img"), lax.axis_index("rep")
    side, core = r // 2, r % 2
    mate = side * 2 + (1 - core)
    img_dev, share, width = both.shape[1:]
    rows = img_dev * share
    kp = width // DESC
    slots = ccells.shape[2]
    qn = qcells.shape[1]
    half = n // 2

    def remote(src, dst, send, recv, img, rep):
        return pltpu.make_async_remote_copy(
            src_ref=src, dst_ref=dst, send_sem=send, recv_sem=recv,
            device_id=(img, rep), device_id_type=MESH,
        )

    def other(i):
        return partner(me, 2 * i + core, n)

    barrier = pltpu.get_barrier_semaphore()

    def greet(img, rep):
        pl.semaphore_signal(barrier, inc=1, device_id=(img, rep), device_id_type=MESH)

    def around(s):
        return (side + s) % sides

    greet(me, mate)
    for s in range(1, sides):
        greet(other(0), around(s) * 2 + core)

    @pl.when(core == 1)
    def _():
        greet(other(0), r)

    def greet_all(i):
        for s in range(sides):
            greet(other(i), around(s) * 2 + core)

    repeat(1, half, greet_all)

    small = [
        pltpu.make_async_copy(src, dst, in_sem.at[i])
        for i, (src, dst) in enumerate((
            (counts_hbm, counts), (pairs_hbm, pairs),
            (ccells_hbm, ccells), (ccounts_hbm, ccounts), (qcells_hbm, qcells),
        ))
    ]
    shard = pltpu.make_async_copy(desc_hbm, both.at[core], in_sem.at[len(small)])
    for load in small:
        load.start()
    shard.start()
    for load in small:
        load.wait()

    local = (pairs[...] % img_dev).astype(f32)
    first = column(local[0:1], n).astype(i32)
    second = column(local[1:2], n).astype(i32)
    live_cells = column(ccounts[...].astype(f32), n).astype(i32)
    wanted = core * rows + second * share + ccells[:, 0, :] % share
    wanted = jnp.where(lax.broadcasted_iota(i32, (n, slots), 1) < live_cells, wanted, -1)
    info[core, 0:n, 0:slots] = wanted
    info[core, n : n + img_dev, 0:share] = counts[...]

    cells = qcells[...]
    quarter = cells // share
    where = (quarter % 2) * rows + first * share + cells % share
    where = jnp.where(quarter // 2 == side, where, -1)
    lists_out[0:n, 0:qn] = where
    shard.wait()

    pl.semaphore_wait(barrier, half * sides + core)

    info_copy = remote(info.at[core], info.at[core], info_send, info_recv, me, mate)
    info_copy.start()
    shard_copy = remote(both.at[core], both.at[core], both_send, both_recv, me, mate)
    shard_copy.start()

    group = min(half, 4)
    found_at = []
    for g in range(0, half, group):
        picks = [
            column(lists_out[pl.ds(other(i), 1), 0:qn].astype(f32), qn) for i in range(g, g + group)
        ]
        found_at.append(jnp.concatenate(picks, axis=0).astype(i32))

    there = pltpu.make_async_copy(info.at[1 - core], info.at[1 - core], info_recv)
    there.wait()

    def send_list(i):
        j = other(i)
        lists_out[pl.ds(n + i, 1), 0:slots] = info[0, pl.ds(j, 1), 0:slots]
        lists_out[pl.ds(n + i, 1), slots : 2 * slots] = info[1, pl.ds(j, 1), 0:slots]

    repeat(0, half, send_list)

    def list_to(i):
        return lists_out.at[pl.ds(n + i, 1)], lists_in.at[pl.ds(i, 1)]

    @pl.when(core == 0)
    def _():
        pltpu.make_async_copy(*list_to(0), list_recv.at[0]).start()

    @pl.when(core == 1)
    def _():
        remote(*list_to(0), list_send, list_recv.at[0], other(0), r).start()

    repeat(1, half, lambda i: remote(*list_to(i), list_send, list_recv.at[i], other(i), r).start())

    count_row = jnp.concatenate(
        [info[q, n + i : n + i + 1, 0:share] for q in range(2) for i in range(img_dev)], axis=1
    ).astype(f32)
    pltpu.make_async_copy(both.at[1 - core], both.at[1 - core], both_recv).wait()
    table = both[...].reshape(2 * rows, width)

    def pick(asked, none, dead):
        at = lax.broadcasted_iota(i32, (asked.shape[0], 2 * rows), 1)
        chosen = jnp.where(asked == at, 1.0, 0.0)
        live = jnp.sum(chosen * count_row, axis=1, keepdims=True)
        live = jnp.where(asked < 0, none, live)
        found = dot(chosen.astype(bf16), table)
        slot_of = (lax.broadcasted_iota(i32, found.shape, 1) // DESC).astype(f32)
        return jnp.where(slot_of < live, found, dead).astype(bf16)

    for g in range(0, half, group):
        block = pick(found_at[g // group], float(kp), -far_entry)
        for i in range(g, g + group):
            q_out[i] = block[(i - g) * qn : (i - g + 1) * qn]

    def q_to(i):
        return q_out.at[i], q_in.at[side * half + i]

    def send_queries(i):
        for s in range(1, sides):
            remote(*q_to(i), q_send, q_recv.at[s, i], other(i), around(s) * 2 + core).start()
        if isinstance(i, int) and i == 0:
            @pl.when(core == 0)
            def _():
                pltpu.make_async_copy(*q_to(0), q_recv.at[0, 0]).start()

            @pl.when(core == 1)
            def _():
                remote(*q_to(0), q_send, q_recv.at[0, 0], other(0), r).start()
        else:
            remote(*q_to(i), q_send, q_recv.at[0, i], other(i), r).start()

    repeat(0, half - 1, lambda i: send_queries(half - 1 - i))
    send_queries(0)

    for g in range(0, half, group):
        picks = []
        for i in range(g, g + group):
            pltpu.make_async_copy(*list_to(i), list_recv.at[i]).wait()
            asked = lists_in[i : i + 1, 0 : 2 * slots]
            picks.append(column(asked.astype(f32), 2 * slots))
        block = pick(jnp.concatenate(picks, axis=0).astype(i32), 0.0, far_entry)
        for i in range(g, g + group):
            stack = stacked(block[(i - g) * 2 * slots : (i - g + 1) * 2 * slots])
            wide = stack.astype(f32)
            high, low = split(wide * wide)
            ones = jnp.ones(stack.shape, bf16)
            lhs[i] = jnp.concatenate([high, low, (-2.0 * wide).astype(bf16), ones, ones], axis=1)

    qd = qn * kp
    to = lax.broadcasted_iota(i32, (qd, sides * qd), 0)
    at = lax.broadcasted_iota(i32, (qd, sides * qd), 1) % qd
    order = jnp.where(at == (to % kp) * qn + to // kp, 1.0, 0.0).astype(bf16)
    ones = jnp.ones((qd, DESC), bf16)

    def one_pair(i):
        for s in range(sides):
            pltpu.make_async_copy(*q_to(i), q_recv.at[s, i]).wait()
        stack = jnp.concatenate([stacked(q_in[s * half + i]) for s in range(sides)], axis=0)
        query = dot(order, stack)
        high, low = split(query * query)
        rhs = jnp.concatenate([ones, ones, query.astype(bf16), high, low], axis=1)
        best, runner = lowest_two(dot_t(lhs[i], rhs))
        image = lists_in[pl.ds(i, 1), 0:1] // share
        image = jnp.broadcast_to(image.astype(f32), (1, qd))
        part_out[i] = jnp.minimum(
            jnp.concatenate([best, runner, image, image], axis=0), distant
        )
        j = other(i)
        place = own.at[side * n + me]
        for s in range(sides):
            for c in range(2):
                to_rep = around(s) * 2 + (core + c) % 2
                if s == 0 and c == 0 and isinstance(i, int) and i == 0:
                    @pl.when(core == 0)
                    def _():
                        pltpu.make_async_copy(part_out.at[i], place, own_recv).start()

                    @pl.when(core == 1)
                    def _():
                        remote(part_out.at[i], place, own_send, own_recv, j, to_rep).start()
                else:
                    remote(part_out.at[i], place, own_send, own_recv, j, to_rep).start()

    one_pair(0)
    repeat(1, half, one_pair)

    kept = arr.at[r]
    for s in range(sides):
        for c in range(2):
            if s or c:
                to_rep = around(s) * 2 + (core + c) % 2
                remote(part_out, kept, arr_send, arr_recv, me, to_rep).start()
    pltpu.make_async_copy(part_out, kept, arr_recv).start()

    def drain(ref, sem):
        pltpu.make_async_copy(ref, ref, sem).wait()

    drain(info.at[0], info_send)
    drain(both.at[0], both_send)
    @pl.when(core == 0)
    def _():
        drain(lists_in.at[pl.ds(0, half - 1)], list_send)
        drain(q_in.at[pl.ds(0, sides * half - 1)], q_send)
        drain(own.at[pl.ds(0, sides * n - 1)], own_send)

    @pl.when(core == 1)
    def _():
        drain(lists_in.at[pl.ds(0, half)], list_send)
        drain(q_in, q_send)
        drain(own, own_send)

    drain(arr.at[pl.ds(0, 2 * sides - 1)], arr_send)
    drain(own, own_recv)
    drain(arr, arr_recv)


def finish(n, sides, img_dev, own, arr, pairs, matches, scores):
    half = n // 2

    def gathered(pieces):
        two, image = (pieces[0][:, 0, :], pieces[0][:, 1, :]), pieces[0][:, 2, 0:1]
        for piece in pieces[1:]:
            two = merge(two, (piece[:, 0, :], piece[:, 1, :]))
        live = two[0] < 0.5 * distant
        best, runner = jnp.where(live, two[0], 0.0), jnp.where(live, two[1], 0.0)
        margin = jnp.where(live, (runner - best) / (runner + 1.0), 0.0)
        total = jnp.sum(margin, axis=1, keepdims=True)
        return best, runner, total / jnp.sum(live.astype(f32), axis=1, keepdims=True), image

    best, runner, score, _ = gathered([own[s * n : (s + 1) * n] for s in range(sides)])
    matches[:, 0, :] = best
    matches[:, 1, :] = runner
    other = [
        gathered([arr[s * 2 + c] for s in range(sides)])[2:] for c in range(2)
    ]
    first = column((pairs[0:1] % img_dev).astype(f32), n)
    for i in range(img_dev):
        total = jnp.sum(jnp.where(first == i, score, 0.0))
        for second_score, image in other:
            total = total + jnp.sum(jnp.where(image == i, second_score, 0.0))
        scores[i] = total


def on_device(n, m, descriptors, cell_counts, pair_images, query_cells, cand_cells, cand_counts):
    img_dev, share, width = descriptors.shape
    slots, qn = cand_cells.shape[2], query_cells.shape[1]
    qd = qn * width // DESC
    sides, half = m // 2, n // 2
    vmem = pl.BlockSpec(memory_space=pltpu.VMEM)
    dma = pltpu.SemaphoreType.DMA
    operands = (
        descriptors, cell_counts, pair_images.T, query_cells, cand_cells, cand_counts.T,
    )
    hbm = pl.BlockSpec(memory_space=pltpu.HBM)
    info_rows = (n + img_dev + 7) // 8 * 8
    own, arr = pl.pallas_call(
        functools.partial(kernel, n, sides),
        out_shape=(
            jax.ShapeDtypeStruct((sides * n, 4, qd), f32),
            jax.ShapeDtypeStruct((sides * 2, half, 4, qd), f32),
        ),
        in_specs=[hbm] * 6,
        out_specs=(hbm,) * 2,
        scratch_shapes=[
            pltpu.VMEM((2, *descriptors.shape), bf16),
            *(pltpu.VMEM(x.shape, x.dtype) for x in operands[1:]),
            dma((len(operands),)),
            pltpu.VMEM((2, info_rows, DESC), i32),
            pltpu.VMEM((n + (half + 7) // 8 * 8, DESC), i32),
            pltpu.VMEM(((half + 7) // 8 * 8, DESC), i32),
            pltpu.VMEM((half, qn, width), bf16),
            pltpu.VMEM((sides * half, qn, width), bf16),
            pltpu.VMEM((half, 2 * slots * width // DESC, 5 * DESC), bf16),
            pltpu.VMEM((half, 4, qd), f32),
            dma, dma, dma, dma, dma, dma((half,)),
            dma, dma((sides, half)), dma, dma, dma, dma,
        ],
        compiler_params=pltpu.CompilerParams(
            collective_id=0, has_side_effects=True
        ),
    )(*operands)
    return pl.pallas_call(
        functools.partial(finish, n, sides, img_dev),
        out_shape=(
            jax.ShapeDtypeStruct((n, 2, qd), f32),
            jax.ShapeDtypeStruct((img_dev,), f32),
        ),
        in_specs=[vmem] * 3,
        out_specs=(vmem, pl.BlockSpec(memory_space=pltpu.SMEM)),
    )(own, arr, pair_images.T)


def solution(mesh):
    n, m = mesh.shape["img"], mesh.shape["rep"]
    in_specs = (
        P("img", "rep", None),
        P("img", "rep"),
        P("img", None),
        P("img", None),
        P("img", "rep", None),
        P("img", "rep"),
    )
    out_specs = (P("img", None, None), P("img"))
    return jax.shard_map(
        functools.partial(on_device, n, m),
        mesh=mesh, in_specs=in_specs, out_specs=out_specs, check_vma=False,
    )
```

```python
import functools

import jax
import jax.numpy as jnp
from jax import lax
from jax.experimental import pallas as pl
from jax.experimental.pallas import tpu as pltpu
from jax.sharding import PartitionSpec as P

DESC = 128
MESH = pl.DeviceIdType.MESH
distant = 1.0e9
far_entry = 32768.0
f32, bf16, i32 = jnp.float32, jnp.bfloat16, jnp.int32


def partner(me, step, size):
    other, bit = 0, 1
    while bit < size:
        other = other + ((me // bit + step // bit) % 2) * bit
        bit *= 2
    return other


def repeat(first, last, body):
    if last - first <= 8:
        for t in range(first, last):
            body(t)
    else:
        lax.fori_loop(first, last, lambda t, c: (body(t), c)[1], 0)


def dot(a, b):
    return jnp.dot(a, b, preferred_element_type=f32)


def dot_t(a, b):
    return lax.dot_general(a, b, (((1,), (1,)), ((), ())), preferred_element_type=f32)


def split(square):
    high = square.astype(bf16)
    return high, (square - high.astype(f32)).astype(bf16)


def column(row, length):
    rows = lax.broadcasted_iota(i32, (length, length), 0)
    cols = lax.broadcasted_iota(i32, (length, length), 1)
    return jnp.sum(jnp.where(rows == cols, row, 0.0), axis=1, keepdims=True)


def merge(a, b):
    low = jnp.minimum(a[0], b[0])
    high = jnp.minimum(jnp.maximum(a[0], b[0]), jnp.minimum(a[1], b[1]))
    return low, high


def lowest_two(d):
    half = d.shape[0] // 2
    a, b = d[:half], d[half:]
    two = (jnp.minimum(a, b), jnp.maximum(a, b))
    while half > 1:
        half //= 2
        two = merge((two[0][:half], two[1][:half]), (two[0][half:], two[1][half:]))
    return two


def stacked(cells):
    kp = cells.shape[1] // DESC
    return jnp.concatenate([cells[:, s * DESC : (s + 1) * DESC] for s in range(kp)], axis=0)


def kernel(
    n, sides,
    desc_hbm, counts_hbm, pairs_hbm, qcells_hbm, ccells_hbm, ccounts_hbm,
    own, arr,
    both, counts, pairs, qcells, ccells, ccounts, in_sem,
    info, lists_out, lists_in, q_out, q_in, lhs, part_out,
    info_send, info_recv, both_send, both_recv, list_send, list_recv,
    q_send, q_recv, own_send, own_recv, arr_send, arr_recv, met,
):
    me, r = lax.axis_index("img"), lax.axis_index("rep")
    side, core = r // 2, r % 2
    mate = side * 2 + (1 - core)
    img_dev, share, width = both.shape[1:]
    rows = img_dev * share
    kp = width // DESC
    slots = ccells.shape[2]
    qn = qcells.shape[1]
    half = n // 2

    def remote(src, dst, send, recv, img, rep):
        return pltpu.make_async_remote_copy(
            src_ref=src, dst_ref=dst, send_sem=send, recv_sem=recv,
            device_id=(img, rep), device_id_type=MESH,
        )

    def other(i):
        return partner(me, 2 * i + core, n)

    barrier = pltpu.get_barrier_semaphore()

    def greet(img, rep):
        pl.semaphore_signal(barrier, inc=1, device_id=(img, rep), device_id_type=MESH)

    def around(s):
        return (side + s) % sides

    @pl.when(core == 1)
    def _():
        greet(me, mate)
        greet(other(0), side * 2 + 1)

    for s in range(1, sides):
        greet(other(0), around(s) * 2 + 1)

    def greet_all(i):
        for s in range(sides):
            greet(other(i), around(s) * 2 + 1)

    repeat(1, half, greet_all)

    small = [
        pltpu.make_async_copy(src, dst, in_sem.at[i])
        for i, (src, dst) in enumerate((
            (counts_hbm, counts), (pairs_hbm, pairs),
            (ccells_hbm, ccells), (ccounts_hbm, ccounts), (qcells_hbm, qcells),
        ))
    ]
    shard = pltpu.make_async_copy(desc_hbm, both.at[core], in_sem.at[len(small)])
    for load in small:
        load.start()
    shard.start()
    for load in small:
        load.wait()

    local = (pairs[...] % img_dev).astype(f32)
    first = column(local[0:1], n).astype(i32)
    second = column(local[1:2], n).astype(i32)
    live_cells = column(ccounts[...].astype(f32), n).astype(i32)
    wanted = core * rows + second * share + ccells[:, 0, :] % share
    wanted = jnp.where(lax.broadcasted_iota(i32, (n, slots), 1) < live_cells, wanted, -1)
    info[core, 0:n, 0:slots] = wanted
    info[core, n : n + img_dev, 0:share] = counts[...]

    cells = qcells[...]
    quarter = cells // share
    where = (quarter % 2) * rows + first * share + cells % share
    where = jnp.where(quarter // 2 == side, where, -1)
    lists_out[0:n, 0:qn] = where
    @pl.when(core == 0)
    def _():
        pl.semaphore_wait(barrier, 1)
        pl.semaphore_signal(met, inc=1, device_id=(me, mate), device_id_type=MESH)

    @pl.when(core == 1)
    def _():
        pl.semaphore_wait(met, 1)

    info_copy = remote(info.at[core], info.at[core], info_send, info_recv, me, mate)
    info_copy.start()
    shard.wait()
    shard_copy = remote(both.at[core], both.at[core], both_send, both_recv, me, mate)
    shard_copy.start()

    group = min(half, 4)
    found_at = []
    for g in range(0, half, group):
        picks = [
            column(lists_out[pl.ds(other(i), 1), 0:qn].astype(f32), qn) for i in range(g, g + group)
        ]
        found_at.append(jnp.concatenate(picks, axis=0).astype(i32))

    there = pltpu.make_async_copy(info.at[1 - core], info.at[1 - core], info_recv)
    there.wait()

    def send_list(i):
        j = other(i)
        lists_out[pl.ds(n + i, 1), 0:slots] = info[0, pl.ds(j, 1), 0:slots]
        lists_out[pl.ds(n + i, 1), slots : 2 * slots] = info[1, pl.ds(j, 1), 0:slots]

    repeat(0, half, send_list)

    def list_to(i):
        return lists_out.at[pl.ds(n + i, 1)], lists_in.at[pl.ds(i, 1)]

    count_row = jnp.concatenate(
        [info[q, n + i : n + i + 1, 0:share] for q in range(2) for i in range(img_dev)], axis=1
    ).astype(f32)
    pltpu.make_async_copy(both.at[1 - core], both.at[1 - core], both_recv).wait()
    table = both[...].reshape(2 * rows, width)

    def pick(asked, none, dead):
        at = lax.broadcasted_iota(i32, (asked.shape[0], 2 * rows), 1)
        chosen = jnp.where(asked == at, 1.0, 0.0)
        live = jnp.sum(chosen * count_row, axis=1, keepdims=True)
        live = jnp.where(asked < 0, none, live)
        found = dot(chosen.astype(bf16), table)
        slot_of = (lax.broadcasted_iota(i32, found.shape, 1) // DESC).astype(f32)
        return jnp.where(slot_of < live, found, dead).astype(bf16)

    for g in range(0, half, group):
        block = pick(found_at[g // group], float(kp), -far_entry)
        for i in range(g, g + group):
            q_out[i] = block[(i - g) * qn : (i - g + 1) * qn]

    def q_to(i):
        return q_out.at[i], q_in.at[side * half + i]

    def send_queries(i):
        for s in range(1, sides):
            remote(*q_to(i), q_send, q_recv.at[s, i], other(i), around(s) * 2 + core).start()
        if isinstance(i, int) and i == 0:
            @pl.when(core == 0)
            def _():
                pltpu.make_async_copy(*q_to(0), q_recv.at[0, 0]).start()

            @pl.when(core == 1)
            def _():
                remote(*q_to(0), q_send, q_recv.at[0, 0], other(0), r).start()
        else:
            remote(*q_to(i), q_send, q_recv.at[0, i], other(i), r).start()

    @pl.when(core == 0)
    def _():
        pl.semaphore_wait(met, 1)

    @pl.when(core == 1)
    def _():
        pl.semaphore_wait(barrier, n * sides - 1)
        pl.semaphore_signal(met, inc=1, device_id=(me, mate), device_id_type=MESH)

    @pl.when(core == 0)
    def _():
        pltpu.make_async_copy(*list_to(0), list_recv.at[0]).start()

    @pl.when(core == 1)
    def _():
        remote(*list_to(0), list_send, list_recv.at[0], other(0), r).start()

    repeat(1, half, lambda i: remote(*list_to(i), list_send, list_recv.at[i], other(i), r).start())

    repeat(0, half - 1, lambda i: send_queries(half - 1 - i))
    send_queries(0)

    for g in range(0, half, group):
        picks = []
        for i in range(g, g + group):
            pltpu.make_async_copy(*list_to(i), list_recv.at[i]).wait()
            asked = lists_in[i : i + 1, 0 : 2 * slots]
            picks.append(column(asked.astype(f32), 2 * slots))
        block = pick(jnp.concatenate(picks, axis=0).astype(i32), 0.0, far_entry)
        for i in range(g, g + group):
            stack = stacked(block[(i - g) * 2 * slots : (i - g + 1) * 2 * slots])
            wide = stack.astype(f32)
            high, low = split(wide * wide)
            ones = jnp.ones(stack.shape, bf16)
            lhs[i] = jnp.concatenate([high, low, (-2.0 * wide).astype(bf16), ones, ones], axis=1)

    qd = qn * kp
    to = lax.broadcasted_iota(i32, (qd, sides * qd), 0)
    at = lax.broadcasted_iota(i32, (qd, sides * qd), 1) % qd
    order = jnp.where(at == (to % kp) * qn + to // kp, 1.0, 0.0).astype(bf16)
    ones = jnp.ones((qd, DESC), bf16)

    def one_pair(i):
        for s in range(sides):
            pltpu.make_async_copy(*q_to(i), q_recv.at[s, i]).wait()
        stack = jnp.concatenate([stacked(q_in[s * half + i]) for s in range(sides)], axis=0)
        query = dot(order, stack)
        high, low = split(query * query)
        rhs = jnp.concatenate([ones, ones, query.astype(bf16), high, low], axis=1)
        best, runner = lowest_two(dot_t(lhs[i], rhs))
        image = lists_in[pl.ds(i, 1), 0:1] // share
        image = jnp.broadcast_to(image.astype(f32), (1, qd))
        part_out[i] = jnp.minimum(
            jnp.concatenate([best, runner, image, image], axis=0), distant
        )
        j = other(i)
        place = own.at[side * n + me]
        for s in range(sides):
            for c in range(2):
                to_rep = around(s) * 2 + (core + c) % 2
                if s == 0 and c == 0 and isinstance(i, int) and i == 0:
                    @pl.when(core == 0)
                    def _():
                        pltpu.make_async_copy(part_out.at[i], place, own_recv).start()

                    @pl.when(core == 1)
                    def _():
                        remote(part_out.at[i], place, own_send, own_recv, j, to_rep).start()
                else:
                    remote(part_out.at[i], place, own_send, own_recv, j, to_rep).start()

    one_pair(0)
    repeat(1, half, one_pair)

    kept = arr.at[r]
    for s in range(sides):
        for c in range(2):
            if s or c:
                to_rep = around(s) * 2 + (core + c) % 2
                remote(part_out, kept, arr_send, arr_recv, me, to_rep).start()
    pltpu.make_async_copy(part_out, kept, arr_recv).start()

    def drain(ref, sem):
        pltpu.make_async_copy(ref, ref, sem).wait()

    drain(info.at[0], info_send)
    drain(both.at[0], both_send)
    @pl.when(core == 0)
    def _():
        drain(lists_in.at[pl.ds(0, half - 1)], list_send)
        drain(q_in.at[pl.ds(0, sides * half - 1)], q_send)
        drain(own.at[pl.ds(0, sides * n - 1)], own_send)

    @pl.when(core == 1)
    def _():
        drain(lists_in.at[pl.ds(0, half)], list_send)
        drain(q_in, q_send)
        drain(own, own_send)

    drain(arr.at[pl.ds(0, 2 * sides - 1)], arr_send)
    drain(own, own_recv)
    drain(arr, arr_recv)


def finish(n, sides, img_dev, own, arr, pairs, matches, scores):
    half = n // 2

    def gathered(pieces):
        two, image = (pieces[0][:, 0, :], pieces[0][:, 1, :]), pieces[0][:, 2, 0:1]
        for piece in pieces[1:]:
            two = merge(two, (piece[:, 0, :], piece[:, 1, :]))
        live = two[0] < 0.5 * distant
        best, runner = jnp.where(live, two[0], 0.0), jnp.where(live, two[1], 0.0)
        margin = jnp.where(live, (runner - best) / (runner + 1.0), 0.0)
        total = jnp.sum(margin, axis=1, keepdims=True)
        return best, runner, total / jnp.sum(live.astype(f32), axis=1, keepdims=True), image

    best, runner, score, _ = gathered([own[s * n : (s + 1) * n] for s in range(sides)])
    matches[:, 0, :] = best
    matches[:, 1, :] = runner
    other = [
        gathered([arr[s * 2 + c] for s in range(sides)])[2:] for c in range(2)
    ]
    first = column((pairs[0:1] % img_dev).astype(f32), n)
    for i in range(img_dev):
        total = jnp.sum(jnp.where(first == i, score, 0.0))
        for second_score, image in other:
            total = total + jnp.sum(jnp.where(image == i, second_score, 0.0))
        scores[i] = total


def on_device(n, m, descriptors, cell_counts, pair_images, query_cells, cand_cells, cand_counts):
    img_dev, share, width = descriptors.shape
    slots, qn = cand_cells.shape[2], query_cells.shape[1]
    qd = qn * width // DESC
    sides, half = m // 2, n // 2
    vmem = pl.BlockSpec(memory_space=pltpu.VMEM)
    dma = pltpu.SemaphoreType.DMA
    operands = (
        descriptors, cell_counts, pair_images.T, query_cells, cand_cells, cand_counts.T,
    )
    hbm = pl.BlockSpec(memory_space=pltpu.HBM)
    info_rows = (n + img_dev + 7) // 8 * 8
    own, arr = pl.pallas_call(
        functools.partial(kernel, n, sides),
        out_shape=(
            jax.ShapeDtypeStruct((sides * n, 4, qd), f32),
            jax.ShapeDtypeStruct((sides * 2, half, 4, qd), f32),
        ),
        in_specs=[hbm] * 6,
        out_specs=(hbm,) * 2,
        scratch_shapes=[
            pltpu.VMEM((2, *descriptors.shape), bf16),
            *(pltpu.VMEM(x.shape, x.dtype) for x in operands[1:]),
            dma((len(operands),)),
            pltpu.VMEM((2, info_rows, DESC), i32),
            pltpu.VMEM((n + (half + 7) // 8 * 8, DESC), i32),
            pltpu.VMEM(((half + 7) // 8 * 8, DESC), i32),
            pltpu.VMEM((half, qn, width), bf16),
            pltpu.VMEM((sides * half, qn, width), bf16),
            pltpu.VMEM((half, 2 * slots * width // DESC, 5 * DESC), bf16),
            pltpu.VMEM((half, 4, qd), f32),
            dma, dma, dma, dma, dma, dma((half,)),
            dma, dma((sides, half)), dma, dma, dma, dma,
            pltpu.SemaphoreType.REGULAR,
        ],
        compiler_params=pltpu.CompilerParams(
            collective_id=0, has_side_effects=True
        ),
    )(*operands)
    return pl.pallas_call(
        functools.partial(finish, n, sides, img_dev),
        out_shape=(
            jax.ShapeDtypeStruct((n, 2, qd), f32),
            jax.ShapeDtypeStruct((img_dev,), f32),
        ),
        in_specs=[vmem] * 3,
        out_specs=(vmem, pl.BlockSpec(memory_space=pltpu.SMEM)),
    )(own, arr, pair_images.T)


def solution(mesh):
    n, m = mesh.shape["img"], mesh.shape["rep"]
    in_specs = (
        P("img", "rep", None),
        P("img", "rep"),
        P("img", None),
        P("img", None),
        P("img", "rep", None),
        P("img", "rep"),
    )
    out_specs = (P("img", None, None), P("img"))
    return jax.shard_map(
        functools.partial(on_device, n, m),
        mesh=mesh, in_specs=in_specs, out_specs=out_specs, check_vma=False,
    )
```

```python
import functools

import jax
import jax.numpy as jnp
from jax import lax
from jax.experimental import pallas as pl
from jax.experimental.pallas import tpu as pltpu
from jax.sharding import PartitionSpec as P

DESC = 128
MESH = pl.DeviceIdType.MESH
distant = 1.0e9
far_entry = 32768.0
f32, bf16, i32 = jnp.float32, jnp.bfloat16, jnp.int32


def flips(me, size):
    steps, bit = [], 1
    while bit < size:
        steps.append(bit - (me // bit) % 2 * (2 * bit))
        bit *= 2
    return steps


def repeat(first, last, body):
    if last - first <= 8:
        for t in range(first, last):
            body(t)
    else:
        lax.fori_loop(first, last, lambda t, c: (body(t), c)[1], 0)


def dot(a, b):
    return jnp.dot(a, b, preferred_element_type=f32)


def dot_t(a, b):
    return lax.dot_general(a, b, (((1,), (1,)), ((), ())), preferred_element_type=f32)


def split(square):
    high = square.astype(bf16)
    return high, (square - high.astype(f32)).astype(bf16)


def column(row, length):
    rows = lax.broadcasted_iota(i32, (length, length), 0)
    cols = lax.broadcasted_iota(i32, (length, length), 1)
    return jnp.sum(jnp.where(rows == cols, row, 0.0), axis=1, keepdims=True)


def merge(a, b):
    low = jnp.minimum(a[0], b[0])
    high = jnp.minimum(jnp.maximum(a[0], b[0]), jnp.minimum(a[1], b[1]))
    return low, high


def lowest_two(d):
    half = d.shape[0] // 2
    a, b = d[:half], d[half:]
    two = (jnp.minimum(a, b), jnp.maximum(a, b))
    while half > 1:
        half //= 2
        two = merge((two[0][:half], two[1][:half]), (two[0][half:], two[1][half:]))
    return two


def stacked(cells):
    kp = cells.shape[1] // DESC
    return jnp.concatenate([cells[:, s * DESC : (s + 1) * DESC] for s in range(kp)], axis=0)


def kernel(
    n, sides,
    desc_hbm, counts_hbm, pairs_hbm, qcells_hbm, ccells_hbm, ccounts_hbm,
    own, arr,
    both, counts, pairs, qcells, ccells, ccounts, in_sem,
    info, lists_in, asked_at, q_out, q_in, c_out, c_in, lhs, part_out,
    info_send, info_recv, both_send, both_recv, list_send, list_recv,
    q_send, q_recv, c_send, c_recv, own_send, own_recv, arr_send, arr_recv, met,
):
    me, r = lax.axis_index("img"), lax.axis_index("rep")
    side, core = r // 2, r % 2
    mate = side * 2 + (1 - core)
    across = (1 - side) * 2 + core
    img_dev, share, width = both.shape[1:]
    rows = img_dev * share
    kp = width // DESC
    slots = ccells.shape[2]
    qn = qcells.shape[1]
    half, near, far = n // 2, n // 4, n // 8

    def remote(src, dst, send, recv, img, rep):
        return pltpu.make_async_remote_copy(
            src_ref=src, dst_ref=dst, send_sem=send, recv_sem=recv,
            device_id=(img, rep), device_id_type=MESH,
        )

    def drain(ref, sem):
        pltpu.make_async_copy(ref, ref, sem).wait()

    steps = flips(me, n)
    base = me + core * steps[0]

    def other(i):
        if isinstance(i, int):
            return base + sum(step for k, step in enumerate(steps[1:]) if i >> k & 1)
        return base + sum(i // 2**k % 2 * step for k, step in enumerate(steps[1:]))

    barrier = pltpu.get_barrier_semaphore()

    def greet(img, rep):
        pl.semaphore_signal(barrier, inc=1, device_id=(img, rep), device_id_type=MESH)

    @pl.when(core == 1)
    def _():
        greet(me, mate)

    def greet_all(i):
        greet(other(i), side * 2 + 1)
        greet(other(i), (1 - side) * 2 + 1)

    repeat(0, half - 1, lambda i: greet_all(half - 1 - i))
    greet(other(0), (1 - side) * 2 + 1)

    @pl.when(core == 1)
    def _():
        greet(other(0), side * 2 + 1)

    small = [
        pltpu.make_async_copy(src, dst, in_sem.at[i])
        for i, (src, dst) in enumerate((
            (counts_hbm, counts), (pairs_hbm, pairs),
            (ccells_hbm, ccells), (ccounts_hbm, ccounts), (qcells_hbm, qcells),
        ))
    ]
    shard = pltpu.make_async_copy(desc_hbm, both.at[core], in_sem.at[len(small)])
    for load in small:
        load.start()
    shard.start()
    for load in small:
        load.wait()

    local = (pairs[...] % img_dev).astype(f32)
    first = column(local[0:1], n).astype(i32)
    second = column(local[1:2], n).astype(i32)
    live_cells = column(ccounts[...].astype(f32), n).astype(i32)
    wanted = core * rows + second * share + ccells[:, 0, :] % share
    wanted = jnp.where(lax.broadcasted_iota(i32, (n, slots), 1) < live_cells, wanted, -1)
    info[core, 0:n, 0:slots] = wanted
    info[core, n : n + img_dev, 0:share] = counts[...]

    @pl.when(core == 0)
    def _():
        pl.semaphore_wait(barrier, 1)
        pl.semaphore_signal(met, inc=1, device_id=(me, mate), device_id_type=MESH)

    @pl.when(core == 1)
    def _():
        pl.semaphore_wait(met, 1)

    remote(info.at[core], info.at[core], info_send, info_recv, me, mate).start()
    shard.wait()
    remote(both.at[core], both.at[core], both_send, both_recv, me, mate).start()

    cells = qcells[...]
    quarter = cells // share
    where = (quarter % 2) * rows + first * share + cells % share
    asked_at[...] = jnp.where(quarter // 2 == side, where, -1)
    group = min(half, 4)
    found_at = []
    for g in range(0, half, group):
        picks = [
            column(asked_at[pl.ds(other(i), 1), :].astype(f32), qn) for i in range(g, g + group)
        ]
        found_at.append(jnp.concatenate(picks, axis=0).astype(i32))

    pltpu.make_async_copy(info.at[1 - core], info.at[1 - core], info_recv).wait()

    @pl.when(core == 0)
    def _():
        pl.semaphore_wait(met, 1)

    @pl.when(core == 1)
    def _():
        pl.semaphore_wait(barrier, n * sides - 1)
        pl.semaphore_signal(met, inc=1, device_id=(me, mate), device_id_type=MESH)

    def list_to(i):
        return info.at[:, pl.ds(other(i), 1)], lists_in.at[:, pl.ds(i, 1)]

    def send_list(i):
        remote(*list_to(i), list_send, list_recv.at[i], other(i), r).start()

    repeat(0, half - 1, lambda i: send_list(half - 1 - i))

    @pl.when(core == 0)
    def _():
        pltpu.make_async_copy(*list_to(0), list_recv.at[0]).start()

    @pl.when(core == 1)
    def _():
        send_list(0)

    count_row = jnp.concatenate(
        [info[q, n + i : n + i + 1, 0:share] for q in range(2) for i in range(img_dev)], axis=1
    ).astype(f32)
    pltpu.make_async_copy(both.at[1 - core], both.at[1 - core], both_recv).wait()
    table = both[...].reshape(2 * rows, width)

    def pick(asked, none, dead):
        at = lax.broadcasted_iota(i32, (asked.shape[0], 2 * rows), 1)
        chosen = jnp.where(asked == at, 1.0, 0.0)
        live = jnp.sum(chosen * count_row, axis=1, keepdims=True)
        live = jnp.where(asked < 0, none, live)
        found = dot(chosen.astype(bf16), table)
        slot_of = (lax.broadcasted_iota(i32, found.shape, 1) // DESC).astype(f32)
        return jnp.where(slot_of < live, found, dead).astype(bf16)

    for g in range(0, half, group):
        block = pick(found_at[g // group], float(kp), -far_entry)
        for i in range(g, g + group):
            q_out[i] = block[(i - g) * qn : (i - g + 1) * qn]

    def q_to(i):
        return q_out.at[i], q_in.at[side * half + i]

    def send_far(i):
        to_side = (i - near) % 2
        remote(*q_to(i), q_send, q_recv.at[(side + to_side) % 2, i], other(i), to_side * 2 + core).start()

    def send_near(i):
        remote(*q_to(i), q_send, q_recv.at[1, i], other(i), across).start()
        remote(*q_to(i), q_send, q_recv.at[0, i], other(i), r).start()

    repeat(0, half - near, lambda i: send_far(half - 1 - i))
    repeat(0, near - 1, lambda i: send_near(near - 1 - i))
    remote(*q_to(0), q_send, q_recv.at[1, 0], other(0), across).start()

    @pl.when(core == 0)
    def _():
        pltpu.make_async_copy(*q_to(0), q_recv.at[0, 0]).start()

    @pl.when(core == 1)
    def _():
        remote(*q_to(0), q_send, q_recv.at[0, 0], other(0), r).start()

    def candidates(indices):
        picks = []
        for i in indices:
            ref = lists_in.at[:, pl.ds(i, 1)]
            pltpu.make_async_copy(ref, ref, list_recv.at[i]).wait()
            for q in range(2):
                asked = lists_in[q, pl.ds(i, 1), 0:slots]
                picks.append(column(asked.astype(f32), slots))
        return pick(jnp.concatenate(picks, axis=0).astype(i32), 0.0, far_entry)

    def prepared(block):
        wide = stacked(block).astype(f32)
        high, low = split(wide * wide)
        ones = jnp.ones(wide.shape, bf16)
        return jnp.concatenate([high, low, (-2.0 * wide).astype(bf16), ones, ones], axis=1)

    cn = 2 * slots
    given = [near + 2 * p + 1 - side for p in range(far)]
    taken = [near + 2 * p + side for p in range(far)]
    for g in range(0, far, group):
        block = candidates(given[g : g + group])
        for p in range(g, min(g + group, far)):
            c_out[p] = block[(p - g) * cn : (p - g + 1) * cn]
            remote(c_out.at[p], c_in.at[p], c_send, c_recv.at[p], me, across).start()

    kept = [*range(near), *taken]
    for g in range(0, len(kept), group):
        block = candidates(kept[g : g + group])
        for p in range(g, min(g + group, len(kept))):
            at = p if p < near else 2 * p - near
            lhs[at] = prepared(block[(p - g) * cn : (p - g + 1) * cn])

    qd = qn * kp
    to = lax.broadcasted_iota(i32, (qd, sides * qd), 0)
    at = lax.broadcasted_iota(i32, (qd, sides * qd), 1) % qd
    order = jnp.where(at == (to % kp) * qn + to // kp, 1.0, 0.0).astype(bf16)
    ones = jnp.ones((qd, DESC), bf16)

    def queries(i):
        stack = []
        for s in range(sides):
            ref = q_in.at[s * half + i]
            pltpu.make_async_copy(ref, ref, q_recv.at[s, i]).wait()
        for s in range(sides):
            stack.append(stacked(q_in[s * half + i]))
        query = dot(order, jnp.concatenate(stack, axis=0))
        high, low = split(query * query)
        return jnp.concatenate([ones, ones, query.astype(bf16), high, low], axis=1)

    def result(p, i, dist):
        best, runner = lowest_two(dist)
        image = lists_in[0, pl.ds(i, 1), 0:1] // share
        image = jnp.broadcast_to(image.astype(f32), (1, qd))
        part_out[p] = jnp.minimum(
            jnp.concatenate([best, runner, image, image], axis=0), distant
        )

    def to_owner(p, j, place, skip=False):
        if not skip:
            remote(part_out.at[p], place, own_send, own_recv, j, r).start()
        for to_rep in (mate, across, (1 - side) * 2 + (1 - core)):
            remote(part_out.at[p], place, own_send, own_recv, j, to_rep).start()

    def to_group(ref, place):
        for to_rep in (mate, across, (1 - side) * 2 + (1 - core)):
            remote(ref, place, arr_send, arr_recv, me, to_rep).start()
        pltpu.make_async_copy(ref, place, arr_recv).start()

    def near_pair(i):
        result(i, i, dot_t(lhs[i], queries(i)))

    near_pair(0)
    to_owner(0, other(0), own.at[side * n + me], skip=True)

    @pl.when(core == 0)
    def _():
        pltpu.make_async_copy(part_out.at[0], own.at[side * n + me], own_recv).start()

    @pl.when(core == 1)
    def _():
        remote(part_out.at[0], own.at[side * n + me], own_send, own_recv, other(0), r).start()

    def near_step(i):
        near_pair(i)
        to_owner(i, other(i), own.at[side * n + me])

    repeat(1, near, near_step)
    to_group(part_out.at[pl.ds(0, near)], arr.at[pl.ds(r * near, near)])

    def far_step(p):
        i = near + 2 * p + side
        pltpu.make_async_copy(c_in.at[p], c_in.at[p], c_recv.at[p]).wait()
        lhs[near + 2 * p + 1] = prepared(c_in[p])
        two = lhs[pl.ds(near + 2 * p, 2)].reshape(sides * cn * kp, 5 * DESC)
        result(near + p, i, dot_t(two, queries(i)))
        to_owner(near + p, other(i), own.at[me])

    repeat(0, far, far_step)
    to_group(part_out.at[pl.ds(near, far)], arr.at[pl.ds(n + r * far, far)])

    drain(info.at[0], info_send)
    drain(both.at[0], both_send)
    drain(c_in, c_send)
    sent = half + near

    @pl.when(core == 0)
    def _():
        drain(lists_in.at[:, pl.ds(0, half - 1)], list_send)
        drain(q_in.at[pl.ds(0, sent - 1)], q_send)
        drain(own.at[pl.ds(0, n + half - 1)], own_send)

    @pl.when(core == 1)
    def _():
        drain(lists_in.at[:, pl.ds(0, half)], list_send)
        drain(q_in.at[pl.ds(0, sent)], q_send)
        drain(own.at[pl.ds(0, n + half)], own_send)

    drain(arr.at[pl.ds(0, 3 * (near + far))], arr_send)
    drain(own.at[pl.ds(0, n + half)], own_recv)
    drain(arr, arr_recv)


def finish(n, img_dev, own, arr, pairs, matches, scores):
    half = n // 2

    def pair(ref, first, last):
        return ref[first:last, 0, :], ref[first:last, 1, :]

    def scored(two):
        live = two[0] < 0.5 * distant
        best, runner = jnp.where(live, two[0], 0.0), jnp.where(live, two[1], 0.0)
        margin = jnp.where(live, (runner - best) / (runner + 1.0), 0.0)
        total = jnp.sum(margin, axis=1, keepdims=True)
        return best, runner, total / jnp.sum(live.astype(f32), axis=1, keepdims=True)

    whole = pair(own, 0, n)
    halves = merge(whole, pair(own, n, 2 * n))
    mine = lax.axis_index("img") // half
    is_near = lax.broadcasted_iota(i32, whole[0].shape, 0) // half == mine
    best, runner, score = scored([jnp.where(is_near, a, b) for a, b in zip(halves, whole)])
    matches[:, 0, :] = best
    matches[:, 1, :] = runner
    first = column((pairs[0:1] % img_dev).astype(f32), n)

    def per_image(image, score):
        at = lax.broadcasted_iota(i32, (image.shape[0], img_dev), 1).astype(f32)
        return jnp.sum(jnp.where(image == at, score, 0.0), axis=0)

    close = merge(pair(arr, 0, half), pair(arr, half, n))
    apart = pair(arr, n, n + half)
    total = per_image(first, score)
    total = total + per_image(arr[0:half, 2, 0:1], scored(close)[2])
    scores[...] = total + per_image(arr[n : n + half, 2, 0:1], scored(apart)[2])


def on_device(n, m, descriptors, cell_counts, pair_images, query_cells, cand_cells, cand_counts):
    img_dev, share, width = descriptors.shape
    slots, qn = cand_cells.shape[2], query_cells.shape[1]
    qd = qn * width // DESC
    sides, half, far = m // 2, n // 2, n // 8
    vmem = pl.BlockSpec(memory_space=pltpu.VMEM)
    dma = pltpu.SemaphoreType.DMA
    operands = (
        descriptors, cell_counts, pair_images.T, query_cells, cand_cells, cand_counts.T,
    )
    hbm = pl.BlockSpec(memory_space=pltpu.HBM)
    info_rows = (n + img_dev + 7) // 8 * 8
    own, arr = pl.pallas_call(
        functools.partial(kernel, n, sides),
        out_shape=(
            pltpu.VMEM((sides * n, 4, qd), f32),
            pltpu.VMEM((n + half, 4, qd), f32),
        ),
        in_specs=[hbm] * 6,
        out_specs=(vmem,) * 2,
        scratch_shapes=[
            pltpu.VMEM((2, *descriptors.shape), bf16),
            *(pltpu.VMEM(x.shape, x.dtype) for x in operands[1:]),
            dma((len(operands),)),
            pltpu.VMEM((2, info_rows, DESC), i32),
            pltpu.VMEM((2, (half + 7) // 8 * 8, DESC), i32),
            pltpu.VMEM(query_cells.shape, i32),
            pltpu.VMEM((half, qn, width), bf16),
            pltpu.VMEM((sides * half, qn, width), bf16),
            pltpu.VMEM((far, 2 * slots, width), bf16),
            pltpu.VMEM((far, 2 * slots, width), bf16),
            pltpu.VMEM((half, 2 * slots * width // DESC, 5 * DESC), bf16),
            pltpu.VMEM((half // 2 + far, 4, qd), f32),
            dma, dma, dma, dma, dma, dma((half,)),
            dma, dma((sides, half)), dma, dma((far,)), dma, dma, dma, dma,
            pltpu.SemaphoreType.REGULAR,
        ],
        compiler_params=pltpu.CompilerParams(
            collective_id=0, has_side_effects=True
        ),
    )(*operands)
    held = functools.partial(pltpu.with_memory_space_constraint, memory_space=pltpu.VMEM)
    return pl.pallas_call(
        functools.partial(finish, n, img_dev),
        out_shape=(
            jax.ShapeDtypeStruct((n, 2, qd), f32),
            jax.ShapeDtypeStruct((img_dev,), f32),
        ),
        in_specs=[vmem] * 3,
        out_specs=(vmem, vmem),
    )(held(own), held(arr), pair_images.T)


def solution(mesh):
    n, m = mesh.shape["img"], mesh.shape["rep"]
    in_specs = (
        P("img", "rep", None),
        P("img", "rep"),
        P("img", None),
        P("img", None),
        P("img", "rep", None),
        P("img", "rep"),
    )
    out_specs = (P("img", None, None), P("img"))
    return jax.shard_map(
        functools.partial(on_device, n, m),
        mesh=mesh, in_specs=in_specs, out_specs=out_specs, check_vma=False,
    )
```

```python
import functools

import jax
import jax.numpy as jnp
from jax import lax
from jax.experimental import pallas as pl
from jax.experimental.pallas import tpu as pltpu
from jax.sharding import PartitionSpec as P

DESC = 128
MESH = pl.DeviceIdType.MESH
distant = 1.0e9
far_entry = 32768.0
f32, bf16, i32 = jnp.float32, jnp.bfloat16, jnp.int32


def flips(me, size):
    steps, bit = [], 1
    while bit < size:
        steps.append(bit - (me // bit) % 2 * (2 * bit))
        bit *= 2
    return steps


def repeat(first, last, body):
    if last - first <= 8:
        for t in range(first, last):
            body(t)
    else:
        lax.fori_loop(first, last, lambda t, c: (body(t), c)[1], 0)


def dot(a, b):
    return jnp.dot(a, b, preferred_element_type=f32)


def dot_t(a, b):
    return lax.dot_general(a, b, (((1,), (1,)), ((), ())), preferred_element_type=f32)


def split(square):
    high = square.astype(bf16)
    return high, (square - high.astype(f32)).astype(bf16)


def column(row, length):
    rows = lax.broadcasted_iota(i32, (length, length), 0)
    cols = lax.broadcasted_iota(i32, (length, length), 1)
    return jnp.sum(jnp.where(rows == cols, row, 0.0), axis=1, keepdims=True)


def merge(a, b):
    low = jnp.minimum(a[0], b[0])
    high = jnp.minimum(jnp.maximum(a[0], b[0]), jnp.minimum(a[1], b[1]))
    return low, high


def lowest_two(d):
    half = d.shape[0] // 2
    a, b = d[:half], d[half:]
    two = (jnp.minimum(a, b), jnp.maximum(a, b))
    while half > 1:
        half //= 2
        two = merge((two[0][:half], two[1][:half]), (two[0][half:], two[1][half:]))
    return two


def stacked(cells):
    kp = cells.shape[1] // DESC
    return jnp.concatenate([cells[:, s * DESC : (s + 1) * DESC] for s in range(kp)], axis=0)


def kernel(
    n, sides,
    desc_hbm, counts_hbm, pairs_hbm, qcells_hbm, ccells_hbm, ccounts_hbm,
    own, arr,
    both, counts, pairs, qcells, ccells, ccounts, in_sem,
    info, lists_in, asked_at, q_out, q_in, c_out, c_in, lhs, rhs, part_out,
    info_send, info_recv, both_send, both_recv, list_send, list_recv,
    q_send, q_recv, c_send, c_recv, own_send, own_recv, arr_send, arr_recv, met,
):
    me, r = lax.axis_index("img"), lax.axis_index("rep")
    side, core = r // 2, r % 2
    mate = side * 2 + (1 - core)
    across = (1 - side) * 2 + core
    img_dev, share, width = both.shape[1:]
    rows = img_dev * share
    kp = width // DESC
    slots = ccells.shape[2]
    qn = qcells.shape[1]
    half, mine = n // 2, n // 4

    def remote(src, dst, send, recv, img, rep):
        return pltpu.make_async_remote_copy(
            src_ref=src, dst_ref=dst, send_sem=send, recv_sem=recv,
            device_id=(img, rep), device_id_type=MESH,
        )

    def drain(ref, sem):
        pltpu.make_async_copy(ref, ref, sem).wait()

    steps = flips(me, n)
    base = me + core * steps[-1]

    def other(i):
        if isinstance(i, int):
            return base + sum(step for k, step in enumerate(steps[:-1]) if i >> k & 1)
        return base + sum(i // 2**k % 2 * step for k, step in enumerate(steps[:-1]))

    barrier = pltpu.get_barrier_semaphore()

    def greet(img, rep):
        pl.semaphore_signal(barrier, inc=1, device_id=(img, rep), device_id_type=MESH)

    @pl.when(core == 0)
    def _():
        def greet_near(i):
            greet(other(i), r)
            greet(other(i), across)

        repeat(0, half - 1, lambda i: greet_near(half - 1 - i))
        greet(other(0), across)

    @pl.when(core == 1)
    def _():
        greet(me, mate)
        repeat(0, half, lambda i: greet(other(half - 1 - i), r))
        repeat(0, mine, lambda p: greet(other(2 * (mine - 1 - p) + side), across))

    small = [
        pltpu.make_async_copy(src, dst, in_sem.at[i])
        for i, (src, dst) in enumerate((
            (counts_hbm, counts), (pairs_hbm, pairs),
            (ccells_hbm, ccells), (ccounts_hbm, ccounts), (qcells_hbm, qcells),
        ))
    ]
    shard = pltpu.make_async_copy(desc_hbm, both.at[core], in_sem.at[len(small)])
    for load in small:
        load.start()
    shard.start()
    for load in small:
        load.wait()

    local = (pairs[...] % img_dev).astype(f32)
    first = column(local[0:1], n).astype(i32)
    second = column(local[1:2], n).astype(i32)
    live_cells = column(ccounts[...].astype(f32), n).astype(i32)
    wanted = core * rows + second * share + ccells[:, 0, :] % share
    wanted = jnp.where(lax.broadcasted_iota(i32, (n, slots), 1) < live_cells, wanted, -1)
    info[core, 0:n, 0:slots] = wanted
    info[core, n : n + img_dev, 0:share] = counts[...]

    @pl.when(core == 0)
    def _():
        pl.semaphore_wait(barrier, 2 * half)
        pl.semaphore_signal(met, inc=1, device_id=(me, mate), device_id_type=MESH)

    @pl.when(core == 1)
    def _():
        pl.semaphore_wait(met, 1)

    remote(info.at[core], info.at[core], info_send, info_recv, me, mate).start()
    shard.wait()
    remote(both.at[core], both.at[core], both_send, both_recv, me, mate).start()

    cells = qcells[...]
    quarter = cells // share
    where = (quarter % 2) * rows + first * share + cells % share
    asked_at[...] = jnp.where(quarter // 2 == side, where, -1)
    group = min(half, 4)
    found_at = []
    for g in range(0, half, group):
        picks = [
            column(asked_at[pl.ds(other(i), 1), :].astype(f32), qn) for i in range(g, g + group)
        ]
        found_at.append(jnp.concatenate(picks, axis=0).astype(i32))

    pltpu.make_async_copy(info.at[1 - core], info.at[1 - core], info_recv).wait()

    def list_to(i):
        return info.at[:, pl.ds(other(i), 1)], lists_in.at[:, pl.ds(i, 1)]

    def send_list(i):
        remote(*list_to(i), list_send, list_recv.at[i], other(i), r).start()

    @pl.when(core == 0)
    def _():
        repeat(0, half - 1, lambda i: send_list(half - 1 - i))
        pltpu.make_async_copy(*list_to(0), list_recv.at[0]).start()

    @pl.when(core == 1)
    def _():
        pl.semaphore_wait(barrier, half + mine)
        repeat(0, half, lambda i: send_list(half - 1 - i))

    count_row = jnp.concatenate(
        [info[q, n + i : n + i + 1, 0:share] for q in range(2) for i in range(img_dev)], axis=1
    ).astype(f32)
    pltpu.make_async_copy(both.at[1 - core], both.at[1 - core], both_recv).wait()

    def pick(asked, none, dead):
        at = lax.broadcasted_iota(i32, (asked.shape[0], 2 * rows), 1)
        chosen = jnp.where(asked == at, 1.0, 0.0)
        live = jnp.sum(chosen * count_row, axis=1, keepdims=True)
        live = jnp.where(asked < 0, none, live)
        found = dot(chosen.astype(bf16), both[...].reshape(2 * rows, width))
        slot_of = (lax.broadcasted_iota(i32, found.shape, 1) // DESC).astype(f32)
        return jnp.where(slot_of < live, found, dead).astype(bf16)

    for g in range(0, half, group):
        block = pick(found_at[g // group], float(kp), -far_entry)
        for i in range(g, g + group):
            q_out[i] = block[(i - g) * qn : (i - g + 1) * qn]

    def q_to(i):
        return q_out.at[i], q_in.at[side * half + i]

    def candidates(indices):
        picks = []
        for i in indices:
            ref = lists_in.at[:, pl.ds(i, 1)]
            pltpu.make_async_copy(ref, ref, list_recv.at[i]).wait()
            for q in range(2):
                asked = lists_in[q, pl.ds(i, 1), 0:slots]
                picks.append(column(asked.astype(f32), slots))
        return pick(jnp.concatenate(picks, axis=0).astype(i32), 0.0, far_entry)

    def prepared(block):
        wide = stacked(block).astype(f32)
        high, low = split(wide * wide)
        ones = jnp.ones(wide.shape, bf16)
        return jnp.concatenate([high, low, (-2.0 * wide).astype(bf16), ones, ones], axis=1)

    cn = 2 * slots

    def prepare(indices, place):
        for g in range(0, len(indices), group):
            block = candidates(indices[g : g + group])
            for p in range(g, min(g + group, len(indices))):
                lhs[place(p)] = prepared(block[(p - g) * cn : (p - g + 1) * cn])

    qd = qn * kp

    def queries(i):
        for s in range(sides):
            ref = q_in.at[s * half + i]
            pltpu.make_async_copy(ref, ref, q_recv.at[s, i]).wait()
        to = lax.broadcasted_iota(i32, (qd, sides * qd), 0)
        at = lax.broadcasted_iota(i32, (qd, sides * qd), 1) % qd
        order = jnp.where(at == (to % kp) * qn + to // kp, 1.0, 0.0).astype(bf16)
        stack = jnp.concatenate([stacked(q_in[s * half + i]) for s in range(sides)], axis=0)
        query = dot(order, stack)
        high, low = split(query * query)
        ones = jnp.ones((qd, DESC), bf16)
        return jnp.concatenate([ones, ones, query.astype(bf16), high, low], axis=1)

    def keep(p, i, two):
        image = lists_in[0, pl.ds(i, 1), 0:1] // share
        image = jnp.broadcast_to(image.astype(f32), (1, qd))
        part_out[p] = jnp.minimum(jnp.concatenate([*two, image, image], axis=0), distant)

    everyone = [s * 2 + c for s in range(sides) for c in range(2)]
    others = (across, mate, (1 - side) * 2 + (1 - core))

    def to_owner(p, j, place):
        for to_rep in everyone:
            remote(part_out.at[p], place, own_send, own_recv, j, to_rep).start()

    def to_group(ref, place):
        for to_rep in others:
            remote(ref, place, arr_send, arr_recv, me, to_rep).start()
        pltpu.make_async_copy(ref, place, arr_recv).start()

    @pl.when(core == 0)
    def _():
        def send_near(i):
            remote(*q_to(i), q_send, q_recv.at[1, i], other(i), across).start()
            remote(*q_to(i), q_send, q_recv.at[0, i], other(i), r).start()

        repeat(0, half - 1, lambda i: send_near(half - 1 - i))
        remote(*q_to(0), q_send, q_recv.at[1, 0], me, across).start()
        pltpu.make_async_copy(*q_to(0), q_recv.at[0, 0]).start()

        prepare(list(range(half)), lambda p: p)
        place = own.at[side * n + me]

        def near_pair(i):
            keep(i, i, lowest_two(dot_t(lhs[i], queries(i))))

        near_pair(0)
        for to_rep in others:
            remote(part_out.at[0], place, own_send, own_recv, me, to_rep).start()
        pltpu.make_async_copy(part_out.at[0], place, own_recv).start()

        def near_step(i):
            near_pair(i)
            to_owner(i, other(i), place)

        repeat(1, half, near_step)
        to_group(part_out, arr.at[pl.ds(side * half, half)])

    @pl.when(core == 1)
    def _():
        def send_far(i):
            to_side = i % 2
            remote(
                *q_to(i), q_send, q_recv.at[(side + to_side) % 2, i], other(i), to_side * 2 + 1
            ).start()

        repeat(0, half, lambda i: send_far(half - 1 - i))

        for g in range(0, mine, group):
            given = [2 * p + 1 - side for p in range(g, min(g + group, mine))]
            block = candidates(given)
            for p in range(g, min(g + group, mine)):
                c_out[p] = block[(p - g) * cn : (p - g + 1) * cn]
                remote(c_out.at[p], c_in.at[p], c_send, c_recv.at[p], me, across).start()

        prepare([2 * p + side for p in range(mine)], lambda p: p)

        def far_first(p):
            i = 2 * p + side
            rhs[p] = queries(i)
            keep(p, i, lowest_two(dot_t(lhs[p], rhs[p])))

        repeat(0, mine, far_first)

        def far_last(p):
            pltpu.make_async_copy(c_in.at[p], c_in.at[p], c_recv.at[p]).wait()
            two = lowest_two(dot_t(prepared(c_in[p]), rhs[p]))
            before = part_out[p]
            i = 2 * p + side
            keep(p, i, merge((before[0:1], before[1:2]), two))
            to_owner(p, other(i), own.at[me])

        repeat(0, mine, far_last)
        to_group(part_out.at[pl.ds(0, mine)], arr.at[pl.ds(n + side * mine, mine)])

    drain(info.at[0], info_send)
    drain(both.at[0], both_send)

    @pl.when(core == 0)
    def _():
        drain(lists_in.at[:, pl.ds(0, half - 1)], list_send)
        drain(q_in.at[pl.ds(0, n - 1)], q_send)
        drain(own.at[pl.ds(0, 2 * n - 1)], own_send)
        drain(arr, arr_send)

    @pl.when(core == 1)
    def _():
        drain(lists_in.at[:, pl.ds(0, half)], list_send)
        drain(q_in.at[pl.ds(0, half)], q_send)
        drain(c_in, c_send)
        drain(own.at[pl.ds(0, n)], own_send)
        drain(arr.at[pl.ds(0, 3 * mine)], arr_send)

    drain(own.at[pl.ds(0, n + half)], own_recv)
    drain(arr, arr_recv)


def finish(n, img_dev, own, arr, pairs, matches, scores):
    half = n // 2

    def pair(ref, first, last):
        return ref[first:last, 0, :], ref[first:last, 1, :]

    def scored(two):
        live = two[0] < 0.5 * distant
        best, runner = jnp.where(live, two[0], 0.0), jnp.where(live, two[1], 0.0)
        margin = jnp.where(live, (runner - best) / (runner + 1.0), 0.0)
        total = jnp.sum(margin, axis=1, keepdims=True)
        return best, runner, total / jnp.sum(live.astype(f32), axis=1, keepdims=True)

    whole = pair(own, 0, n)
    halves = merge(whole, pair(own, n, 2 * n))
    mine = lax.axis_index("img") // half
    is_near = lax.broadcasted_iota(i32, whole[0].shape, 0) // half == mine
    best, runner, score = scored([jnp.where(is_near, a, b) for a, b in zip(halves, whole)])
    matches[:, 0, :] = best
    matches[:, 1, :] = runner
    first = column((pairs[0:1] % img_dev).astype(f32), n)

    def per_image(image, score):
        at = lax.broadcasted_iota(i32, (image.shape[0], img_dev), 1).astype(f32)
        return jnp.sum(jnp.where(image == at, score, 0.0), axis=0)

    close = merge(pair(arr, 0, half), pair(arr, half, n))
    apart = pair(arr, n, n + half)
    total = per_image(first, score)
    total = total + per_image(arr[0:half, 2, 0:1], scored(close)[2])
    scores[...] = total + per_image(arr[n : n + half, 2, 0:1], scored(apart)[2])


def on_device(n, m, descriptors, cell_counts, pair_images, query_cells, cand_cells, cand_counts):
    img_dev, share, width = descriptors.shape
    slots, qn = cand_cells.shape[2], query_cells.shape[1]
    qd = qn * width // DESC
    sides, half, mine = m // 2, n // 2, n // 4
    vmem = pl.BlockSpec(memory_space=pltpu.VMEM)
    dma = pltpu.SemaphoreType.DMA
    operands = (
        descriptors, cell_counts, pair_images.T, query_cells, cand_cells, cand_counts.T,
    )
    hbm = pl.BlockSpec(memory_space=pltpu.HBM)
    info_rows = (n + img_dev + 7) // 8 * 8
    own, arr = pl.pallas_call(
        functools.partial(kernel, n, sides),
        out_shape=(
            pltpu.VMEM((sides * n, 4, qd), f32),
            pltpu.VMEM((n + half, 4, qd), f32),
        ),
        in_specs=[hbm] * 6,
        out_specs=(vmem,) * 2,
        scratch_shapes=[
            pltpu.VMEM((2, *descriptors.shape), bf16),
            *(pltpu.VMEM(x.shape, x.dtype) for x in operands[1:]),
            dma((len(operands),)),
            pltpu.VMEM((2, info_rows, DESC), i32),
            pltpu.VMEM((2, (half + 7) // 8 * 8, DESC), i32),
            pltpu.VMEM(query_cells.shape, i32),
            pltpu.VMEM((half, qn, width), bf16),
            pltpu.VMEM((sides * half, qn, width), bf16),
            pltpu.VMEM((mine, 2 * slots, width), bf16),
            pltpu.VMEM((mine, 2 * slots, width), bf16),
            pltpu.VMEM((half, 2 * slots * width // DESC, 5 * DESC), bf16),
            pltpu.VMEM((mine, qd, 5 * DESC), bf16),
            pltpu.VMEM((half, 4, qd), f32),
            dma, dma, dma, dma, dma, dma((half,)),
            dma, dma((sides, half)), dma, dma((mine,)), dma, dma, dma, dma,
            pltpu.SemaphoreType.REGULAR,
        ],
        compiler_params=pltpu.CompilerParams(
            collective_id=0, has_side_effects=True
        ),
    )(*operands)
    held = functools.partial(pltpu.with_memory_space_constraint, memory_space=pltpu.VMEM)
    return pl.pallas_call(
        functools.partial(finish, n, img_dev),
        out_shape=(
            jax.ShapeDtypeStruct((n, 2, qd), f32),
            jax.ShapeDtypeStruct((img_dev,), f32),
        ),
        in_specs=[vmem] * 3,
        out_specs=(vmem, vmem),
    )(held(own), held(arr), pair_images.T)


def solution(mesh):
    n, m = mesh.shape["img"], mesh.shape["rep"]
    in_specs = (
        P("img", "rep", None),
        P("img", "rep"),
        P("img", None),
        P("img", None),
        P("img", "rep", None),
        P("img", "rep"),
    )
    out_specs = (P("img", None, None), P("img"))
    return jax.shard_map(
        functools.partial(on_device, n, m),
        mesh=mesh, in_specs=in_specs, out_specs=out_specs, check_vma=False,
    )
```

```python
import functools

import jax
import jax.numpy as jnp
from jax import lax
from jax.experimental import pallas as pl
from jax.experimental.pallas import tpu as pltpu
from jax.sharding import PartitionSpec as P

DESC = 128
MESH = pl.DeviceIdType.MESH
distant = 1.0e9
far_entry = 32768.0
f32, bf16, i32 = jnp.float32, jnp.bfloat16, jnp.int32


def flips(me, size):
    steps, bit = [], 1
    while bit < size:
        steps.append(bit - (me // bit) % 2 * (2 * bit))
        bit *= 2
    return steps


def repeat(first, last, body):
    if last - first <= 8:
        for t in range(first, last):
            body(t)
    else:
        lax.fori_loop(first, last, lambda t, c: (body(t), c)[1], 0)


def dot(a, b):
    return jnp.dot(a, b, preferred_element_type=f32)


def dot_t(a, b):
    return lax.dot_general(a, b, (((1,), (1,)), ((), ())), preferred_element_type=f32)


def split(square):
    high = square.astype(bf16)
    return high, (square - high.astype(f32)).astype(bf16)


def column(row, length):
    rows = lax.broadcasted_iota(i32, (length, length), 0)
    cols = lax.broadcasted_iota(i32, (length, length), 1)
    return jnp.sum(jnp.where(rows == cols, row, 0.0), axis=1, keepdims=True)


def merge(a, b):
    low = jnp.minimum(a[0], b[0])
    high = jnp.minimum(jnp.maximum(a[0], b[0]), jnp.minimum(a[1], b[1]))
    return low, high


def lowest_two(d):
    half = d.shape[0] // 2
    a, b = d[:half], d[half:]
    two = (jnp.minimum(a, b), jnp.maximum(a, b))
    while half > 1:
        half //= 2
        two = merge((two[0][:half], two[1][:half]), (two[0][half:], two[1][half:]))
    return two


def stacked(cells):
    kp = cells.shape[1] // DESC
    return jnp.concatenate([cells[:, s * DESC : (s + 1) * DESC] for s in range(kp)], axis=0)


def kernel(
    n, sides,
    desc_hbm, counts_hbm, pairs_hbm, qcells_hbm, ccells_hbm, ccounts_hbm,
    own, arr, firsts,
    both, counts, pairs, qcells, ccells, ccounts, in_sem,
    info, lists_in, asked_at, q_out, q_in, c_out, c_in, lhs, rhs, part_out,
    info_send, info_recv, both_send, both_recv, list_send, list_recv,
    q_send, q_recv, c_send, c_recv, own_send, own_recv, arr_send, arr_recv, met,
):
    me, r = lax.axis_index("img"), lax.axis_index("rep")
    side, core = r // 2, r % 2
    mate = side * 2 + (1 - core)
    across = (1 - side) * 2 + core
    img_dev, share, width = both.shape[1:]
    rows = img_dev * share
    kp = width // DESC
    slots = ccells.shape[2]
    qn = qcells.shape[1]
    half, mine = n // 2, n // 4

    def remote(src, dst, send, recv, img, rep):
        return pltpu.make_async_remote_copy(
            src_ref=src, dst_ref=dst, send_sem=send, recv_sem=recv,
            device_id=(img, rep), device_id_type=MESH,
        )

    def drain(ref, sem):
        pltpu.make_async_copy(ref, ref, sem).wait()

    steps = flips(me, n)
    base = me + core * steps[-1]

    def other(i):
        if isinstance(i, int):
            return base + sum(step for k, step in enumerate(steps[:-1]) if i >> k & 1)
        return base + sum(i // 2**k % 2 * step for k, step in enumerate(steps[:-1]))

    barrier = pltpu.get_barrier_semaphore()

    def greet(img, rep):
        pl.semaphore_signal(barrier, inc=1, device_id=(img, rep), device_id_type=MESH)

    @pl.when(core == 0)
    def _():
        def greet_near(i):
            greet(other(i), mate)
            greet(other(i), (1 - side) * 2 + 1)

        repeat(0, half - 1, lambda i: greet_near(half - 1 - i))
        greet(other(0), (1 - side) * 2 + 1)

    @pl.when(core == 1)
    def _():
        greet(me, mate)
        repeat(0, half, lambda i: greet(other(half - 1 - i), r))
        repeat(0, mine, lambda p: greet(other(2 * (mine - 1 - p) + side), across))

    small = [
        pltpu.make_async_copy(src, dst, in_sem.at[i])
        for i, (src, dst) in enumerate((
            (counts_hbm, counts), (pairs_hbm, pairs),
            (ccells_hbm, ccells), (ccounts_hbm, ccounts), (qcells_hbm, qcells),
        ))
    ]
    shard = pltpu.make_async_copy(desc_hbm, both.at[core], in_sem.at[len(small)])
    for load in small:
        load.start()
    shard.start()
    for load in small:
        load.wait()

    local = (pairs[...] % img_dev).astype(f32)
    first = column(local[0:1], n).astype(i32)
    second = column(local[1:2], n).astype(i32)
    live_cells = column(ccounts[...].astype(f32), n).astype(i32)
    wanted = core * rows + second * share + ccells[:, 0, :] % share
    wanted = jnp.where(lax.broadcasted_iota(i32, (n, slots), 1) < live_cells, wanted, -1)
    info[core, 0:n, 0:slots] = wanted
    firsts[...] = jnp.broadcast_to(first, firsts.shape).astype(f32)
    info[core, n : n + img_dev, 0:share] = counts[...]

    @pl.when(core == 0)
    def _():
        pl.semaphore_wait(barrier, 1)
        pl.semaphore_signal(met, inc=1, device_id=(me, mate), device_id_type=MESH)

    @pl.when(core == 1)
    def _():
        pl.semaphore_wait(met, 1)

    remote(info.at[core], info.at[core], info_send, info_recv, me, mate).start()
    shard.wait()
    remote(both.at[core], both.at[core], both_send, both_recv, me, mate).start()

    cells = qcells[...]
    quarter = cells // share
    where = (quarter % 2) * rows + first * share + cells % share
    asked_at[...] = jnp.where(quarter // 2 == side, where, -1)
    group = min(half, 4)
    found_at = []
    for g in range(0, half, group):
        picks = [
            column(asked_at[pl.ds(other(i), 1), :].astype(f32), qn) for i in range(g, g + group)
        ]
        found_at.append(jnp.concatenate(picks, axis=0).astype(i32))

    pltpu.make_async_copy(info.at[1 - core], info.at[1 - core], info_recv).wait()

    def list_to(i):
        return info.at[:, pl.ds(other(i), 1)], lists_in.at[:, pl.ds(i, 1)]

    def send_list(i):
        remote(*list_to(i), list_send, list_recv.at[i], other(i), r).start()

    @pl.when(core == 0)
    def _():
        pl.semaphore_wait(met, 1)
        repeat(0, half - 1, lambda i: send_list(half - 1 - i))
        pltpu.make_async_copy(*list_to(0), list_recv.at[0]).start()

    @pl.when(core == 1)
    def _():
        pl.semaphore_wait(barrier, n - 1 + half + mine)
        pl.semaphore_signal(met, inc=1, device_id=(me, mate), device_id_type=MESH)
        repeat(0, half, lambda i: send_list(half - 1 - i))

    count_row = jnp.concatenate(
        [info[q, n + i : n + i + 1, 0:share] for q in range(2) for i in range(img_dev)], axis=1
    ).astype(f32)
    pltpu.make_async_copy(both.at[1 - core], both.at[1 - core], both_recv).wait()

    def pick(asked, none, dead):
        at = lax.broadcasted_iota(i32, (asked.shape[0], 2 * rows), 1)
        chosen = jnp.where(asked == at, 1.0, 0.0)
        live = jnp.sum(chosen * count_row, axis=1, keepdims=True)
        live = jnp.where(asked < 0, none, live)
        found = dot(chosen.astype(bf16), both[...].reshape(2 * rows, width))
        slot_of = (lax.broadcasted_iota(i32, found.shape, 1) // DESC).astype(f32)
        return jnp.where(slot_of < live, found, dead).astype(bf16)

    for g in range(0, half, group):
        block = pick(found_at[g // group], float(kp), -far_entry)
        for i in range(g, g + group):
            q_out[i] = block[(i - g) * qn : (i - g + 1) * qn]

    def q_to(i):
        return q_out.at[i], q_in.at[side * half + i]

    def candidates(indices):
        picks = []
        for i in indices:
            ref = lists_in.at[:, pl.ds(i, 1)]
            pltpu.make_async_copy(ref, ref, list_recv.at[i]).wait()
            for q in range(2):
                asked = lists_in[q, pl.ds(i, 1), 0:slots]
                picks.append(column(asked.astype(f32), slots))
        return pick(jnp.concatenate(picks, axis=0).astype(i32), 0.0, far_entry)

    def prepared(block):
        wide = stacked(block).astype(f32)
        high, low = split(wide * wide)
        ones = jnp.ones(wide.shape, bf16)
        return jnp.concatenate([high, low, (-2.0 * wide).astype(bf16), ones, ones], axis=1)

    cn = 2 * slots

    def prepare(indices, place):
        for g in range(0, len(indices), group):
            block = candidates(indices[g : g + group])
            for p in range(g, min(g + group, len(indices))):
                lhs[place(p)] = prepared(block[(p - g) * cn : (p - g + 1) * cn])

    qd = qn * kp

    def queries(i):
        for s in range(sides):
            ref = q_in.at[s * half + i]
            pltpu.make_async_copy(ref, ref, q_recv.at[s, i]).wait()
        to = lax.broadcasted_iota(i32, (qd, sides * qd), 0)
        at = lax.broadcasted_iota(i32, (qd, sides * qd), 1) % qd
        order = jnp.where(at == (to % kp) * qn + to // kp, 1.0, 0.0).astype(bf16)
        stack = jnp.concatenate([stacked(q_in[s * half + i]) for s in range(sides)], axis=0)
        query = dot(order, stack)
        high, low = split(query * query)
        ones = jnp.ones((qd, DESC), bf16)
        return jnp.concatenate([ones, ones, query.astype(bf16), high, low], axis=1)

    def keep(p, i, two):
        image = lists_in[0, pl.ds(i, 1), 0:1] // share
        image = jnp.broadcast_to(image.astype(f32), (1, qd))
        part_out[p] = jnp.minimum(jnp.concatenate([*two, image, image], axis=0), distant)

    everyone = [s * 2 + c for s in range(sides) for c in range(2)]
    others = (across, mate, (1 - side) * 2 + (1 - core))

    def to_owner(p, j, place):
        for to_rep in everyone:
            remote(part_out.at[p], place, own_send, own_recv, j, to_rep).start()

    def to_group(ref, place):
        for to_rep in others:
            remote(ref, place, arr_send, arr_recv, me, to_rep).start()
        pltpu.make_async_copy(ref, place, arr_recv).start()

    @pl.when(core == 0)
    def _():
        def send_near(i):
            remote(*q_to(i), q_send, q_recv.at[1, i], other(i), across).start()
            remote(*q_to(i), q_send, q_recv.at[0, i], other(i), r).start()

        repeat(0, half - 1, lambda i: send_near(half - 1 - i))
        remote(*q_to(0), q_send, q_recv.at[1, 0], me, across).start()
        pltpu.make_async_copy(*q_to(0), q_recv.at[0, 0]).start()

        prepare(list(range(half)), lambda p: p)
        place = own.at[side * n + me]

        def near_pair(i):
            keep(i, i, lowest_two(dot_t(lhs[i], queries(i))))

        near_pair(0)
        for to_rep in others:
            remote(part_out.at[0], place, own_send, own_recv, me, to_rep).start()
        pltpu.make_async_copy(part_out.at[0], place, own_recv).start()

        def near_step(i):
            near_pair(i)
            to_owner(i, other(i), place)

        repeat(1, half, near_step)
        to_group(part_out, arr.at[pl.ds(side * half, half)])

    @pl.when(core == 1)
    def _():
        def send_far(i):
            to_side = i % 2
            remote(
                *q_to(i), q_send, q_recv.at[(side + to_side) % 2, i], other(i), to_side * 2 + 1
            ).start()

        repeat(0, half, lambda i: send_far(half - 1 - i))

        for g in range(0, mine, group):
            given = [2 * p + 1 - side for p in range(g, min(g + group, mine))]
            block = candidates(given)
            for p in range(g, min(g + group, mine)):
                c_out[p] = block[(p - g) * cn : (p - g + 1) * cn]
                remote(c_out.at[p], c_in.at[p], c_send, c_recv.at[p], me, across).start()

        prepare([2 * p + side for p in range(mine)], lambda p: p)

        def far_first(p):
            i = 2 * p + side
            rhs[p] = queries(i)
            keep(p, i, lowest_two(dot_t(lhs[p], rhs[p])))

        repeat(0, mine, far_first)

        def far_last(p):
            pltpu.make_async_copy(c_in.at[p], c_in.at[p], c_recv.at[p]).wait()
            two = lowest_two(dot_t(prepared(c_in[p]), rhs[p]))
            before = part_out[p]
            i = 2 * p + side
            keep(p, i, merge((before[0:1], before[1:2]), two))
            to_owner(p, other(i), own.at[me])

        repeat(0, mine, far_last)
        to_group(part_out.at[pl.ds(0, mine)], arr.at[pl.ds(n + side * mine, mine)])

    drain(info.at[0], info_send)
    drain(both.at[0], both_send)

    @pl.when(core == 0)
    def _():
        drain(lists_in.at[:, pl.ds(0, half - 1)], list_send)
        drain(q_in.at[pl.ds(0, n - 1)], q_send)
        drain(own.at[pl.ds(0, 2 * n - 1)], own_send)
        drain(arr, arr_send)

    @pl.when(core == 1)
    def _():
        drain(lists_in.at[:, pl.ds(0, half)], list_send)
        drain(q_in.at[pl.ds(0, half)], q_send)
        drain(c_in, c_send)
        drain(own.at[pl.ds(0, n)], own_send)
        drain(arr.at[pl.ds(0, 3 * mine)], arr_send)

    drain(own.at[pl.ds(0, n + half)], own_recv)
    drain(arr, arr_recv)


def finish(n, img_dev, own, arr, firsts, matches, scores):
    half = n // 2

    def pair(ref, first, last):
        return ref[first:last, 0, :], ref[first:last, 1, :]

    def scored(two):
        live = two[0] < 0.5 * distant
        best, runner = jnp.where(live, two[0], 0.0), jnp.where(live, two[1], 0.0)
        margin = jnp.where(live, (runner - best) / (runner + 1.0), 0.0)
        total = jnp.sum(margin, axis=1, keepdims=True)
        return best, runner, total / jnp.sum(live.astype(f32), axis=1, keepdims=True)

    whole = pair(own, 0, n)
    halves = merge(whole, pair(own, n, 2 * n))
    mine = lax.axis_index("img") // half
    is_near = lax.broadcasted_iota(i32, whole[0].shape, 0) // half == mine
    best, runner, score = scored([jnp.where(is_near, a, b) for a, b in zip(halves, whole)])
    matches[:, 0, :] = best
    matches[:, 1, :] = runner
    first = firsts[:, 0:1]

    def per_image(image, score):
        at = lax.broadcasted_iota(i32, (image.shape[0], img_dev), 1).astype(f32)
        return jnp.sum(jnp.where(image == at, score, 0.0), axis=0)

    close = merge(pair(arr, 0, half), pair(arr, half, n))
    apart = pair(arr, n, n + half)
    total = per_image(first, score)
    total = total + per_image(arr[0:half, 2, 0:1], scored(close)[2])
    scores[...] = total + per_image(arr[n : n + half, 2, 0:1], scored(apart)[2])


def on_device(n, m, descriptors, cell_counts, pair_images, query_cells, cand_cells, cand_counts):
    img_dev, share, width = descriptors.shape
    slots, qn = cand_cells.shape[2], query_cells.shape[1]
    qd = qn * width // DESC
    sides, half, mine = m // 2, n // 2, n // 4
    vmem = pl.BlockSpec(memory_space=pltpu.VMEM)
    dma = pltpu.SemaphoreType.DMA
    operands = (
        descriptors, cell_counts, pair_images.T, query_cells, cand_cells, cand_counts.T,
    )
    hbm = pl.BlockSpec(memory_space=pltpu.HBM)
    info_rows = (n + img_dev + 7) // 8 * 8
    own, arr, firsts = pl.pallas_call(
        functools.partial(kernel, n, sides),
        out_shape=(
            pltpu.VMEM((sides * n, 4, qd), f32),
            pltpu.VMEM((n + half, 4, qd), f32),
            pltpu.VMEM((n, DESC), f32),
        ),
        in_specs=[hbm] * 6,
        out_specs=(vmem,) * 3,
        scratch_shapes=[
            pltpu.VMEM((2, *descriptors.shape), bf16),
            *(pltpu.VMEM(x.shape, x.dtype) for x in operands[1:]),
            dma((len(operands),)),
            pltpu.VMEM((2, info_rows, DESC), i32),
            pltpu.VMEM((2, (half + 7) // 8 * 8, DESC), i32),
            pltpu.VMEM(query_cells.shape, i32),
            pltpu.VMEM((half, qn, width), bf16),
            pltpu.VMEM((sides * half, qn, width), bf16),
            pltpu.VMEM((mine, 2 * slots, width), bf16),
            pltpu.VMEM((mine, 2 * slots, width), bf16),
            pltpu.VMEM((half, 2 * slots * width // DESC, 5 * DESC), bf16),
            pltpu.VMEM((mine, qd, 5 * DESC), bf16),
            pltpu.VMEM((half, 4, qd), f32),
            dma, dma, dma, dma, dma, dma((half,)),
            dma, dma((sides, half)), dma, dma((mine,)), dma, dma, dma, dma,
            pltpu.SemaphoreType.REGULAR,
        ],
        compiler_params=pltpu.CompilerParams(
            collective_id=0, has_side_effects=True
        ),
    )(*operands)
    held = functools.partial(pltpu.with_memory_space_constraint, memory_space=pltpu.VMEM)
    return pl.pallas_call(
        functools.partial(finish, n, img_dev),
        out_shape=(
            jax.ShapeDtypeStruct((n, 2, qd), f32),
            jax.ShapeDtypeStruct((img_dev,), f32),
        ),
        in_specs=[vmem] * 3,
        out_specs=(vmem, vmem),
    )(held(own), held(arr), held(firsts))


def solution(mesh):
    n, m = mesh.shape["img"], mesh.shape["rep"]
    in_specs = (
        P("img", "rep", None),
        P("img", "rep"),
        P("img", None),
        P("img", None),
        P("img", "rep", None),
        P("img", "rep"),
    )
    out_specs = (P("img", None, None), P("img"))
    return jax.shard_map(
        functools.partial(on_device, n, m),
        mesh=mesh, in_specs=in_specs, out_specs=out_specs, check_vma=False,
    )
```

```python
import functools

import jax
import jax.numpy as jnp
from jax import lax
from jax.experimental import pallas as pl
from jax.experimental.pallas import tpu as pltpu
from jax.sharding import PartitionSpec as P

DESC = 128
MESH = pl.DeviceIdType.MESH
distant = 1.0e9
far_entry = 32768.0
f32, bf16, i32 = jnp.float32, jnp.bfloat16, jnp.int32


def flips(me, size):
    steps, bit = [], 1
    while bit < size:
        steps.append(bit - (me // bit) % 2 * (2 * bit))
        bit *= 2
    return steps


def repeat(first, last, body):
    if last - first <= 8:
        for t in range(first, last):
            body(t)
    else:
        lax.fori_loop(first, last, lambda t, c: (body(t), c)[1], 0)


def dot(a, b):
    return jnp.dot(a, b, preferred_element_type=f32)


def dot_t(a, b):
    return lax.dot_general(a, b, (((1,), (1,)), ((), ())), preferred_element_type=f32)


def split(square):
    high = square.astype(bf16)
    return high, (square - high.astype(f32)).astype(bf16)


def column(row, length):
    rows = lax.broadcasted_iota(i32, (length, length), 0)
    cols = lax.broadcasted_iota(i32, (length, length), 1)
    return jnp.sum(jnp.where(rows == cols, row, 0.0), axis=1, keepdims=True)


def merge(a, b):
    low = jnp.minimum(a[0], b[0])
    high = jnp.minimum(jnp.maximum(a[0], b[0]), jnp.minimum(a[1], b[1]))
    return low, high


def lowest_two(d):
    half = d.shape[0] // 2
    a, b = d[:half], d[half:]
    two = (jnp.minimum(a, b), jnp.maximum(a, b))
    while half > 1:
        half //= 2
        two = merge((two[0][:half], two[1][:half]), (two[0][half:], two[1][half:]))
    return two


def stacked(cells):
    kp = cells.shape[1] // DESC
    return jnp.concatenate([cells[:, s * DESC : (s + 1) * DESC] for s in range(kp)], axis=0)


def kernel(
    n, sides,
    desc_hbm, counts_hbm, pairs_hbm, qcells_hbm, ccells_hbm, ccounts_hbm,
    own, arr, firsts,
    both, counts, pairs, qcells, ccells, ccounts, in_sem,
    info, lists_in, asked_at, q_out, q_in, c_out, c_in, lhs, rhs, part_out,
    info_send, info_recv, both_send, both_recv, list_send, list_recv,
    q_send, q_recv, c_send, c_recv, own_send, own_recv, arr_send, arr_recv, met,
):
    me, r = lax.axis_index("img"), lax.axis_index("rep")
    side, core = r // 2, r % 2
    mate = side * 2 + (1 - core)
    across = (1 - side) * 2 + core
    img_dev, share, width = both.shape[1:]
    rows = img_dev * share
    kp = width // DESC
    slots = ccells.shape[2]
    qn = qcells.shape[1]
    half, mine = n // 2, n // 4

    def remote(src, dst, send, recv, img, rep):
        return pltpu.make_async_remote_copy(
            src_ref=src, dst_ref=dst, send_sem=send, recv_sem=recv,
            device_id=(img, rep), device_id_type=MESH,
        )

    def drain(ref, sem):
        pltpu.make_async_copy(ref, ref, sem).wait()

    steps = flips(me, n)
    base = me + core * steps[-1]

    def other(i):
        if isinstance(i, int):
            return base + sum(step for k, step in enumerate(steps[:-1]) if i >> k & 1)
        return base + sum(i // 2**k % 2 * step for k, step in enumerate(steps[:-1]))

    barrier = pltpu.get_barrier_semaphore()

    def greet(img, rep):
        pl.semaphore_signal(barrier, inc=1, device_id=(img, rep), device_id_type=MESH)

    @pl.when(core == 0)
    def _():
        def greet_near(i):
            greet(other(i), mate)
            greet(other(i), (1 - side) * 2 + 1)

        repeat(0, half - 1, lambda i: greet_near(half - 1 - i))
        greet(other(0), (1 - side) * 2 + 1)

    @pl.when(core == 1)
    def _():
        greet(me, mate)
        repeat(0, half, lambda i: greet(other(half - 1 - i), r))
        repeat(0, mine, lambda p: greet(other(2 * (mine - 1 - p) + side), across))

    small = [
        pltpu.make_async_copy(src, dst, in_sem.at[i])
        for i, (src, dst) in enumerate((
            (counts_hbm, counts), (pairs_hbm, pairs),
            (ccells_hbm, ccells), (ccounts_hbm, ccounts), (qcells_hbm, qcells),
        ))
    ]
    shard = pltpu.make_async_copy(desc_hbm, both.at[core], in_sem.at[len(small)])
    for load in small:
        load.start()
    shard.start()
    for load in small:
        load.wait()

    local = (pairs[...] % img_dev).astype(f32)
    first = column(local[0:1], n).astype(i32)
    second = column(local[1:2], n).astype(i32)
    live_cells = column(ccounts[...].astype(f32), n).astype(i32)
    wanted = core * rows + second * share + ccells[:, 0, :] % share
    wanted = jnp.where(lax.broadcasted_iota(i32, (n, slots), 1) < live_cells, wanted, -1)
    info[core, 0:n, 0:slots] = wanted
    firsts[...] = jnp.broadcast_to(first, firsts.shape).astype(f32)
    info[core, n : n + img_dev, 0:share] = counts[...]

    @pl.when(core == 0)
    def _():
        pl.semaphore_wait(barrier, 1)
        pl.semaphore_signal(met, inc=1, device_id=(me, mate), device_id_type=MESH)

    @pl.when(core == 1)
    def _():
        pl.semaphore_wait(met, 1)

    remote(info.at[core], info.at[core], info_send, info_recv, me, mate).start()
    shard.wait()
    remote(both.at[core], both.at[core], both_send, both_recv, me, mate).start()

    cells = qcells[...]
    quarter = cells // share
    where = (quarter % 2) * rows + first * share + cells % share
    asked_at[...] = jnp.where(quarter // 2 == side, where, -1)
    group = min(half, 4)
    found_at = []
    for g in range(0, half, group):
        picks = [
            column(asked_at[pl.ds(other(i), 1), :].astype(f32), qn) for i in range(g, g + group)
        ]
        found_at.append(jnp.concatenate(picks, axis=0).astype(i32))

    pltpu.make_async_copy(info.at[1 - core], info.at[1 - core], info_recv).wait()

    def list_to(i):
        return info.at[:, pl.ds(other(i), 1)], lists_in.at[:, pl.ds(i, 1)]

    def send_list(i):
        remote(*list_to(i), list_send, list_recv.at[i], other(i), r).start()

    @pl.when(core == 0)
    def _():
        pl.semaphore_wait(met, 1)
        repeat(0, half - 1, lambda i: send_list(half - 1 - i))
        pltpu.make_async_copy(*list_to(0), list_recv.at[0]).start()

    @pl.when(core == 1)
    def _():
        pl.semaphore_wait(barrier, n - 1 + half + mine)
        pl.semaphore_signal(met, inc=1, device_id=(me, mate), device_id_type=MESH)
        repeat(0, half, lambda i: send_list(half - 1 - i))

    count_row = jnp.concatenate(
        [info[q, n + i : n + i + 1, 0:share] for q in range(2) for i in range(img_dev)], axis=1
    ).astype(f32)
    pltpu.make_async_copy(both.at[1 - core], both.at[1 - core], both_recv).wait()

    def pick(asked, none, dead):
        at = lax.broadcasted_iota(i32, (asked.shape[0], 2 * rows), 1)
        chosen = jnp.where(asked == at, 1.0, 0.0)
        live = jnp.sum(chosen * count_row, axis=1, keepdims=True)
        live = jnp.where(asked < 0, none, live)
        found = dot(chosen.astype(bf16), both[...].reshape(2 * rows, width))
        slot_of = (lax.broadcasted_iota(i32, found.shape, 1) // DESC).astype(f32)
        return jnp.where(slot_of < live, found, dead).astype(bf16)

    for g in range(0, half, group):
        block = pick(found_at[g // group], float(kp), -far_entry)
        for i in range(g, g + group):
            q_out[i] = block[(i - g) * qn : (i - g + 1) * qn]

    def q_to(i):
        return q_out.at[i], q_in.at[side * half + i]

    def candidates(indices):
        picks = []
        for i in indices:
            ref = lists_in.at[:, pl.ds(i, 1)]
            pltpu.make_async_copy(ref, ref, list_recv.at[i]).wait()
            for q in range(2):
                asked = lists_in[q, pl.ds(i, 1), 0:slots]
                picks.append(column(asked.astype(f32), slots))
        return pick(jnp.concatenate(picks, axis=0).astype(i32), 0.0, far_entry)

    def prepared(block):
        wide = stacked(block).astype(f32)
        high, low = split(wide * wide)
        ones = jnp.ones(wide.shape, bf16)
        return jnp.concatenate([high, low, (-2.0 * wide).astype(bf16), ones, ones], axis=1)

    cn = 2 * slots

    def prepare(indices, place):
        for g in range(0, len(indices), group):
            block = candidates(indices[g : g + group])
            for p in range(g, min(g + group, len(indices))):
                lhs[place(p)] = prepared(block[(p - g) * cn : (p - g + 1) * cn])

    qd = qn * kp

    def queries(i):
        for s in range(sides):
            ref = q_in.at[s * half + i]
            pltpu.make_async_copy(ref, ref, q_recv.at[s, i]).wait()
        to = lax.broadcasted_iota(i32, (qd, sides * qd), 0)
        at = lax.broadcasted_iota(i32, (qd, sides * qd), 1) % qd
        order = jnp.where(at == (to % kp) * qn + to // kp, 1.0, 0.0).astype(bf16)
        stack = jnp.concatenate([stacked(q_in[s * half + i]) for s in range(sides)], axis=0)
        query = dot(order, stack)
        high, low = split(query * query)
        ones = jnp.ones((qd, DESC), bf16)
        return jnp.concatenate([ones, ones, query.astype(bf16), high, low], axis=1)

    def keep(p, i, two):
        image = lists_in[0, pl.ds(i, 1), 0:1] // share
        image = jnp.broadcast_to(image.astype(f32), (1, qd))
        part_out[p] = jnp.minimum(jnp.concatenate([*two, image, image], axis=0), distant)

    everyone = [s * 2 + c for s in range(sides) for c in range(2)]
    others = (across, mate, (1 - side) * 2 + (1 - core))

    def to_owner(p, j, place):
        for to_rep in everyone:
            remote(part_out.at[p], place, own_send, own_recv, j, to_rep).start()

    def to_group(ref, place):
        for to_rep in others:
            remote(ref, place, arr_send, arr_recv, me, to_rep).start()
        pltpu.make_async_copy(ref, place, arr_recv).start()

    @pl.when(core == 0)
    def _():
        def send_near(i):
            remote(*q_to(i), q_send, q_recv.at[1, i], other(i), across).start()
            remote(*q_to(i), q_send, q_recv.at[0, i], other(i), r).start()

        repeat(0, half - 1, lambda i: send_near(half - 1 - i))
        remote(*q_to(0), q_send, q_recv.at[1, 0], me, across).start()
        pltpu.make_async_copy(*q_to(0), q_recv.at[0, 0]).start()

        prepare(list(range(half)), lambda p: p)
        place = own.at[side * n + me]

        def near_pair(i):
            keep(i, i, lowest_two(dot_t(lhs[i], queries(i))))

        near_pair(0)
        for to_rep in others:
            remote(part_out.at[0], place, own_send, own_recv, me, to_rep).start()
        pltpu.make_async_copy(part_out.at[0], place, own_recv).start()

        def near_step(i):
            near_pair(i)
            to_owner(i, other(i), place)

        repeat(1, half, near_step)
        to_group(part_out, arr.at[pl.ds(side * half, half)])

    @pl.when(core == 1)
    def _():
        def send_far(i):
            to_side = i % 2
            remote(
                *q_to(i), q_send, q_recv.at[(side + to_side) % 2, i], other(i), to_side * 2 + 1
            ).start()

        repeat(0, half, lambda i: send_far(half - 1 - i))

        flip = (1 + me // half + me // mine) % 2 * (mine // 2)
        turns = [(q + flip) % mine for q in range(mine)]
        for p in turns:
            c_out[p] = candidates([2 * p + 1 - side])
            remote(c_out.at[p], c_in.at[p], c_send, c_recv.at[p], me, across).start()

        prepare([2 * p + side for p in turns], lambda q: turns[q])

        def far_first(p):
            i = 2 * p + side
            rhs[p] = queries(i)
            keep(p, i, lowest_two(dot_t(lhs[p], rhs[p])))

        for p in turns:
            far_first(p)

        def far_last(p):
            pltpu.make_async_copy(c_in.at[p], c_in.at[p], c_recv.at[p]).wait()
            two = lowest_two(dot_t(prepared(c_in[p]), rhs[p]))
            before = part_out[p]
            i = 2 * p + side
            keep(p, i, merge((before[0:1], before[1:2]), two))
            to_owner(p, other(i), own.at[me])

        for p in turns:
            far_last(p)
        to_group(part_out.at[pl.ds(0, mine)], arr.at[pl.ds(n + side * mine, mine)])

    drain(info.at[0], info_send)
    drain(both.at[0], both_send)

    @pl.when(core == 0)
    def _():
        drain(lists_in.at[:, pl.ds(0, half - 1)], list_send)
        drain(q_in.at[pl.ds(0, n - 1)], q_send)
        drain(own.at[pl.ds(0, 2 * n - 1)], own_send)
        drain(arr, arr_send)

    @pl.when(core == 1)
    def _():
        drain(lists_in.at[:, pl.ds(0, half)], list_send)
        drain(q_in.at[pl.ds(0, half)], q_send)
        drain(c_in, c_send)
        drain(own.at[pl.ds(0, n)], own_send)
        drain(arr.at[pl.ds(0, 3 * mine)], arr_send)

    drain(own.at[pl.ds(0, n + half)], own_recv)
    drain(arr, arr_recv)


def finish(n, img_dev, own, arr, firsts, matches, scores):
    half = n // 2

    def pair(ref, first, last):
        return ref[first:last, 0, :], ref[first:last, 1, :]

    def scored(two):
        live = two[0] < 0.5 * distant
        best, runner = jnp.where(live, two[0], 0.0), jnp.where(live, two[1], 0.0)
        margin = jnp.where(live, (runner - best) / (runner + 1.0), 0.0)
        total = jnp.sum(margin, axis=1, keepdims=True)
        return best, runner, total / jnp.sum(live.astype(f32), axis=1, keepdims=True)

    whole = pair(own, 0, n)
    halves = merge(whole, pair(own, n, 2 * n))
    mine = lax.axis_index("img") // half
    is_near = lax.broadcasted_iota(i32, whole[0].shape, 0) // half == mine
    best, runner, score = scored([jnp.where(is_near, a, b) for a, b in zip(halves, whole)])
    matches[:, 0, :] = best
    matches[:, 1, :] = runner
    first = firsts[:, 0:1]

    def per_image(image, score):
        at = lax.broadcasted_iota(i32, (image.shape[0], img_dev), 1).astype(f32)
        return jnp.sum(jnp.where(image == at, score, 0.0), axis=0)

    close = merge(pair(arr, 0, half), pair(arr, half, n))
    apart = pair(arr, n, n + half)
    total = per_image(first, score)
    total = total + per_image(arr[0:half, 2, 0:1], scored(close)[2])
    scores[...] = total + per_image(arr[n : n + half, 2, 0:1], scored(apart)[2])


def on_device(n, m, descriptors, cell_counts, pair_images, query_cells, cand_cells, cand_counts):
    img_dev, share, width = descriptors.shape
    slots, qn = cand_cells.shape[2], query_cells.shape[1]
    qd = qn * width // DESC
    sides, half, mine = m // 2, n // 2, n // 4
    vmem = pl.BlockSpec(memory_space=pltpu.VMEM)
    dma = pltpu.SemaphoreType.DMA
    operands = (
        descriptors, cell_counts, pair_images.T, query_cells, cand_cells, cand_counts.T,
    )
    hbm = pl.BlockSpec(memory_space=pltpu.HBM)
    info_rows = (n + img_dev + 7) // 8 * 8
    own, arr, firsts = pl.pallas_call(
        functools.partial(kernel, n, sides),
        out_shape=(
            pltpu.VMEM((sides * n, 4, qd), f32),
            pltpu.VMEM((n + half, 4, qd), f32),
            pltpu.VMEM((n, DESC), f32),
        ),
        in_specs=[hbm] * 6,
        out_specs=(vmem,) * 3,
        scratch_shapes=[
            pltpu.VMEM((2, *descriptors.shape), bf16),
            *(pltpu.VMEM(x.shape, x.dtype) for x in operands[1:]),
            dma((len(operands),)),
            pltpu.VMEM((2, info_rows, DESC), i32),
            pltpu.VMEM((2, (half + 7) // 8 * 8, DESC), i32),
            pltpu.VMEM(query_cells.shape, i32),
            pltpu.VMEM((half, qn, width), bf16),
            pltpu.VMEM((sides * half, qn, width), bf16),
            pltpu.VMEM((mine, 2 * slots, width), bf16),
            pltpu.VMEM((mine, 2 * slots, width), bf16),
            pltpu.VMEM((half, 2 * slots * width // DESC, 5 * DESC), bf16),
            pltpu.VMEM((mine, qd, 5 * DESC), bf16),
            pltpu.VMEM((half, 4, qd), f32),
            dma, dma, dma, dma, dma, dma((half,)),
            dma, dma((sides, half)), dma, dma((mine,)), dma, dma, dma, dma,
            pltpu.SemaphoreType.REGULAR,
        ],
        compiler_params=pltpu.CompilerParams(
            collective_id=0, has_side_effects=True
        ),
    )(*operands)
    held = functools.partial(pltpu.with_memory_space_constraint, memory_space=pltpu.VMEM)
    return pl.pallas_call(
        functools.partial(finish, n, img_dev),
        out_shape=(
            jax.ShapeDtypeStruct((n, 2, qd), f32),
            jax.ShapeDtypeStruct((img_dev,), f32),
        ),
        in_specs=[vmem] * 3,
        out_specs=(vmem, vmem),
    )(held(own), held(arr), held(firsts))


def solution(mesh):
    n, m = mesh.shape["img"], mesh.shape["rep"]
    in_specs = (
        P("img", "rep", None),
        P("img", "rep"),
        P("img", None),
        P("img", None),
        P("img", "rep", None),
        P("img", "rep"),
    )
    out_specs = (P("img", None, None), P("img"))
    return jax.shard_map(
        functools.partial(on_device, n, m),
        mesh=mesh, in_specs=in_specs, out_specs=out_specs, check_vma=False,
    )
```

```python
import functools

import jax
import jax.numpy as jnp
from jax import lax
from jax.experimental import pallas as pl
from jax.experimental.pallas import tpu as pltpu
from jax.sharding import PartitionSpec as P

DESC = 128
MESH = pl.DeviceIdType.MESH
distant = 1.0e9
far_entry = 32768.0
f32, bf16, i32 = jnp.float32, jnp.bfloat16, jnp.int32


def flips(me, size):
    steps, bit = [], 1
    while bit < size:
        steps.append(bit - (me // bit) % 2 * (2 * bit))
        bit *= 2
    return steps


def repeat(first, last, body):
    if last - first <= 8:
        for t in range(first, last):
            body(t)
    else:
        lax.fori_loop(first, last, lambda t, c: (body(t), c)[1], 0)


def dot(a, b):
    return jnp.dot(a, b, preferred_element_type=f32)


def dot_t(a, b):
    return lax.dot_general(a, b, (((1,), (1,)), ((), ())), preferred_element_type=f32)


def split(square):
    high = square.astype(bf16)
    return high, (square - high.astype(f32)).astype(bf16)


def column(row, length):
    rows = lax.broadcasted_iota(i32, (length, length), 0)
    cols = lax.broadcasted_iota(i32, (length, length), 1)
    return jnp.sum(jnp.where(rows == cols, row, 0.0), axis=1, keepdims=True)


def merge(a, b):
    low = jnp.minimum(a[0], b[0])
    high = jnp.minimum(jnp.maximum(a[0], b[0]), jnp.minimum(a[1], b[1]))
    return low, high


def lowest_two(d):
    half = d.shape[0] // 2
    a, b = d[:half], d[half:]
    two = (jnp.minimum(a, b), jnp.maximum(a, b))
    while half > 1:
        half //= 2
        two = merge((two[0][:half], two[1][:half]), (two[0][half:], two[1][half:]))
    return two


def stacked(cells):
    kp = cells.shape[1] // DESC
    return jnp.concatenate([cells[:, s * DESC : (s + 1) * DESC] for s in range(kp)], axis=0)


def kernel(
    n, sides,
    desc_hbm, counts_hbm, pairs_hbm, qcells_hbm, ccells_hbm, ccounts_hbm,
    own, arr, firsts,
    both, counts, pairs, qcells, ccells, ccounts, in_sem,
    info, lists_in, asked_at, q_out, q_in, c_out, c_in, lhs, rhs, part_out,
    info_send, info_recv, both_send, both_recv, list_send, list_recv,
    q_send, q_recv, c_send, c_recv, own_send, own_recv, arr_send, arr_recv, met,
):
    me, r = lax.axis_index("img"), lax.axis_index("rep")
    side, core = r // 2, r % 2
    mate = side * 2 + (1 - core)
    across = (1 - side) * 2 + core
    img_dev, share, width = both.shape[1:]
    rows = img_dev * share
    kp = width // DESC
    slots = ccells.shape[2]
    qn = qcells.shape[1]
    half, mine = n // 2, n // 4
    lane = (side + me) % 2

    def remote(src, dst, send, recv, img, rep):
        return pltpu.make_async_remote_copy(
            src_ref=src, dst_ref=dst, send_sem=send, recv_sem=recv,
            device_id=(img, rep), device_id_type=MESH,
        )

    def drain(ref, sem):
        pltpu.make_async_copy(ref, ref, sem).wait()

    steps = flips(me, n)
    base = me + core * steps[-1]

    def other(i):
        if isinstance(i, int):
            return base + sum(step for k, step in enumerate(steps[:-1]) if i >> k & 1)
        return base + sum(i // 2**k % 2 * step for k, step in enumerate(steps[:-1]))

    barrier = pltpu.get_barrier_semaphore()

    def greet(img, rep):
        pl.semaphore_signal(barrier, inc=1, device_id=(img, rep), device_id_type=MESH)

    @pl.when(core == 0)
    def _():
        def greet_near(i):
            greet(other(i), mate)
            greet(other(i), (1 - side) * 2 + 1)

        repeat(0, half - 1, lambda i: greet_near(half - 1 - i))
        greet(other(0), (1 - side) * 2 + 1)

    @pl.when(core == 1)
    def _():
        greet(me, mate)
        repeat(0, half, lambda i: greet(other(half - 1 - i), r))
        repeat(0, mine, lambda p: greet(other(2 * (mine - 1 - p) + lane), across))

    small = [
        pltpu.make_async_copy(src, dst, in_sem.at[i])
        for i, (src, dst) in enumerate((
            (counts_hbm, counts), (pairs_hbm, pairs),
            (ccells_hbm, ccells), (ccounts_hbm, ccounts), (qcells_hbm, qcells),
        ))
    ]
    shard = pltpu.make_async_copy(desc_hbm, both.at[core], in_sem.at[len(small)])
    for load in small:
        load.start()
    shard.start()
    for load in small:
        load.wait()

    local = (pairs[...] % img_dev).astype(f32)
    first = column(local[0:1], n).astype(i32)
    second = column(local[1:2], n).astype(i32)
    live_cells = column(ccounts[...].astype(f32), n).astype(i32)
    wanted = core * rows + second * share + ccells[:, 0, :] % share
    wanted = jnp.where(lax.broadcasted_iota(i32, (n, slots), 1) < live_cells, wanted, -1)
    info[core, 0:n, 0:slots] = wanted
    firsts[...] = jnp.broadcast_to(first, firsts.shape).astype(f32)
    info[core, n : n + img_dev, 0:share] = counts[...]

    @pl.when(core == 0)
    def _():
        pl.semaphore_wait(barrier, 1)
        pl.semaphore_signal(met, inc=1, device_id=(me, mate), device_id_type=MESH)

    @pl.when(core == 1)
    def _():
        pl.semaphore_wait(met, 1)

    remote(info.at[core], info.at[core], info_send, info_recv, me, mate).start()
    shard.wait()
    remote(both.at[core], both.at[core], both_send, both_recv, me, mate).start()

    cells = qcells[...]
    quarter = cells // share
    where = (quarter % 2) * rows + first * share + cells % share
    asked_at[...] = jnp.where(quarter // 2 == side, where, -1)
    group = min(half, 4)
    found_at = []
    for g in range(0, half, group):
        picks = [
            column(asked_at[pl.ds(other(i), 1), :].astype(f32), qn) for i in range(g, g + group)
        ]
        found_at.append(jnp.concatenate(picks, axis=0).astype(i32))

    pltpu.make_async_copy(info.at[1 - core], info.at[1 - core], info_recv).wait()

    def list_to(i):
        return info.at[:, pl.ds(other(i), 1)], lists_in.at[:, pl.ds(i, 1)]

    def send_list(i):
        remote(*list_to(i), list_send, list_recv.at[i], other(i), r).start()

    @pl.when(core == 0)
    def _():
        pl.semaphore_wait(met, 1)
        repeat(0, half - 1, lambda i: send_list(half - 1 - i))
        pltpu.make_async_copy(*list_to(0), list_recv.at[0]).start()

    @pl.when(core == 1)
    def _():
        pl.semaphore_wait(barrier, n - 1 + half + lane * half)
        pl.semaphore_signal(met, inc=1, device_id=(me, mate), device_id_type=MESH)
        repeat(0, half, lambda i: send_list(half - 1 - i))

    count_row = jnp.concatenate(
        [info[q, n + i : n + i + 1, 0:share] for q in range(2) for i in range(img_dev)], axis=1
    ).astype(f32)
    pltpu.make_async_copy(both.at[1 - core], both.at[1 - core], both_recv).wait()

    def pick(asked, none, dead):
        at = lax.broadcasted_iota(i32, (asked.shape[0], 2 * rows), 1)
        chosen = jnp.where(asked == at, 1.0, 0.0)
        live = jnp.sum(chosen * count_row, axis=1, keepdims=True)
        live = jnp.where(asked < 0, none, live)
        found = dot(chosen.astype(bf16), both[...].reshape(2 * rows, width))
        slot_of = (lax.broadcasted_iota(i32, found.shape, 1) // DESC).astype(f32)
        return jnp.where(slot_of < live, found, dead).astype(bf16)

    for g in range(0, half, group):
        block = pick(found_at[g // group], float(kp), -far_entry)
        for i in range(g, g + group):
            q_out[i] = block[(i - g) * qn : (i - g + 1) * qn]

    def q_to(i):
        return q_out.at[i], q_in.at[side * half + i]

    def candidates(indices):
        picks = []
        for i in indices:
            ref = lists_in.at[:, pl.ds(i, 1)]
            pltpu.make_async_copy(ref, ref, list_recv.at[i]).wait()
            for q in range(2):
                asked = lists_in[q, pl.ds(i, 1), 0:slots]
                picks.append(column(asked.astype(f32), slots))
        return pick(jnp.concatenate(picks, axis=0).astype(i32), 0.0, far_entry)

    def prepared(block):
        wide = stacked(block).astype(f32)
        high, low = split(wide * wide)
        ones = jnp.ones(wide.shape, bf16)
        return jnp.concatenate([high, low, (-2.0 * wide).astype(bf16), ones, ones], axis=1)

    cn = 2 * slots

    def prepare(indices, place):
        for g in range(0, len(indices), group):
            block = candidates(indices[g : g + group])
            for p in range(g, min(g + group, len(indices))):
                lhs[place(p)] = prepared(block[(p - g) * cn : (p - g + 1) * cn])

    qd = qn * kp

    def queries(i):
        for s in range(sides):
            ref = q_in.at[s * half + i]
            pltpu.make_async_copy(ref, ref, q_recv.at[s, i]).wait()
        to = lax.broadcasted_iota(i32, (qd, sides * qd), 0)
        at = lax.broadcasted_iota(i32, (qd, sides * qd), 1) % qd
        order = jnp.where(at == (to % kp) * qn + to // kp, 1.0, 0.0).astype(bf16)
        stack = jnp.concatenate([stacked(q_in[s * half + i]) for s in range(sides)], axis=0)
        query = dot(order, stack)
        high, low = split(query * query)
        ones = jnp.ones((qd, DESC), bf16)
        return jnp.concatenate([ones, ones, query.astype(bf16), high, low], axis=1)

    def keep(p, i, two):
        image = lists_in[0, pl.ds(i, 1), 0:1] // share
        image = jnp.broadcast_to(image.astype(f32), (1, qd))
        part_out[p] = jnp.minimum(jnp.concatenate([*two, image, image], axis=0), distant)

    everyone = [s * 2 + c for s in range(sides) for c in range(2)]
    others = (across, mate, (1 - side) * 2 + (1 - core))

    def to_owner(p, j, place):
        for to_rep in everyone:
            remote(part_out.at[p], place, own_send, own_recv, j, to_rep).start()

    def to_group(ref, place):
        for to_rep in others:
            remote(ref, place, arr_send, arr_recv, me, to_rep).start()
        pltpu.make_async_copy(ref, place, arr_recv).start()

    @pl.when(core == 0)
    def _():
        def send_near(i):
            remote(*q_to(i), q_send, q_recv.at[1, i], other(i), across).start()
            remote(*q_to(i), q_send, q_recv.at[0, i], other(i), r).start()

        repeat(0, half - 1, lambda i: send_near(half - 1 - i))
        remote(*q_to(0), q_send, q_recv.at[1, 0], me, across).start()
        pltpu.make_async_copy(*q_to(0), q_recv.at[0, 0]).start()

        prepare(list(range(half)), lambda p: p)
        place = own.at[side * n + me]

        def near_pair(i):
            keep(i, i, lowest_two(dot_t(lhs[i], queries(i))))

        near_pair(0)
        for to_rep in others:
            remote(part_out.at[0], place, own_send, own_recv, me, to_rep).start()
        pltpu.make_async_copy(part_out.at[0], place, own_recv).start()

        def near_step(i):
            near_pair(i)
            to_owner(i, other(i), place)

        repeat(1, half, near_step)
        to_group(part_out, arr.at[pl.ds(side * half, half)])

    @pl.when(core == 1)
    def _():
        def send_far(i):
            remote(*q_to(i), q_send, q_recv.at[lane, i], other(i), me % 2 * 2 + 1).start()

        repeat(0, half, lambda i: send_far(half - 1 - i))

        flip = (1 + me // half + me // mine) % 2 * (mine // 2)
        turns = [(q + flip) % mine for q in range(mine)]
        for p in turns:
            c_out[p] = candidates([2 * p + 1 - lane])
            remote(c_out.at[p], c_in.at[p], c_send, c_recv.at[p], me, across).start()

        prepare([2 * p + lane for p in turns], lambda q: turns[q])

        def far_first(p):
            i = 2 * p + lane
            rhs[p] = queries(i)
            keep(p, i, lowest_two(dot_t(lhs[p], rhs[p])))


        def far_last(p):
            pltpu.make_async_copy(c_in.at[p], c_in.at[p], c_recv.at[p]).wait()
            two = lowest_two(dot_t(prepared(c_in[p]), rhs[p]))
            before = part_out[p]
            i = 2 * p + lane
            keep(p, i, merge((before[0:1], before[1:2]), two))
            to_owner(p, other(i), own.at[me])

        for p in turns:
            far_first(p)
            far_last(p)
        to_group(part_out.at[pl.ds(0, mine)], arr.at[pl.ds(n + side * mine, mine)])

    drain(info.at[0], info_send)
    drain(both.at[0], both_send)

    @pl.when(core == 0)
    def _():
        drain(lists_in.at[:, pl.ds(0, half - 1)], list_send)
        drain(q_in.at[pl.ds(0, n - 1)], q_send)
        drain(own.at[pl.ds(0, 2 * n - 1)], own_send)
        drain(arr, arr_send)

    @pl.when(core == 1)
    def _():
        drain(lists_in.at[:, pl.ds(0, half)], list_send)
        drain(q_in.at[pl.ds(0, half)], q_send)
        drain(c_in, c_send)
        drain(own.at[pl.ds(0, n)], own_send)
        drain(arr.at[pl.ds(0, 3 * mine)], arr_send)

    drain(own.at[pl.ds(0, n + half)], own_recv)
    drain(arr, arr_recv)


def finish(n, img_dev, own, arr, firsts, matches, scores):
    half = n // 2

    def pair(ref, first, last):
        return ref[first:last, 0, :], ref[first:last, 1, :]

    def scored(two):
        live = two[0] < 0.5 * distant
        best, runner = jnp.where(live, two[0], 0.0), jnp.where(live, two[1], 0.0)
        margin = jnp.where(live, (runner - best) / (runner + 1.0), 0.0)
        total = jnp.sum(margin, axis=1, keepdims=True)
        return best, runner, total / jnp.sum(live.astype(f32), axis=1, keepdims=True)

    whole = pair(own, 0, n)
    halves = merge(whole, pair(own, n, 2 * n))
    mine = lax.axis_index("img") // half
    is_near = lax.broadcasted_iota(i32, whole[0].shape, 0) // half == mine
    best, runner, score = scored([jnp.where(is_near, a, b) for a, b in zip(halves, whole)])
    matches[:, 0, :] = best
    matches[:, 1, :] = runner
    first = firsts[:, 0:1]

    def per_image(image, score):
        at = lax.broadcasted_iota(i32, (image.shape[0], img_dev), 1).astype(f32)
        return jnp.sum(jnp.where(image == at, score, 0.0), axis=0)

    close = merge(pair(arr, 0, half), pair(arr, half, n))
    apart = pair(arr, n, n + half)
    total = per_image(first, score)
    total = total + per_image(arr[0:half, 2, 0:1], scored(close)[2])
    scores[...] = total + per_image(arr[n : n + half, 2, 0:1], scored(apart)[2])


def on_device(n, m, descriptors, cell_counts, pair_images, query_cells, cand_cells, cand_counts):
    img_dev, share, width = descriptors.shape
    slots, qn = cand_cells.shape[2], query_cells.shape[1]
    qd = qn * width // DESC
    sides, half, mine = m // 2, n // 2, n // 4
    vmem = pl.BlockSpec(memory_space=pltpu.VMEM)
    dma = pltpu.SemaphoreType.DMA
    operands = (
        descriptors, cell_counts, pair_images.T, query_cells, cand_cells, cand_counts.T,
    )
    hbm = pl.BlockSpec(memory_space=pltpu.HBM)
    info_rows = (n + img_dev + 7) // 8 * 8
    own, arr, firsts = pl.pallas_call(
        functools.partial(kernel, n, sides),
        out_shape=(
            pltpu.VMEM((sides * n, 4, qd), f32),
            pltpu.VMEM((n + half, 4, qd), f32),
            pltpu.VMEM((n, DESC), f32),
        ),
        in_specs=[hbm] * 6,
        out_specs=(vmem,) * 3,
        scratch_shapes=[
            pltpu.VMEM((2, *descriptors.shape), bf16),
            *(pltpu.VMEM(x.shape, x.dtype) for x in operands[1:]),
            dma((len(operands),)),
            pltpu.VMEM((2, info_rows, DESC), i32),
            pltpu.VMEM((2, (half + 7) // 8 * 8, DESC), i32),
            pltpu.VMEM(query_cells.shape, i32),
            pltpu.VMEM((half, qn, width), bf16),
            pltpu.VMEM((sides * half, qn, width), bf16),
            pltpu.VMEM((mine, 2 * slots, width), bf16),
            pltpu.VMEM((mine, 2 * slots, width), bf16),
            pltpu.VMEM((half, 2 * slots * width // DESC, 5 * DESC), bf16),
            pltpu.VMEM((mine, qd, 5 * DESC), bf16),
            pltpu.VMEM((half, 4, qd), f32),
            dma, dma, dma, dma, dma, dma((half,)),
            dma, dma((sides, half)), dma, dma((mine,)), dma, dma, dma, dma,
            pltpu.SemaphoreType.REGULAR,
        ],
        compiler_params=pltpu.CompilerParams(
            collective_id=0, has_side_effects=True
        ),
    )(*operands)
    held = functools.partial(pltpu.with_memory_space_constraint, memory_space=pltpu.VMEM)
    return pl.pallas_call(
        functools.partial(finish, n, img_dev),
        out_shape=(
            jax.ShapeDtypeStruct((n, 2, qd), f32),
            jax.ShapeDtypeStruct((img_dev,), f32),
        ),
        in_specs=[vmem] * 3,
        out_specs=(vmem, vmem),
    )(held(own), held(arr), held(firsts))


def solution(mesh):
    n, m = mesh.shape["img"], mesh.shape["rep"]
    in_specs = (
        P("img", "rep", None),
        P("img", "rep"),
        P("img", None),
        P("img", None),
        P("img", "rep", None),
        P("img", "rep"),
    )
    out_specs = (P("img", None, None), P("img"))
    return jax.shard_map(
        functools.partial(on_device, n, m),
        mesh=mesh, in_specs=in_specs, out_specs=out_specs, check_vma=False,
    )
```

```python
import functools

import jax
import jax.numpy as jnp
from jax import lax
from jax.experimental import pallas as pl
from jax.experimental.pallas import tpu as pltpu
from jax.sharding import PartitionSpec as P

DESC = 128
MESH = pl.DeviceIdType.MESH
distant = 1.0e9
far_entry = 32768.0
f32, bf16, i32 = jnp.float32, jnp.bfloat16, jnp.int32


def flips(me, size):
    steps, bit = [], 1
    while bit < size:
        steps.append(bit - (me // bit) % 2 * (2 * bit))
        bit *= 2
    return steps


def repeat(first, last, body):
    if last - first <= 8:
        for t in range(first, last):
            body(t)
    else:
        lax.fori_loop(first, last, lambda t, c: (body(t), c)[1], 0)


def dot(a, b):
    return jnp.dot(a, b, preferred_element_type=f32)


def dot_t(a, b):
    return lax.dot_general(a, b, (((1,), (1,)), ((), ())), preferred_element_type=f32)


def split(square):
    high = square.astype(bf16)
    return high, (square - high.astype(f32)).astype(bf16)


def column(row, length):
    rows = lax.broadcasted_iota(i32, (length, length), 0)
    cols = lax.broadcasted_iota(i32, (length, length), 1)
    return jnp.sum(jnp.where(rows == cols, row, 0.0), axis=1, keepdims=True)


def merge(a, b):
    low = jnp.minimum(a[0], b[0])
    high = jnp.minimum(jnp.maximum(a[0], b[0]), jnp.minimum(a[1], b[1]))
    return low, high


def lowest_two(d):
    half = d.shape[0] // 2
    a, b = d[:half], d[half:]
    two = (jnp.minimum(a, b), jnp.maximum(a, b))
    while half > 1:
        half //= 2
        two = merge((two[0][:half], two[1][:half]), (two[0][half:], two[1][half:]))
    return two


def stacked(cells):
    kp = cells.shape[1] // DESC
    return jnp.concatenate([cells[:, s * DESC : (s + 1) * DESC] for s in range(kp)], axis=0)


def kernel(
    n, sides,
    desc_hbm, counts_hbm, pairs_hbm, qcells_hbm, ccells_hbm, ccounts_hbm,
    own, arr, firsts,
    both, counts, pairs, qcells, ccells, ccounts, in_sem,
    info, lists_in, asked_at, q_out, q_in, c_out, c_in, lhs, rhs, part_out,
    info_send, info_recv, both_send, both_recv, list_send, list_recv,
    q_send, q_recv, c_send, c_recv, own_send, own_recv, arr_send, arr_recv, met,
):
    me, r = lax.axis_index("img"), lax.axis_index("rep")
    side, core = r // 2, r % 2
    mate = side * 2 + (1 - core)
    across = (1 - side) * 2 + core
    img_dev, share, width = both.shape[1:]
    rows = img_dev * share
    kp = width // DESC
    slots = ccells.shape[2]
    qn = qcells.shape[1]
    half, mine = n // 2, n // 4
    lane = (side + me) % 2

    def remote(src, dst, send, recv, img, rep):
        return pltpu.make_async_remote_copy(
            src_ref=src, dst_ref=dst, send_sem=send, recv_sem=recv,
            device_id=(img, rep), device_id_type=MESH,
        )

    def drain(ref, sem):
        pltpu.make_async_copy(ref, ref, sem).wait()

    steps = flips(me, n)
    base = me + core * steps[-1]

    def other(i):
        if isinstance(i, int):
            return base + sum(step for k, step in enumerate(steps[:-1]) if i >> k & 1)
        return base + sum(i // 2**k % 2 * step for k, step in enumerate(steps[:-1]))

    barrier = pltpu.get_barrier_semaphore()

    def greet(img, rep):
        pl.semaphore_signal(barrier, inc=1, device_id=(img, rep), device_id_type=MESH)

    @pl.when(core == 0)
    def _():
        def greet_near(i):
            greet(other(i), mate)
            greet(other(i), (1 - side) * 2 + 1)

        repeat(0, half - 1, lambda i: greet_near(half - 1 - i))
        greet(other(0), (1 - side) * 2 + 1)

    @pl.when(core == 1)
    def _():
        greet(me, mate)
        repeat(0, half, lambda i: greet(other(half - 1 - i), r))
        repeat(0, mine, lambda p: greet(other(2 * (mine - 1 - p) + lane), across))

    small = [
        pltpu.make_async_copy(src, dst, in_sem.at[i])
        for i, (src, dst) in enumerate((
            (counts_hbm, counts), (pairs_hbm, pairs),
            (ccells_hbm, ccells), (ccounts_hbm, ccounts), (qcells_hbm, qcells),
        ))
    ]
    shard = pltpu.make_async_copy(desc_hbm, both.at[core], in_sem.at[len(small)])
    for load in small:
        load.start()
    shard.start()
    for load in small:
        load.wait()

    local = (pairs[...] % img_dev).astype(f32)
    first = column(local[0:1], n).astype(i32)
    second = column(local[1:2], n).astype(i32)
    live_cells = column(ccounts[...].astype(f32), n).astype(i32)
    wanted = core * rows + second * share + ccells[:, 0, :] % share
    wanted = jnp.where(lax.broadcasted_iota(i32, (n, slots), 1) < live_cells, wanted, -1)
    info[core, 0:n, 0:slots] = wanted
    firsts[...] = jnp.broadcast_to(first, firsts.shape).astype(f32)
    info[core, n : n + img_dev, 0:share] = counts[...]

    @pl.when(core == 0)
    def _():
        pl.semaphore_wait(barrier, 1)
        pl.semaphore_signal(met, inc=1, device_id=(me, mate), device_id_type=MESH)

    @pl.when(core == 1)
    def _():
        pl.semaphore_wait(met, 1)

    remote(info.at[core], info.at[core], info_send, info_recv, me, mate).start()
    shard.wait()
    remote(both.at[core], both.at[core], both_send, both_recv, me, mate).start()

    cells = qcells[...]
    quarter = cells // share
    where = (quarter % 2) * rows + first * share + cells % share
    asked_at[...] = jnp.where(quarter // 2 == side, where, -1)
    group = min(half, 4)
    found_at = []
    for g in range(0, half, group):
        picks = [
            column(asked_at[pl.ds(other(i), 1), :].astype(f32), qn) for i in range(g, g + group)
        ]
        found_at.append(jnp.concatenate(picks, axis=0).astype(i32))

    pltpu.make_async_copy(info.at[1 - core], info.at[1 - core], info_recv).wait()

    def list_to(i):
        return info.at[:, pl.ds(other(i), 1)], lists_in.at[:, pl.ds(i, 1)]

    def send_list(i):
        remote(*list_to(i), list_send, list_recv.at[i], other(i), r).start()

    @pl.when(core == 0)
    def _():
        pl.semaphore_wait(met, 1)
        repeat(0, half - 1, lambda i: send_list(half - 1 - i))
        pltpu.make_async_copy(*list_to(0), list_recv.at[0]).start()

    @pl.when(core == 1)
    def _():
        pl.semaphore_wait(barrier, n - 1 + half + lane * half)
        pl.semaphore_signal(met, inc=1, device_id=(me, mate), device_id_type=MESH)
        repeat(0, half, lambda i: send_list(half - 1 - i))

    count_row = jnp.concatenate(
        [info[q, n + i : n + i + 1, 0:share] for q in range(2) for i in range(img_dev)], axis=1
    ).astype(f32)
    pltpu.make_async_copy(both.at[1 - core], both.at[1 - core], both_recv).wait()

    def pick(asked, none, dead):
        at = lax.broadcasted_iota(i32, (asked.shape[0], 2 * rows), 1)
        chosen = jnp.where(asked == at, 1.0, 0.0)
        live = jnp.sum(chosen * count_row, axis=1, keepdims=True)
        live = jnp.where(asked < 0, none, live)
        found = dot(chosen.astype(bf16), both[...].reshape(2 * rows, width))
        slot_of = (lax.broadcasted_iota(i32, found.shape, 1) // DESC).astype(f32)
        return jnp.where(slot_of < live, found, dead).astype(bf16)

    for g in range(0, half, group):
        block = pick(found_at[g // group], float(kp), -far_entry)
        for i in range(g, g + group):
            q_out[i] = block[(i - g) * qn : (i - g + 1) * qn]

    def q_to(i):
        return q_out.at[i], q_in.at[side * half + i]

    def candidates(indices):
        picks = []
        for i in indices:
            ref = lists_in.at[:, pl.ds(i, 1)]
            pltpu.make_async_copy(ref, ref, list_recv.at[i]).wait()
            for q in range(2):
                asked = lists_in[q, pl.ds(i, 1), 0:slots]
                picks.append(column(asked.astype(f32), slots))
        return pick(jnp.concatenate(picks, axis=0).astype(i32), 0.0, far_entry)

    def prepared(block):
        wide = stacked(block).astype(f32)
        high, low = split(wide * wide)
        ones = jnp.ones(wide.shape, bf16)
        return jnp.concatenate([high, low, (-2.0 * wide).astype(bf16), ones, ones], axis=1)

    cn = 2 * slots

    def prepare(indices, place):
        for g in range(0, len(indices), group):
            block = candidates(indices[g : g + group])
            for p in range(g, min(g + group, len(indices))):
                lhs[place(p)] = prepared(block[(p - g) * cn : (p - g + 1) * cn])

    qd = qn * kp

    def queries(i):
        for s in range(sides):
            ref = q_in.at[s * half + i]
            pltpu.make_async_copy(ref, ref, q_recv.at[s, i]).wait()
        to = lax.broadcasted_iota(i32, (qd, sides * qd), 0)
        at = lax.broadcasted_iota(i32, (qd, sides * qd), 1) % qd
        order = jnp.where(at == (to % kp) * qn + to // kp, 1.0, 0.0).astype(bf16)
        stack = jnp.concatenate([stacked(q_in[s * half + i]) for s in range(sides)], axis=0)
        query = dot(order, stack)
        high, low = split(query * query)
        ones = jnp.ones((qd, DESC), bf16)
        return jnp.concatenate([ones, ones, query.astype(bf16), high, low], axis=1)

    def keep(p, i, two):
        image = lists_in[0, pl.ds(i, 1), 0:1] // share
        image = jnp.broadcast_to(image.astype(f32), (1, qd))
        part_out[p] = jnp.minimum(jnp.concatenate([*two, image, image], axis=0), distant)

    everyone = [s * 2 + c for s in range(sides) for c in range(2)]
    others = (across, mate, (1 - side) * 2 + (1 - core))

    def to_owner(p, j, place):
        for to_rep in everyone:
            remote(part_out.at[p], place, own_send, own_recv, j, to_rep).start()

    def to_group(ref, place):
        for to_rep in others:
            remote(ref, place, arr_send, arr_recv, me, to_rep).start()
        pltpu.make_async_copy(ref, place, arr_recv).start()

    @pl.when(core == 0)
    def _():
        def send_near(i):
            remote(*q_to(i), q_send, q_recv.at[1, i], other(i), across).start()
            remote(*q_to(i), q_send, q_recv.at[0, i], other(i), r).start()

        repeat(0, half - 1, lambda i: send_near(half - 1 - i))
        remote(*q_to(0), q_send, q_recv.at[1, 0], me, across).start()
        pltpu.make_async_copy(*q_to(0), q_recv.at[0, 0]).start()

        prepare(list(range(half)), lambda p: p)
        place = own.at[side * n + me]

        def near_pair(i):
            keep(i, i, lowest_two(dot_t(lhs[i], queries(i))))

        def near_step(i):
            near_pair(i)
            to_owner(i, other(i), place)

        repeat(0, half - 1, lambda i: near_step(half - 1 - i))
        near_pair(0)
        for to_rep in others:
            remote(part_out.at[0], place, own_send, own_recv, me, to_rep).start()
        pltpu.make_async_copy(part_out.at[0], place, own_recv).start()
        to_group(part_out, arr.at[pl.ds(side * half, half)])

    @pl.when(core == 1)
    def _():
        def send_far(i):
            remote(*q_to(i), q_send, q_recv.at[lane, i], other(i), me % 2 * 2 + 1).start()

        repeat(0, half, lambda i: send_far(half - 1 - i))

        flip = (1 + me // half + me // mine) % 2 * (mine // 2)
        turns = [(q + flip) % mine for q in range(mine)]
        for p in turns:
            c_out[p] = candidates([2 * p + 1 - lane])
            remote(c_out.at[p], c_in.at[p], c_send, c_recv.at[p], me, across).start()

        prepare([2 * p + lane for p in turns], lambda q: turns[q])

        def far_first(p):
            i = 2 * p + lane
            rhs[p] = queries(i)
            keep(p, i, lowest_two(dot_t(lhs[p], rhs[p])))


        def far_last(p):
            pltpu.make_async_copy(c_in.at[p], c_in.at[p], c_recv.at[p]).wait()
            two = lowest_two(dot_t(prepared(c_in[p]), rhs[p]))
            before = part_out[p]
            i = 2 * p + lane
            keep(p, i, merge((before[0:1], before[1:2]), two))
            to_owner(p, other(i), own.at[me])

        for p in turns:
            far_first(p)
            far_last(p)
        to_group(part_out.at[pl.ds(0, mine)], arr.at[pl.ds(n + side * mine, mine)])

    drain(info.at[0], info_send)
    drain(both.at[0], both_send)

    @pl.when(core == 0)
    def _():
        drain(lists_in.at[:, pl.ds(0, half - 1)], list_send)
        drain(q_in.at[pl.ds(0, n - 1)], q_send)
        drain(own.at[pl.ds(0, 2 * n - 1)], own_send)
        drain(arr, arr_send)

    @pl.when(core == 1)
    def _():
        drain(lists_in.at[:, pl.ds(0, half)], list_send)
        drain(q_in.at[pl.ds(0, half)], q_send)
        drain(c_in, c_send)
        drain(own.at[pl.ds(0, n)], own_send)
        drain(arr.at[pl.ds(0, 3 * mine)], arr_send)

    drain(own.at[pl.ds(0, n + half)], own_recv)
    drain(arr, arr_recv)


def finish(n, img_dev, own, arr, firsts, matches, scores):
    half = n // 2

    def pair(ref, first, last):
        return ref[first:last, 0, :], ref[first:last, 1, :]

    def scored(two):
        live = two[0] < 0.5 * distant
        best, runner = jnp.where(live, two[0], 0.0), jnp.where(live, two[1], 0.0)
        margin = jnp.where(live, (runner - best) / (runner + 1.0), 0.0)
        total = jnp.sum(margin, axis=1, keepdims=True)
        return best, runner, total / jnp.sum(live.astype(f32), axis=1, keepdims=True)

    whole = pair(own, 0, n)
    halves = merge(whole, pair(own, n, 2 * n))
    mine = lax.axis_index("img") // half
    is_near = lax.broadcasted_iota(i32, whole[0].shape, 0) // half == mine
    best, runner, score = scored([jnp.where(is_near, a, b) for a, b in zip(halves, whole)])
    matches[:, 0, :] = best
    matches[:, 1, :] = runner
    first = firsts[:, 0:1]

    def per_image(image, score):
        at = lax.broadcasted_iota(i32, (image.shape[0], img_dev), 1).astype(f32)
        return jnp.sum(jnp.where(image == at, score, 0.0), axis=0)

    close = merge(pair(arr, 0, half), pair(arr, half, n))
    apart = pair(arr, n, n + half)
    total = per_image(first, score)
    total = total + per_image(arr[0:half, 2, 0:1], scored(close)[2])
    scores[...] = total + per_image(arr[n : n + half, 2, 0:1], scored(apart)[2])


def on_device(n, m, descriptors, cell_counts, pair_images, query_cells, cand_cells, cand_counts):
    img_dev, share, width = descriptors.shape
    slots, qn = cand_cells.shape[2], query_cells.shape[1]
    qd = qn * width // DESC
    sides, half, mine = m // 2, n // 2, n // 4
    vmem = pl.BlockSpec(memory_space=pltpu.VMEM)
    dma = pltpu.SemaphoreType.DMA
    operands = (
        descriptors, cell_counts, pair_images.T, query_cells, cand_cells, cand_counts.T,
    )
    hbm = pl.BlockSpec(memory_space=pltpu.HBM)
    info_rows = (n + img_dev + 7) // 8 * 8
    own, arr, firsts = pl.pallas_call(
        functools.partial(kernel, n, sides),
        out_shape=(
            pltpu.VMEM((sides * n, 4, qd), f32),
            pltpu.VMEM((n + half, 4, qd), f32),
            pltpu.VMEM((n, DESC), f32),
        ),
        in_specs=[hbm] * 6,
        out_specs=(vmem,) * 3,
        scratch_shapes=[
            pltpu.VMEM((2, *descriptors.shape), bf16),
            *(pltpu.VMEM(x.shape, x.dtype) for x in operands[1:]),
            dma((len(operands),)),
            pltpu.VMEM((2, info_rows, DESC), i32),
            pltpu.VMEM((2, (half + 7) // 8 * 8, DESC), i32),
            pltpu.VMEM(query_cells.shape, i32),
            pltpu.VMEM((half, qn, width), bf16),
            pltpu.VMEM((sides * half, qn, width), bf16),
            pltpu.VMEM((mine, 2 * slots, width), bf16),
            pltpu.VMEM((mine, 2 * slots, width), bf16),
            pltpu.VMEM((half, 2 * slots * width // DESC, 5 * DESC), bf16),
            pltpu.VMEM((mine, qd, 5 * DESC), bf16),
            pltpu.VMEM((half, 4, qd), f32),
            dma, dma, dma, dma, dma, dma((half,)),
            dma, dma((sides, half)), dma, dma((mine,)), dma, dma, dma, dma,
            pltpu.SemaphoreType.REGULAR,
        ],
        compiler_params=pltpu.CompilerParams(
            collective_id=0, has_side_effects=True
        ),
    )(*operands)
    held = functools.partial(pltpu.with_memory_space_constraint, memory_space=pltpu.VMEM)
    return pl.pallas_call(
        functools.partial(finish, n, img_dev),
        out_shape=(
            jax.ShapeDtypeStruct((n, 2, qd), f32),
            jax.ShapeDtypeStruct((img_dev,), f32),
        ),
        in_specs=[vmem] * 3,
        out_specs=(vmem, vmem),
    )(held(own), held(arr), held(firsts))


def solution(mesh):
    n, m = mesh.shape["img"], mesh.shape["rep"]
    in_specs = (
        P("img", "rep", None),
        P("img", "rep"),
        P("img", None),
        P("img", None),
        P("img", "rep", None),
        P("img", "rep"),
    )
    out_specs = (P("img", None, None), P("img"))
    return jax.shard_map(
        functools.partial(on_device, n, m),
        mesh=mesh, in_specs=in_specs, out_specs=out_specs, check_vma=False,
    )
```

```python
import functools

import jax
import jax.numpy as jnp
from jax import lax
from jax.experimental import pallas as pl
from jax.experimental.pallas import tpu as pltpu
from jax.sharding import PartitionSpec as P

DESC = 128
MESH = pl.DeviceIdType.MESH
distant = 1.0e9
far_entry = 32768.0
f32, bf16, i32 = jnp.float32, jnp.bfloat16, jnp.int32


def flips(me, size):
    steps, bit = [], 1
    while bit < size:
        steps.append(bit - (me // bit) % 2 * (2 * bit))
        bit *= 2
    return steps


def repeat(first, last, body):
    if last - first <= 8:
        for t in range(first, last):
            body(t)
    else:
        lax.fori_loop(first, last, lambda t, c: (body(t), c)[1], 0)


def dot(a, b):
    return jnp.dot(a, b, preferred_element_type=f32)


def dot_t(a, b):
    return lax.dot_general(a, b, (((1,), (1,)), ((), ())), preferred_element_type=f32)


def split(square):
    high = square.astype(bf16)
    return high, (square - high.astype(f32)).astype(bf16)


def column(row, length):
    rows = lax.broadcasted_iota(i32, (length, length), 0)
    cols = lax.broadcasted_iota(i32, (length, length), 1)
    return jnp.sum(jnp.where(rows == cols, row, 0.0), axis=1, keepdims=True)


def merge(a, b):
    low = jnp.minimum(a[0], b[0])
    high = jnp.minimum(jnp.maximum(a[0], b[0]), jnp.minimum(a[1], b[1]))
    return low, high


def lowest_two(d):
    half = d.shape[0] // 2
    a, b = d[:half], d[half:]
    two = (jnp.minimum(a, b), jnp.maximum(a, b))
    while half > 1:
        half //= 2
        two = merge((two[0][:half], two[1][:half]), (two[0][half:], two[1][half:]))
    return two


def stacked(cells):
    kp = cells.shape[1] // DESC
    return jnp.concatenate([cells[:, s * DESC : (s + 1) * DESC] for s in range(kp)], axis=0)


def kernel(
    n, sides,
    desc_hbm, counts_hbm, pairs_hbm, qcells_hbm, ccells_hbm, ccounts_hbm,
    own, arr, firsts,
    both, counts, pairs, qcells, ccells, ccounts, in_sem,
    info, lists_in, asked_at, q_out, q_in, c_out, c_in, lhs, rhs, part_out,
    info_send, info_recv, both_send, both_recv, list_send, list_recv,
    q_send, q_recv, c_send, c_recv, own_send, own_recv, arr_send, arr_recv, met,
):
    me, r = lax.axis_index("img"), lax.axis_index("rep")
    side, core = r // 2, r % 2
    mate = side * 2 + (1 - core)
    across = (1 - side) * 2 + core
    img_dev, share, width = both.shape[1:]
    rows = img_dev * share
    kp = width // DESC
    slots = ccells.shape[2]
    qn = qcells.shape[1]
    half, mine = n // 2, n // 4
    lane = (side + me) % 2

    def remote(src, dst, send, recv, img, rep):
        return pltpu.make_async_remote_copy(
            src_ref=src, dst_ref=dst, send_sem=send, recv_sem=recv,
            device_id=(img, rep), device_id_type=MESH,
        )

    def drain(ref, sem):
        pltpu.make_async_copy(ref, ref, sem).wait()

    steps = flips(me, n)
    base = me + core * steps[-1]

    def other(i):
        if isinstance(i, int):
            return base + sum(step for k, step in enumerate(steps[:-1]) if i >> k & 1)
        return base + sum(i // 2**k % 2 * step for k, step in enumerate(steps[:-1]))

    barrier = pltpu.get_barrier_semaphore()

    def greet(img, rep):
        pl.semaphore_signal(barrier, inc=1, device_id=(img, rep), device_id_type=MESH)

    @pl.when(core == 0)
    def _():
        def greet_near(i):
            greet(other(i), mate)
            greet(other(i), (1 - side) * 2 + 1)

        repeat(0, half - 1, lambda i: greet_near(half - 1 - i))
        greet(other(0), (1 - side) * 2 + 1)

    @pl.when(core == 1)
    def _():
        greet(me, mate)
        repeat(0, half, lambda i: greet(other(half - 1 - i), r))
        repeat(0, mine, lambda p: greet(other(2 * (mine - 1 - p) + lane), across))

    small = [
        pltpu.make_async_copy(src, dst, in_sem.at[i])
        for i, (src, dst) in enumerate((
            (counts_hbm, counts), (pairs_hbm, pairs),
            (ccells_hbm, ccells), (ccounts_hbm, ccounts), (qcells_hbm, qcells),
        ))
    ]
    shard = pltpu.make_async_copy(desc_hbm, both.at[core], in_sem.at[len(small)])
    for load in small:
        load.start()
    shard.start()
    for load in small:
        load.wait()

    local = (pairs[...] % img_dev).astype(f32)
    first = column(local[0:1], n).astype(i32)
    second = column(local[1:2], n).astype(i32)
    live_cells = column(ccounts[...].astype(f32), n).astype(i32)
    wanted = core * rows + second * share + ccells[:, 0, :] % share
    wanted = jnp.where(lax.broadcasted_iota(i32, (n, slots), 1) < live_cells, wanted, -1)
    info[core, 0:n, 0:slots] = wanted
    firsts[...] = jnp.broadcast_to(first, firsts.shape).astype(f32)
    info[core, n : n + img_dev, 0:share] = counts[...]

    @pl.when(core == 0)
    def _():
        pl.semaphore_wait(barrier, 1)
        pl.semaphore_signal(met, inc=1, device_id=(me, mate), device_id_type=MESH)

    @pl.when(core == 1)
    def _():
        pl.semaphore_wait(met, 1)

    remote(info.at[core], info.at[core], info_send, info_recv, me, mate).start()
    shard.wait()
    remote(both.at[core], both.at[core], both_send, both_recv, me, mate).start()

    cells = qcells[...]
    quarter = cells // share
    where = (quarter % 2) * rows + first * share + cells % share
    asked_at[...] = jnp.where(quarter // 2 == side, where, -1)
    group = min(half, 4)
    found_at = []
    for g in range(0, half, group):
        picks = [
            column(asked_at[pl.ds(other(i), 1), :].astype(f32), qn) for i in range(g, g + group)
        ]
        found_at.append(jnp.concatenate(picks, axis=0).astype(i32))

    pltpu.make_async_copy(info.at[1 - core], info.at[1 - core], info_recv).wait()

    def list_to(i):
        return info.at[:, pl.ds(other(i), 1)], lists_in.at[:, pl.ds(i, 1)]

    def send_list(i):
        remote(*list_to(i), list_send, list_recv.at[i], other(i), r).start()

    count_row = jnp.concatenate(
        [info[q, n + i : n + i + 1, 0:share] for q in range(2) for i in range(img_dev)], axis=1
    ).astype(f32)
    pltpu.make_async_copy(both.at[1 - core], both.at[1 - core], both_recv).wait()

    def pick(asked, none, dead):
        at = lax.broadcasted_iota(i32, (asked.shape[0], 2 * rows), 1)
        chosen = jnp.where(asked == at, 1.0, 0.0)
        live = jnp.sum(chosen * count_row, axis=1, keepdims=True)
        live = jnp.where(asked < 0, none, live)
        found = dot(chosen.astype(bf16), both[...].reshape(2 * rows, width))
        slot_of = (lax.broadcasted_iota(i32, found.shape, 1) // DESC).astype(f32)
        return jnp.where(slot_of < live, found, dead).astype(bf16)

    for g in range(0, half, group):
        block = pick(found_at[g // group], float(kp), -far_entry)
        for i in range(g, g + group):
            q_out[i] = block[(i - g) * qn : (i - g + 1) * qn]

    @pl.when(core == 0)
    def _():
        pl.semaphore_wait(met, 1)
        repeat(0, half - 1, lambda i: send_list(half - 1 - i))
        pltpu.make_async_copy(*list_to(0), list_recv.at[0]).start()

    @pl.when(core == 1)
    def _():
        pl.semaphore_wait(barrier, n - 1 + half + lane * half)
        pl.semaphore_signal(met, inc=1, device_id=(me, mate), device_id_type=MESH)
        repeat(0, half, lambda i: send_list(half - 1 - i))

    def q_to(i):
        return q_out.at[i], q_in.at[side * half + i]

    def candidates(indices):
        picks = []
        for i in indices:
            ref = lists_in.at[:, pl.ds(i, 1)]
            pltpu.make_async_copy(ref, ref, list_recv.at[i]).wait()
            for q in range(2):
                asked = lists_in[q, pl.ds(i, 1), 0:slots]
                picks.append(column(asked.astype(f32), slots))
        return pick(jnp.concatenate(picks, axis=0).astype(i32), 0.0, far_entry)

    def prepared(block):
        wide = stacked(block).astype(f32)
        high, low = split(wide * wide)
        ones = jnp.ones(wide.shape, bf16)
        return jnp.concatenate([high, low, (-2.0 * wide).astype(bf16), ones, ones], axis=1)

    cn = 2 * slots

    def prepare(indices, place):
        for g in range(0, len(indices), group):
            block = candidates(indices[g : g + group])
            for p in range(g, min(g + group, len(indices))):
                lhs[place(p)] = prepared(block[(p - g) * cn : (p - g + 1) * cn])

    qd = qn * kp

    def queries(i):
        for s in range(sides):
            ref = q_in.at[s * half + i]
            pltpu.make_async_copy(ref, ref, q_recv.at[s, i]).wait()
        to = lax.broadcasted_iota(i32, (qd, sides * qd), 0)
        at = lax.broadcasted_iota(i32, (qd, sides * qd), 1) % qd
        order = jnp.where(at == (to % kp) * qn + to // kp, 1.0, 0.0).astype(bf16)
        stack = jnp.concatenate([stacked(q_in[s * half + i]) for s in range(sides)], axis=0)
        query = dot(order, stack)
        high, low = split(query * query)
        ones = jnp.ones((qd, DESC), bf16)
        return jnp.concatenate([ones, ones, query.astype(bf16), high, low], axis=1)

    def keep(p, i, two):
        image = lists_in[0, pl.ds(i, 1), 0:1] // share
        image = jnp.broadcast_to(image.astype(f32), (1, qd))
        part_out[p] = jnp.minimum(jnp.concatenate([*two, image, image], axis=0), distant)

    everyone = [s * 2 + c for s in range(sides) for c in range(2)]
    others = (across, mate, (1 - side) * 2 + (1 - core))

    def to_owner(p, j, place):
        for to_rep in everyone:
            remote(part_out.at[p], place, own_send, own_recv, j, to_rep).start()

    def to_group(ref, place):
        for to_rep in others:
            remote(ref, place, arr_send, arr_recv, me, to_rep).start()
        pltpu.make_async_copy(ref, place, arr_recv).start()

    @pl.when(core == 0)
    def _():
        def send_near(i):
            remote(*q_to(i), q_send, q_recv.at[1, i], other(i), across).start()
            remote(*q_to(i), q_send, q_recv.at[0, i], other(i), r).start()

        repeat(0, half - 1, lambda i: send_near(half - 1 - i))
        remote(*q_to(0), q_send, q_recv.at[1, 0], me, across).start()
        pltpu.make_async_copy(*q_to(0), q_recv.at[0, 0]).start()

        prepare(list(range(half)), lambda p: p)
        place = own.at[side * n + me]

        def near_pair(i):
            keep(i, i, lowest_two(dot_t(lhs[i], queries(i))))

        def near_step(i):
            near_pair(i)
            to_owner(i, other(i), place)

        repeat(0, half - 1, lambda i: near_step(half - 1 - i))
        near_pair(0)
        for to_rep in others:
            remote(part_out.at[0], place, own_send, own_recv, me, to_rep).start()
        pltpu.make_async_copy(part_out.at[0], place, own_recv).start()
        to_group(part_out, arr.at[pl.ds(side * half, half)])

    @pl.when(core == 1)
    def _():
        def send_far(i):
            remote(*q_to(i), q_send, q_recv.at[lane, i], other(i), me % 2 * 2 + 1).start()

        repeat(0, half, lambda i: send_far(half - 1 - i))

        flip = (1 + me // half + me // mine) % 2 * (mine // 2)
        turns = [(q + flip) % mine for q in range(mine)]
        for p in turns:
            c_out[p] = candidates([2 * p + 1 - lane])
            remote(c_out.at[p], c_in.at[p], c_send, c_recv.at[p], me, across).start()

        prepare([2 * p + lane for p in turns], lambda q: turns[q])

        def far_first(p):
            i = 2 * p + lane
            rhs[p] = queries(i)
            keep(p, i, lowest_two(dot_t(lhs[p], rhs[p])))


        def far_last(p):
            pltpu.make_async_copy(c_in.at[p], c_in.at[p], c_recv.at[p]).wait()
            two = lowest_two(dot_t(prepared(c_in[p]), rhs[p]))
            before = part_out[p]
            i = 2 * p + lane
            keep(p, i, merge((before[0:1], before[1:2]), two))
            to_owner(p, other(i), own.at[me])

        for p in turns:
            far_first(p)
            far_last(p)
        to_group(part_out.at[pl.ds(0, mine)], arr.at[pl.ds(n + side * mine, mine)])

    drain(info.at[0], info_send)
    drain(both.at[0], both_send)

    @pl.when(core == 0)
    def _():
        drain(lists_in.at[:, pl.ds(0, half - 1)], list_send)
        drain(q_in.at[pl.ds(0, n - 1)], q_send)
        drain(own.at[pl.ds(0, 2 * n - 1)], own_send)
        drain(arr, arr_send)

    @pl.when(core == 1)
    def _():
        drain(lists_in.at[:, pl.ds(0, half)], list_send)
        drain(q_in.at[pl.ds(0, half)], q_send)
        drain(c_in, c_send)
        drain(own.at[pl.ds(0, n)], own_send)
        drain(arr.at[pl.ds(0, 3 * mine)], arr_send)

    drain(own.at[pl.ds(0, n + half)], own_recv)
    drain(arr, arr_recv)


def finish(n, img_dev, own, arr, firsts, matches, scores):
    half = n // 2

    def pair(ref, first, last):
        return ref[first:last, 0, :], ref[first:last, 1, :]

    def scored(two):
        live = two[0] < 0.5 * distant
        best, runner = jnp.where(live, two[0], 0.0), jnp.where(live, two[1], 0.0)
        margin = jnp.where(live, (runner - best) / (runner + 1.0), 0.0)
        total = jnp.sum(margin, axis=1, keepdims=True)
        return best, runner, total / jnp.sum(live.astype(f32), axis=1, keepdims=True)

    whole = pair(own, 0, n)
    halves = merge(whole, pair(own, n, 2 * n))
    mine = lax.axis_index("img") // half
    is_near = lax.broadcasted_iota(i32, whole[0].shape, 0) // half == mine
    best, runner, score = scored([jnp.where(is_near, a, b) for a, b in zip(halves, whole)])
    matches[:, 0, :] = best
    matches[:, 1, :] = runner
    first = firsts[:, 0:1]

    def per_image(image, score):
        at = lax.broadcasted_iota(i32, (image.shape[0], img_dev), 1).astype(f32)
        return jnp.sum(jnp.where(image == at, score, 0.0), axis=0)

    close = merge(pair(arr, 0, half), pair(arr, half, n))
    apart = pair(arr, n, n + half)
    total = per_image(first, score)
    total = total + per_image(arr[0:half, 2, 0:1], scored(close)[2])
    scores[...] = total + per_image(arr[n : n + half, 2, 0:1], scored(apart)[2])


def on_device(n, m, descriptors, cell_counts, pair_images, query_cells, cand_cells, cand_counts):
    img_dev, share, width = descriptors.shape
    slots, qn = cand_cells.shape[2], query_cells.shape[1]
    qd = qn * width // DESC
    sides, half, mine = m // 2, n // 2, n // 4
    vmem = pl.BlockSpec(memory_space=pltpu.VMEM)
    dma = pltpu.SemaphoreType.DMA
    operands = (
        descriptors, cell_counts, pair_images.T, query_cells, cand_cells, cand_counts.T,
    )
    hbm = pl.BlockSpec(memory_space=pltpu.HBM)
    info_rows = (n + img_dev + 7) // 8 * 8
    own, arr, firsts = pl.pallas_call(
        functools.partial(kernel, n, sides),
        out_shape=(
            pltpu.VMEM((sides * n, 4, qd), f32),
            pltpu.VMEM((n + half, 4, qd), f32),
            pltpu.VMEM((n, DESC), f32),
        ),
        in_specs=[hbm] * 6,
        out_specs=(vmem,) * 3,
        scratch_shapes=[
            pltpu.VMEM((2, *descriptors.shape), bf16),
            *(pltpu.VMEM(x.shape, x.dtype) for x in operands[1:]),
            dma((len(operands),)),
            pltpu.VMEM((2, info_rows, DESC), i32),
            pltpu.VMEM((2, (half + 7) // 8 * 8, DESC), i32),
            pltpu.VMEM(query_cells.shape, i32),
            pltpu.VMEM((half, qn, width), bf16),
            pltpu.VMEM((sides * half, qn, width), bf16),
            pltpu.VMEM((mine, 2 * slots, width), bf16),
            pltpu.VMEM((mine, 2 * slots, width), bf16),
            pltpu.VMEM((half, 2 * slots * width // DESC, 5 * DESC), bf16),
            pltpu.VMEM((mine, qd, 5 * DESC), bf16),
            pltpu.VMEM((half, 4, qd), f32),
            dma, dma, dma, dma, dma, dma((half,)),
            dma, dma((sides, half)), dma, dma((mine,)), dma, dma, dma, dma,
            pltpu.SemaphoreType.REGULAR,
        ],
        compiler_params=pltpu.CompilerParams(
            collective_id=0, has_side_effects=True
        ),
    )(*operands)
    held = functools.partial(pltpu.with_memory_space_constraint, memory_space=pltpu.VMEM)
    return pl.pallas_call(
        functools.partial(finish, n, img_dev),
        out_shape=(
            jax.ShapeDtypeStruct((n, 2, qd), f32),
            jax.ShapeDtypeStruct((img_dev,), f32),
        ),
        in_specs=[vmem] * 3,
        out_specs=(vmem, vmem),
    )(held(own), held(arr), held(firsts))


def solution(mesh):
    n, m = mesh.shape["img"], mesh.shape["rep"]
    in_specs = (
        P("img", "rep", None),
        P("img", "rep"),
        P("img", None),
        P("img", None),
        P("img", "rep", None),
        P("img", "rep"),
    )
    out_specs = (P("img", None, None), P("img"))
    return jax.shard_map(
        functools.partial(on_device, n, m),
        mesh=mesh, in_specs=in_specs, out_specs=out_specs, check_vma=False,
    )
```

```python
import functools

import jax
import jax.numpy as jnp
from jax import lax
from jax.experimental import pallas as pl
from jax.experimental.pallas import tpu as pltpu
from jax.sharding import PartitionSpec as P

DESC = 128
MESH = pl.DeviceIdType.MESH
distant = 1.0e9
far_entry = 32768.0
f32, bf16, i32 = jnp.float32, jnp.bfloat16, jnp.int32


def flips(me, size):
    steps, bit = [], 1
    while bit < size:
        steps.append(bit - (me // bit) % 2 * (2 * bit))
        bit *= 2
    return steps


def repeat(first, last, body):
    if last - first <= 8:
        for t in range(first, last):
            body(t)
    else:
        lax.fori_loop(first, last, lambda t, c: (body(t), c)[1], 0)


def dot(a, b):
    return jnp.dot(a, b, preferred_element_type=f32)


def dot_t(a, b):
    return lax.dot_general(a, b, (((1,), (1,)), ((), ())), preferred_element_type=f32)


def split(square):
    high = square.astype(bf16)
    return high, (square - high.astype(f32)).astype(bf16)


def column(row, length):
    rows = lax.broadcasted_iota(i32, (length, length), 0)
    cols = lax.broadcasted_iota(i32, (length, length), 1)
    return jnp.sum(jnp.where(rows == cols, row, 0.0), axis=1, keepdims=True)


def merge(a, b):
    low = jnp.minimum(a[0], b[0])
    high = jnp.minimum(jnp.maximum(a[0], b[0]), jnp.minimum(a[1], b[1]))
    return low, high


def lowest_two(d):
    half = d.shape[0] // 2
    a, b = d[:half], d[half:]
    two = (jnp.minimum(a, b), jnp.maximum(a, b))
    while half > 1:
        half //= 2
        two = merge((two[0][:half], two[1][:half]), (two[0][half:], two[1][half:]))
    return two


def stacked(cells):
    kp = cells.shape[1] // DESC
    return jnp.concatenate([cells[:, s * DESC : (s + 1) * DESC] for s in range(kp)], axis=0)


def kernel(
    n, sides,
    desc_hbm, counts_hbm, pairs_hbm, qcells_hbm, ccells_hbm, ccounts_hbm,
    own, arr, firsts,
    both, counts, pairs, qcells, ccells, ccounts, in_sem,
    info, lists_in, asked_at, q_out, q_in, c_out, c_in, lhs, rhs, part_out,
    info_send, info_recv, both_send, both_recv, list_send, list_recv,
    q_send, q_recv, c_send, c_recv, own_send, own_recv, arr_send, arr_recv, met,
):
    me, r = lax.axis_index("img"), lax.axis_index("rep")
    side, core = r // 2, r % 2
    mate = side * 2 + (1 - core)
    across = (1 - side) * 2 + core
    img_dev, share, width = both.shape[1:]
    rows = img_dev * share
    kp = width // DESC
    slots = ccells.shape[2]
    qn = qcells.shape[1]
    half, mine = n // 2, n // 4
    lane = (side + me) % 2

    def remote(src, dst, send, recv, img, rep):
        return pltpu.make_async_remote_copy(
            src_ref=src, dst_ref=dst, send_sem=send, recv_sem=recv,
            device_id=(img, rep), device_id_type=MESH,
        )

    def drain(ref, sem):
        pltpu.make_async_copy(ref, ref, sem).wait()

    steps = flips(me, n)
    base = me + core * steps[-1]

    def other(i):
        if isinstance(i, int):
            return base + sum(step for k, step in enumerate(steps[:-1]) if i >> k & 1)
        return base + sum(i // 2**k % 2 * step for k, step in enumerate(steps[:-1]))

    barrier = pltpu.get_barrier_semaphore()

    def greet(img, rep):
        pl.semaphore_signal(barrier, inc=1, device_id=(img, rep), device_id_type=MESH)

    @pl.when(core == 0)
    def _():
        def greet_near(i):
            greet(other(i), mate)
            greet(other(i), (1 - side) * 2 + 1)

        repeat(0, half - 1, lambda i: greet_near(half - 1 - i))
        greet(other(0), (1 - side) * 2 + 1)

    @pl.when(core == 1)
    def _():
        greet(me, mate)
        repeat(0, half, lambda i: greet(other(half - 1 - i), r))
        repeat(0, mine, lambda p: greet(other(2 * (mine - 1 - p) + lane), across))

    small = [
        pltpu.make_async_copy(src, dst, in_sem.at[i])
        for i, (src, dst) in enumerate((
            (counts_hbm, counts), (pairs_hbm, pairs),
            (ccells_hbm, ccells), (ccounts_hbm, ccounts), (qcells_hbm, qcells),
        ))
    ]
    shard = pltpu.make_async_copy(desc_hbm, both.at[core], in_sem.at[len(small)])
    for load in small:
        load.start()
    shard.start()
    for load in small:
        load.wait()

    local = (pairs[...] % img_dev).astype(f32)
    first = column(local[0:1], n).astype(i32)
    second = column(local[1:2], n).astype(i32)
    live_cells = column(ccounts[...].astype(f32), n).astype(i32)
    wanted = core * rows + second * share + ccells[:, 0, :] % share
    wanted = jnp.where(lax.broadcasted_iota(i32, (n, slots), 1) < live_cells, wanted, -1)
    info[core, 0:n, 0:slots] = wanted
    firsts[...] = jnp.broadcast_to(first, firsts.shape).astype(f32)
    info[core, n : n + img_dev, 0:share] = counts[...]

    @pl.when(core == 0)
    def _():
        pl.semaphore_wait(barrier, 1)
        pl.semaphore_signal(met, inc=1, device_id=(me, mate), device_id_type=MESH)

    @pl.when(core == 1)
    def _():
        pl.semaphore_wait(met, 1)

    remote(info.at[core], info.at[core], info_send, info_recv, me, mate).start()
    shard.wait()
    remote(both.at[core], both.at[core], both_send, both_recv, me, mate).start()

    cells = qcells[...]
    quarter = cells // share
    where = (quarter % 2) * rows + first * share + cells % share
    asked_at[...] = jnp.where(quarter // 2 == side, where, -1)
    group = min(half, 4)
    found_at = []
    for g in range(0, half, group):
        picks = [
            column(asked_at[pl.ds(other(i), 1), :].astype(f32), qn) for i in range(g, g + group)
        ]
        found_at.append(jnp.concatenate(picks, axis=0).astype(i32))

    pltpu.make_async_copy(info.at[1 - core], info.at[1 - core], info_recv).wait()

    def list_to(i):
        return info.at[:, pl.ds(other(i), 1)], lists_in.at[:, pl.ds(i, 1)]

    def send_list(i):
        remote(*list_to(i), list_send, list_recv.at[i], other(i), r).start()

    count_row = jnp.concatenate(
        [info[q, n + i : n + i + 1, 0:share] for q in range(2) for i in range(img_dev)], axis=1
    ).astype(f32)
    pltpu.make_async_copy(both.at[1 - core], both.at[1 - core], both_recv).wait()

    def pick(asked, none, dead):
        at = lax.broadcasted_iota(i32, (asked.shape[0], 2 * rows), 1)
        chosen = jnp.where(asked == at, 1.0, 0.0)
        live = jnp.sum(chosen * count_row, axis=1, keepdims=True)
        live = jnp.where(asked < 0, none, live)
        found = dot(chosen.astype(bf16), both[...].reshape(2 * rows, width))
        slot_of = (lax.broadcasted_iota(i32, found.shape, 1) // DESC).astype(f32)
        return jnp.where(slot_of < live, found, dead).astype(bf16)

    for g in range(0, half, group):
        block = pick(found_at[g // group], float(kp), -far_entry)
        for i in range(g, g + group):
            q_out[i] = block[(i - g) * qn : (i - g + 1) * qn]

    @pl.when(core == 0)
    def _():
        pl.semaphore_wait(met, 1)
        repeat(0, half - 1, lambda i: send_list(half - 1 - i))
        pltpu.make_async_copy(*list_to(0), list_recv.at[0]).start()

    @pl.when(core == 1)
    def _():
        pl.semaphore_wait(barrier, n - 1 + half + lane * half)
        pl.semaphore_signal(met, inc=1, device_id=(me, mate), device_id_type=MESH)
        repeat(0, half, lambda i: send_list(half - 1 - i))

    def q_to(i):
        return q_out.at[i], q_in.at[side * half + i]

    def candidates(indices):
        picks = []
        for i in indices:
            ref = lists_in.at[:, pl.ds(i, 1)]
            pltpu.make_async_copy(ref, ref, list_recv.at[i]).wait()
            for q in range(2):
                asked = lists_in[q, pl.ds(i, 1), 0:slots]
                picks.append(column(asked.astype(f32), slots))
        return pick(jnp.concatenate(picks, axis=0).astype(i32), 0.0, far_entry)

    def prepared(block):
        wide = stacked(block).astype(f32)
        high, low = split(wide * wide)
        ones = jnp.ones(wide.shape, bf16)
        return jnp.concatenate([high, low, (-2.0 * wide).astype(bf16), ones, ones], axis=1)

    cn = 2 * slots

    def prepare(indices, place):
        for g in range(0, len(indices), group):
            block = candidates(indices[g : g + group])
            for p in range(g, min(g + group, len(indices))):
                lhs[place(p)] = prepared(block[(p - g) * cn : (p - g + 1) * cn])

    qd = qn * kp

    def queries(i):
        for s in range(sides):
            ref = q_in.at[s * half + i]
            pltpu.make_async_copy(ref, ref, q_recv.at[s, i]).wait()
        to = lax.broadcasted_iota(i32, (qd, sides * qd), 0)
        at = lax.broadcasted_iota(i32, (qd, sides * qd), 1) % qd
        order = jnp.where(at == (to % kp) * qn + to // kp, 1.0, 0.0).astype(bf16)
        stack = jnp.concatenate([stacked(q_in[s * half + i]) for s in range(sides)], axis=0)
        query = dot(order, stack)
        high, low = split(query * query)
        ones = jnp.ones((qd, DESC), bf16)
        return jnp.concatenate([ones, ones, query.astype(bf16), high, low], axis=1)

    def keep(p, i, two):
        image = lists_in[0, pl.ds(i, 1), 0:1] // share
        image = jnp.broadcast_to(image.astype(f32), (1, qd))
        part_out[p] = jnp.minimum(jnp.concatenate([*two, image, image], axis=0), distant)

    everyone = [s * 2 + c for s in range(sides) for c in range(2)]
    others = (across, mate, (1 - side) * 2 + (1 - core))

    def to_owner(p, j, place):
        for to_rep in everyone:
            remote(part_out.at[p], place, own_send, own_recv, j, to_rep).start()

    def to_group(ref, place):
        for to_rep in others:
            remote(ref, place, arr_send, arr_recv, me, to_rep).start()
        pltpu.make_async_copy(ref, place, arr_recv).start()

    @pl.when(core == 0)
    def _():
        def send_near(i):
            remote(*q_to(i), q_send, q_recv.at[1, i], other(i), across).start()
            remote(*q_to(i), q_send, q_recv.at[0, i], other(i), r).start()

        repeat(0, half - 1, lambda i: send_near(half - 1 - i))
        remote(*q_to(0), q_send, q_recv.at[1, 0], me, across).start()
        pltpu.make_async_copy(*q_to(0), q_recv.at[0, 0]).start()

        prepare(list(range(half)), lambda p: p)
        place = own.at[side * n + me]

        def near_pair(i):
            keep(i, i, lowest_two(dot_t(lhs[i], queries(i))))

        def near_step(i):
            near_pair(i)
            to_owner(i, other(i), place)

        repeat(0, half - 1, lambda i: near_step(half - 1 - i))
        near_pair(0)
        for to_rep in others:
            remote(part_out.at[0], place, own_send, own_recv, me, to_rep).start()
        pltpu.make_async_copy(part_out.at[0], place, own_recv).start()
        to_group(part_out, arr.at[pl.ds(side * half, half)])

    @pl.when(core == 1)
    def _():
        def send_far(i):
            remote(*q_to(i), q_send, q_recv.at[lane, i], other(i), me % 2 * 2 + 1).start()

        repeat(0, half, lambda i: send_far(half - 1 - i))

        flip = (1 + me // half + me // mine) % 2 * (mine // 2)
        turns = [(q + flip) % mine for q in range(mine)]
        for p in turns:
            c_out[p] = candidates([2 * p + 1 - lane])
            for q in range(2):
                piece = pl.ds(q * slots, slots)
                remote(
                    c_out.at[p, piece], c_in.at[p, piece], c_send, c_recv.at[p, q], me, across
                ).start()

        prepare([2 * p + lane for p in turns], lambda q: turns[q])

        def far_first(p):
            i = 2 * p + lane
            rhs[p] = queries(i)
            keep(p, i, lowest_two(dot_t(lhs[p], rhs[p])))


        def far_last(p):
            i = 2 * p + lane
            before = part_out[p]
            two = (before[0:1], before[1:2])
            for q in range(2):
                piece = c_in.at[p, pl.ds(q * slots, slots)]
                pltpu.make_async_copy(piece, piece, c_recv.at[p, q]).wait()
                two = merge(two, lowest_two(dot_t(prepared(piece[...]), rhs[p])))
            keep(p, i, two)
            to_owner(p, other(i), own.at[me])

        for p in turns:
            far_first(p)
            far_last(p)
        to_group(part_out.at[pl.ds(0, mine)], arr.at[pl.ds(n + side * mine, mine)])

    drain(info.at[0], info_send)
    drain(both.at[0], both_send)

    @pl.when(core == 0)
    def _():
        drain(lists_in.at[:, pl.ds(0, half - 1)], list_send)
        drain(q_in.at[pl.ds(0, n - 1)], q_send)
        drain(own.at[pl.ds(0, 2 * n - 1)], own_send)
        drain(arr, arr_send)

    @pl.when(core == 1)
    def _():
        drain(lists_in.at[:, pl.ds(0, half)], list_send)
        drain(q_in.at[pl.ds(0, half)], q_send)
        drain(c_in, c_send)
        drain(own.at[pl.ds(0, n)], own_send)
        drain(arr.at[pl.ds(0, 3 * mine)], arr_send)

    drain(own.at[pl.ds(0, n + half)], own_recv)
    drain(arr, arr_recv)


def finish(n, img_dev, own, arr, firsts, matches, scores):
    half = n // 2

    def pair(ref, first, last):
        return ref[first:last, 0, :], ref[first:last, 1, :]

    def scored(two):
        live = two[0] < 0.5 * distant
        best, runner = jnp.where(live, two[0], 0.0), jnp.where(live, two[1], 0.0)
        margin = jnp.where(live, (runner - best) / (runner + 1.0), 0.0)
        total = jnp.sum(margin, axis=1, keepdims=True)
        return best, runner, total / jnp.sum(live.astype(f32), axis=1, keepdims=True)

    whole = pair(own, 0, n)
    halves = merge(whole, pair(own, n, 2 * n))
    mine = lax.axis_index("img") // half
    is_near = lax.broadcasted_iota(i32, whole[0].shape, 0) // half == mine
    best, runner, score = scored([jnp.where(is_near, a, b) for a, b in zip(halves, whole)])
    matches[:, 0, :] = best
    matches[:, 1, :] = runner
    first = firsts[:, 0:1]

    def per_image(image, score):
        at = lax.broadcasted_iota(i32, (image.shape[0], img_dev), 1).astype(f32)
        return jnp.sum(jnp.where(image == at, score, 0.0), axis=0)

    close = merge(pair(arr, 0, half), pair(arr, half, n))
    apart = pair(arr, n, n + half)
    total = per_image(first, score)
    total = total + per_image(arr[0:half, 2, 0:1], scored(close)[2])
    scores[...] = total + per_image(arr[n : n + half, 2, 0:1], scored(apart)[2])


def on_device(n, m, descriptors, cell_counts, pair_images, query_cells, cand_cells, cand_counts):
    img_dev, share, width = descriptors.shape
    slots, qn = cand_cells.shape[2], query_cells.shape[1]
    qd = qn * width // DESC
    sides, half, mine = m // 2, n // 2, n // 4
    vmem = pl.BlockSpec(memory_space=pltpu.VMEM)
    dma = pltpu.SemaphoreType.DMA
    operands = (
        descriptors, cell_counts, pair_images.T, query_cells, cand_cells, cand_counts.T,
    )
    hbm = pl.BlockSpec(memory_space=pltpu.HBM)
    info_rows = (n + img_dev + 7) // 8 * 8
    own, arr, firsts = pl.pallas_call(
        functools.partial(kernel, n, sides),
        out_shape=(
            pltpu.VMEM((sides * n, 4, qd), f32),
            pltpu.VMEM((n + half, 4, qd), f32),
            pltpu.VMEM((n, DESC), f32),
        ),
        in_specs=[hbm] * 6,
        out_specs=(vmem,) * 3,
        scratch_shapes=[
            pltpu.VMEM((2, *descriptors.shape), bf16),
            *(pltpu.VMEM(x.shape, x.dtype) for x in operands[1:]),
            dma((len(operands),)),
            pltpu.VMEM((2, info_rows, DESC), i32),
            pltpu.VMEM((2, (half + 7) // 8 * 8, DESC), i32),
            pltpu.VMEM(query_cells.shape, i32),
            pltpu.VMEM((half, qn, width), bf16),
            pltpu.VMEM((sides * half, qn, width), bf16),
            pltpu.VMEM((mine, 2 * slots, width), bf16),
            pltpu.VMEM((mine, 2 * slots, width), bf16),
            pltpu.VMEM((half, 2 * slots * width // DESC, 5 * DESC), bf16),
            pltpu.VMEM((mine, qd, 5 * DESC), bf16),
            pltpu.VMEM((half, 4, qd), f32),
            dma, dma, dma, dma, dma, dma((half,)),
            dma, dma((sides, half)), dma, dma((mine, 2)), dma, dma, dma, dma,
            pltpu.SemaphoreType.REGULAR,
        ],
        compiler_params=pltpu.CompilerParams(
            collective_id=0, has_side_effects=True
        ),
    )(*operands)
    held = functools.partial(pltpu.with_memory_space_constraint, memory_space=pltpu.VMEM)
    return pl.pallas_call(
        functools.partial(finish, n, img_dev),
        out_shape=(
            jax.ShapeDtypeStruct((n, 2, qd), f32),
            jax.ShapeDtypeStruct((img_dev,), f32),
        ),
        in_specs=[vmem] * 3,
        out_specs=(vmem, vmem),
    )(held(own), held(arr), held(firsts))


def solution(mesh):
    n, m = mesh.shape["img"], mesh.shape["rep"]
    in_specs = (
        P("img", "rep", None),
        P("img", "rep"),
        P("img", None),
        P("img", None),
        P("img", "rep", None),
        P("img", "rep"),
    )
    out_specs = (P("img", None, None), P("img"))
    return jax.shard_map(
        functools.partial(on_device, n, m),
        mesh=mesh, in_specs=in_specs, out_specs=out_specs, check_vma=False,
    )
```

```python
import functools

import jax
import jax.numpy as jnp
from jax import lax
from jax.experimental import pallas as pl
from jax.experimental.pallas import tpu as pltpu
from jax.sharding import PartitionSpec as P

DESC = 128
MESH = pl.DeviceIdType.MESH
distant = 1.0e9
far_entry = 32768.0
f32, bf16, i32 = jnp.float32, jnp.bfloat16, jnp.int32


def flips(me, size):
    steps, bit = [], 1
    while bit < size:
        steps.append(bit - (me // bit) % 2 * (2 * bit))
        bit *= 2
    return steps


def repeat(first, last, body):
    if last - first <= 8:
        for t in range(first, last):
            body(t)
    else:
        lax.fori_loop(first, last, lambda t, c: (body(t), c)[1], 0)


def dot(a, b):
    return jnp.dot(a, b, preferred_element_type=f32)


def dot_t(a, b):
    return lax.dot_general(a, b, (((1,), (1,)), ((), ())), preferred_element_type=f32)


def split(square):
    high = square.astype(bf16)
    return high, (square - high.astype(f32)).astype(bf16)


def column(row, length):
    rows = lax.broadcasted_iota(i32, (length, length), 0)
    cols = lax.broadcasted_iota(i32, (length, length), 1)
    return jnp.sum(jnp.where(rows == cols, row, 0.0), axis=1, keepdims=True)


def merge(a, b):
    low = jnp.minimum(a[0], b[0])
    high = jnp.minimum(jnp.maximum(a[0], b[0]), jnp.minimum(a[1], b[1]))
    return low, high


def lowest_two(d):
    half = d.shape[0] // 2
    a, b = d[:half], d[half:]
    two = (jnp.minimum(a, b), jnp.maximum(a, b))
    while half > 1:
        half //= 2
        two = merge((two[0][:half], two[1][:half]), (two[0][half:], two[1][half:]))
    return two


def stacked(cells):
    kp = cells.shape[1] // DESC
    return jnp.concatenate([cells[:, s * DESC : (s + 1) * DESC] for s in range(kp)], axis=0)


def kernel(
    n, sides,
    desc_hbm, counts_hbm, pairs_hbm, qcells_hbm, ccells_hbm, ccounts_hbm,
    own, arr, firsts,
    both, counts, pairs, qcells, ccells, ccounts, in_sem,
    info, lists_in, asked_at, q_out, q_in, c_out, c_in, lhs, rhs, part_out,
    info_send, info_recv, both_send, both_recv, list_send, list_recv,
    q_send, q_recv, c_send, c_recv, own_send, own_recv, arr_send, arr_recv, met,
):
    me, r = lax.axis_index("img"), lax.axis_index("rep")
    side, core = r // 2, r % 2
    mate = side * 2 + (1 - core)
    across = (1 - side) * 2 + core
    img_dev, share, width = both.shape[1:]
    rows = img_dev * share
    kp = width // DESC
    slots = ccells.shape[2]
    qn = qcells.shape[1]
    half, mine = n // 2, n // 4
    lane = (side + me) % 2

    def remote(src, dst, send, recv, img, rep):
        return pltpu.make_async_remote_copy(
            src_ref=src, dst_ref=dst, send_sem=send, recv_sem=recv,
            device_id=(img, rep), device_id_type=MESH,
        )

    def drain(ref, sem):
        pltpu.make_async_copy(ref, ref, sem).wait()

    steps = flips(me, n)
    base = me + core * steps[-1]

    def other(i):
        if isinstance(i, int):
            return base + sum(step for k, step in enumerate(steps[:-1]) if i >> k & 1)
        return base + sum(i // 2**k % 2 * step for k, step in enumerate(steps[:-1]))

    barrier = pltpu.get_barrier_semaphore()

    def greet(img, rep):
        pl.semaphore_signal(barrier, inc=1, device_id=(img, rep), device_id_type=MESH)

    @pl.when(core == 0)
    def _():
        def greet_near(i):
            greet(other(i), mate)
            greet(other(i), (1 - side) * 2 + 1)

        repeat(0, half - 1, lambda i: greet_near(half - 1 - i))
        greet(other(0), (1 - side) * 2 + 1)

    @pl.when(core == 1)
    def _():
        greet(me, mate)
        repeat(0, half, lambda i: greet(other(half - 1 - i), r))
        repeat(0, mine, lambda p: greet(other(2 * (mine - 1 - p) + lane), across))

    small = [
        pltpu.make_async_copy(src, dst, in_sem.at[i])
        for i, (src, dst) in enumerate((
            (counts_hbm, counts), (pairs_hbm, pairs),
            (ccells_hbm, ccells), (ccounts_hbm, ccounts), (qcells_hbm, qcells),
        ))
    ]
    shard = pltpu.make_async_copy(desc_hbm, both.at[core], in_sem.at[len(small)])
    for load in small:
        load.start()
    shard.start()
    @pl.when(core == 0)
    def _():
        pl.semaphore_wait(barrier, 1)
        pl.semaphore_signal(met, inc=1, device_id=(me, mate), device_id_type=MESH)

    @pl.when(core == 1)
    def _():
        pl.semaphore_wait(met, 1)

    remote(desc_hbm, both.at[core], both_send, both_recv, me, mate).start()
    for load in small:
        load.wait()

    local = (pairs[...] % img_dev).astype(f32)
    first = column(local[0:1], n).astype(i32)
    second = column(local[1:2], n).astype(i32)
    live_cells = column(ccounts[...].astype(f32), n).astype(i32)
    wanted = core * rows + second * share + ccells[:, 0, :] % share
    wanted = jnp.where(lax.broadcasted_iota(i32, (n, slots), 1) < live_cells, wanted, -1)
    info[core, 0:n, 0:slots] = wanted
    firsts[...] = jnp.broadcast_to(first, firsts.shape).astype(f32)
    info[core, n : n + img_dev, 0:share] = counts[...]

    remote(info.at[core], info.at[core], info_send, info_recv, me, mate).start()

    cells = qcells[...]
    quarter = cells // share
    where = (quarter % 2) * rows + first * share + cells % share
    asked_at[...] = jnp.where(quarter // 2 == side, where, -1)
    group = min(half, 4)
    found_at = []
    for g in range(0, half, group):
        picks = [
            column(asked_at[pl.ds(other(i), 1), :].astype(f32), qn) for i in range(g, g + group)
        ]
        found_at.append(jnp.concatenate(picks, axis=0).astype(i32))

    pltpu.make_async_copy(info.at[1 - core], info.at[1 - core], info_recv).wait()

    def list_to(i):
        return info.at[:, pl.ds(other(i), 1)], lists_in.at[:, pl.ds(i, 1)]

    def send_list(i):
        remote(*list_to(i), list_send, list_recv.at[i], other(i), r).start()

    count_row = jnp.concatenate(
        [info[q, n + i : n + i + 1, 0:share] for q in range(2) for i in range(img_dev)], axis=1
    ).astype(f32)
    shard.wait()
    pltpu.make_async_copy(both.at[1 - core], both.at[1 - core], both_recv).wait()

    def pick(asked, none, dead):
        at = lax.broadcasted_iota(i32, (asked.shape[0], 2 * rows), 1)
        chosen = jnp.where(asked == at, 1.0, 0.0)
        live = jnp.sum(chosen * count_row, axis=1, keepdims=True)
        live = jnp.where(asked < 0, none, live)
        found = dot(chosen.astype(bf16), both[...].reshape(2 * rows, width))
        slot_of = (lax.broadcasted_iota(i32, found.shape, 1) // DESC).astype(f32)
        return jnp.where(slot_of < live, found, dead).astype(bf16)

    for g in range(0, half, group):
        block = pick(found_at[g // group], float(kp), -far_entry)
        for i in range(g, g + group):
            q_out[i] = block[(i - g) * qn : (i - g + 1) * qn]

    @pl.when(core == 0)
    def _():
        pl.semaphore_wait(met, 1)
        repeat(0, half - 1, lambda i: send_list(half - 1 - i))
        pltpu.make_async_copy(*list_to(0), list_recv.at[0]).start()

    @pl.when(core == 1)
    def _():
        pl.semaphore_wait(barrier, n - 1 + half + lane * half)
        pl.semaphore_signal(met, inc=1, device_id=(me, mate), device_id_type=MESH)
        repeat(0, half, lambda i: send_list(half - 1 - i))

    def q_to(i):
        return q_out.at[i], q_in.at[side * half + i]

    def candidates(indices):
        picks = []
        for i in indices:
            ref = lists_in.at[:, pl.ds(i, 1)]
            pltpu.make_async_copy(ref, ref, list_recv.at[i]).wait()
            for q in range(2):
                asked = lists_in[q, pl.ds(i, 1), 0:slots]
                picks.append(column(asked.astype(f32), slots))
        return pick(jnp.concatenate(picks, axis=0).astype(i32), 0.0, far_entry)

    def prepared(block):
        wide = stacked(block).astype(f32)
        high, low = split(wide * wide)
        ones = jnp.ones(wide.shape, bf16)
        return jnp.concatenate([high, low, (-2.0 * wide).astype(bf16), ones, ones], axis=1)

    cn = 2 * slots

    def prepare(indices, place):
        for g in range(0, len(indices), group):
            block = candidates(indices[g : g + group])
            for p in range(g, min(g + group, len(indices))):
                lhs[place(p)] = prepared(block[(p - g) * cn : (p - g + 1) * cn])

    qd = qn * kp

    def queries(i):
        for s in range(sides):
            ref = q_in.at[s * half + i]
            pltpu.make_async_copy(ref, ref, q_recv.at[s, i]).wait()
        to = lax.broadcasted_iota(i32, (qd, sides * qd), 0)
        at = lax.broadcasted_iota(i32, (qd, sides * qd), 1) % qd
        order = jnp.where(at == (to % kp) * qn + to // kp, 1.0, 0.0).astype(bf16)
        stack = jnp.concatenate([stacked(q_in[s * half + i]) for s in range(sides)], axis=0)
        query = dot(order, stack)
        high, low = split(query * query)
        ones = jnp.ones((qd, DESC), bf16)
        return jnp.concatenate([ones, ones, query.astype(bf16), high, low], axis=1)

    def keep(p, i, two):
        image = lists_in[0, pl.ds(i, 1), 0:1] // share
        image = jnp.broadcast_to(image.astype(f32), (1, qd))
        part_out[p] = jnp.minimum(jnp.concatenate([*two, image, image], axis=0), distant)

    everyone = [s * 2 + c for s in range(sides) for c in range(2)]
    others = (across, mate, (1 - side) * 2 + (1 - core))

    def to_owner(p, j, place):
        for to_rep in everyone:
            remote(part_out.at[p], place, own_send, own_recv, j, to_rep).start()

    def to_group(ref, place):
        for to_rep in others:
            remote(ref, place, arr_send, arr_recv, me, to_rep).start()
        pltpu.make_async_copy(ref, place, arr_recv).start()

    @pl.when(core == 0)
    def _():
        def send_near(i, cross):
            if cross:
                remote(*q_to(i), q_send, q_recv.at[1, i], other(i), across).start()
            else:
                remote(*q_to(i), q_send, q_recv.at[0, i], other(i), r).start()

        for cross in (True, False):
            repeat(0, half - 1, lambda i: send_near(half - 1 - i, cross))
        remote(*q_to(0), q_send, q_recv.at[1, 0], me, across).start()
        pltpu.make_async_copy(*q_to(0), q_recv.at[0, 0]).start()

        prepare(list(range(half)), lambda p: p)
        place = own.at[side * n + me]

        def near_pair(i):
            keep(i, i, lowest_two(dot_t(lhs[i], queries(i))))

        def near_step(i):
            near_pair(i)
            to_owner(i, other(i), place)

        repeat(0, half - 1, lambda i: near_step(half - 1 - i))
        near_pair(0)
        for to_rep in others:
            remote(part_out.at[0], place, own_send, own_recv, me, to_rep).start()
        pltpu.make_async_copy(part_out.at[0], place, own_recv).start()
        to_group(part_out, arr.at[pl.ds(side * half, half)])

    @pl.when(core == 1)
    def _():
        def send_far(i):
            remote(*q_to(i), q_send, q_recv.at[lane, i], other(i), me % 2 * 2 + 1).start()

        repeat(0, half, lambda i: send_far(half - 1 - i))

        flip = (1 + me // half + me // mine) % 2 * (mine // 2)
        turns = [(q + flip) % mine for q in range(mine)]
        for p in turns:
            c_out[p] = candidates([2 * p + 1 - lane])
            remote(c_out.at[p], c_in.at[p], c_send, c_recv.at[p], me, across).start()

        prepare([2 * p + lane for p in turns], lambda q: turns[q])

        def far_first(p):
            i = 2 * p + lane
            rhs[p] = queries(i)
            keep(p, i, lowest_two(dot_t(lhs[p], rhs[p])))


        def far_last(p):
            pltpu.make_async_copy(c_in.at[p], c_in.at[p], c_recv.at[p]).wait()
            two = lowest_two(dot_t(prepared(c_in[p]), rhs[p]))
            before = part_out[p]
            i = 2 * p + lane
            keep(p, i, merge((before[0:1], before[1:2]), two))
            to_owner(p, other(i), own.at[me])

        for p in turns:
            far_first(p)
            far_last(p)
        to_group(part_out.at[pl.ds(0, mine)], arr.at[pl.ds(n + side * mine, mine)])

    drain(info.at[0], info_send)
    drain(both.at[0], both_send)

    @pl.when(core == 0)
    def _():
        drain(lists_in.at[:, pl.ds(0, half - 1)], list_send)
        drain(q_in.at[pl.ds(0, n - 1)], q_send)
        drain(own.at[pl.ds(0, 2 * n - 1)], own_send)
        drain(arr, arr_send)

    @pl.when(core == 1)
    def _():
        drain(lists_in.at[:, pl.ds(0, half)], list_send)
        drain(q_in.at[pl.ds(0, half)], q_send)
        drain(c_in, c_send)
        drain(own.at[pl.ds(0, n)], own_send)
        drain(arr.at[pl.ds(0, 3 * mine)], arr_send)

    drain(own.at[pl.ds(0, n + half)], own_recv)
    drain(arr, arr_recv)


def finish(n, img_dev, own, arr, firsts, matches, scores):
    half = n // 2

    def pair(ref, first, last):
        return ref[first:last, 0, :], ref[first:last, 1, :]

    def scored(two):
        live = two[0] < 0.5 * distant
        best, runner = jnp.where(live, two[0], 0.0), jnp.where(live, two[1], 0.0)
        margin = jnp.where(live, (runner - best) / (runner + 1.0), 0.0)
        total = jnp.sum(margin, axis=1, keepdims=True)
        return best, runner, total / jnp.sum(live.astype(f32), axis=1, keepdims=True)

    whole = pair(own, 0, n)
    halves = merge(whole, pair(own, n, 2 * n))
    mine = lax.axis_index("img") // half
    is_near = lax.broadcasted_iota(i32, whole[0].shape, 0) // half == mine
    best, runner, score = scored([jnp.where(is_near, a, b) for a, b in zip(halves, whole)])
    matches[:, 0, :] = best
    matches[:, 1, :] = runner
    first = firsts[:, 0:1]

    def per_image(image, score):
        at = lax.broadcasted_iota(i32, (image.shape[0], img_dev), 1).astype(f32)
        return jnp.sum(jnp.where(image == at, score, 0.0), axis=0)

    close = merge(pair(arr, 0, half), pair(arr, half, n))
    apart = pair(arr, n, n + half)
    total = per_image(first, score)
    total = total + per_image(arr[0:half, 2, 0:1], scored(close)[2])
    scores[...] = total + per_image(arr[n : n + half, 2, 0:1], scored(apart)[2])


def on_device(n, m, descriptors, cell_counts, pair_images, query_cells, cand_cells, cand_counts):
    img_dev, share, width = descriptors.shape
    slots, qn = cand_cells.shape[2], query_cells.shape[1]
    qd = qn * width // DESC
    sides, half, mine = m // 2, n // 2, n // 4
    vmem = pl.BlockSpec(memory_space=pltpu.VMEM)
    dma = pltpu.SemaphoreType.DMA
    operands = (
        descriptors, cell_counts, pair_images.T, query_cells, cand_cells, cand_counts.T,
    )
    hbm = pl.BlockSpec(memory_space=pltpu.HBM)
    info_rows = (n + img_dev + 7) // 8 * 8
    own, arr, firsts = pl.pallas_call(
        functools.partial(kernel, n, sides),
        out_shape=(
            pltpu.VMEM((sides * n, 4, qd), f32),
            pltpu.VMEM((n + half, 4, qd), f32),
            pltpu.VMEM((n, DESC), f32),
        ),
        in_specs=[hbm] * 6,
        out_specs=(vmem,) * 3,
        scratch_shapes=[
            pltpu.VMEM((2, *descriptors.shape), bf16),
            *(pltpu.VMEM(x.shape, x.dtype) for x in operands[1:]),
            dma((len(operands),)),
            pltpu.VMEM((2, info_rows, DESC), i32),
            pltpu.VMEM((2, (half + 7) // 8 * 8, DESC), i32),
            pltpu.VMEM(query_cells.shape, i32),
            pltpu.VMEM((half, qn, width), bf16),
            pltpu.VMEM((sides * half, qn, width), bf16),
            pltpu.VMEM((mine, 2 * slots, width), bf16),
            pltpu.VMEM((mine, 2 * slots, width), bf16),
            pltpu.VMEM((half, 2 * slots * width // DESC, 5 * DESC), bf16),
            pltpu.VMEM((mine, qd, 5 * DESC), bf16),
            pltpu.VMEM((half, 4, qd), f32),
            dma, dma, dma, dma, dma, dma((half,)),
            dma, dma((sides, half)), dma, dma((mine,)), dma, dma, dma, dma,
            pltpu.SemaphoreType.REGULAR,
        ],
        compiler_params=pltpu.CompilerParams(
            collective_id=0, has_side_effects=True
        ),
    )(*operands)
    held = functools.partial(pltpu.with_memory_space_constraint, memory_space=pltpu.VMEM)
    return pl.pallas_call(
        functools.partial(finish, n, img_dev),
        out_shape=(
            jax.ShapeDtypeStruct((n, 2, qd), f32),
            jax.ShapeDtypeStruct((img_dev,), f32),
        ),
        in_specs=[vmem] * 3,
        out_specs=(vmem, vmem),
    )(held(own), held(arr), held(firsts))


def solution(mesh):
    n, m = mesh.shape["img"], mesh.shape["rep"]
    in_specs = (
        P("img", "rep", None),
        P("img", "rep"),
        P("img", None),
        P("img", None),
        P("img", "rep", None),
        P("img", "rep"),
    )
    out_specs = (P("img", None, None), P("img"))
    return jax.shard_map(
        functools.partial(on_device, n, m),
        mesh=mesh, in_specs=in_specs, out_specs=out_specs, check_vma=False,
    )
```
